128 devices in a mesh: chan: 16 (over y, x), stn: 8 (over z, core).
Axes of the slice: x: 4, y: 4, z: 4, core: 2. Of those that a mesh axis runs over, the one named last changes fastest.
Arguments:
- measured_correlation: float32 [16, 8, 8192], P('chan', None, 'stn'), may hold values from -3 to 3
- model_correlation: float32 [16, 8, 16, 8192], P('chan', None, None, 'stn'), may hold values from -0.75 to 0.75
- source_pointing: int32 [16, 1], replicated, may hold values from 0 to 7
- antenna_pairs: int32 [2, 8192], P(None, 'stn'), may hold values from 0 to 511, as said below
- starting_jones_matrices: float32 [16, 8, 8, 512], P('chan'), may hold values from -1 to 2
- starting_polynomial_terms: float32 [3, 8, 8, 512], replicated, may hold values from -1 to 2
- starting_lagrange_scaled: float32 [16, 8, 8, 512], P('chan'), may hold values from -1.5 to 1.5
- augmented_lagrange_rhos: float32 [8], replicated, may hold values from 0.5 to 4
Outputs:
- solved_gains: float32 [16, 8, 8, 512], P('chan', None, None, 'stn')
- solved_dual: float32 [16, 8, 8, 512], P('chan', None, None, 'stn')
- fit_coeffs: float32 [3, 8, 8, 512], P(None, None, None, 'stn')
The draws below stay inside these ranges and needn't reach their ends.
Inputs may be any that keep to these rules, and one draw needn't show every extreme that they name: `antenna_pairs`: row 0 holds a baseline's first station and row 1 its second, which differs from the first. The first station of every baseline in the i-th aligned block of 1024 baselines lies among stations i * 64 to (i + 1) * 64 - 1. `source_pointing`: every direction holds at least one component.
All inputs are finite; a program needn't handle non-finite values.
Results may differ from the reference program's by a relative error of at most 0.0001.
Values sent between devices are 32-bit elements; how exact they have to be, the bound alone decides.
A program may use at most 64 MiB of HBM per device.

```python
import math
import jax
import jax.numpy as jnp
from jax import lax

STATION_COUNT = 512
CALIB_PATHS = 8
SKY_COMPONENTS = 16
TERMS = 3
STEPS = 2
INNER = 2
BL_DEV = 1024
FREQ_CHANNELS = 16
BASELINE_COUNT = 8192
BLOCK_STATIONS = 64


def draw_antenna_pairs(key, part):
    row_index = jnp.arange(BASELINE_COUNT, dtype=jnp.int32)
    block_holder = row_index // BL_DEV
    first_key = jax.random.fold_in(key, 11)
    second_key = jax.random.fold_in(key, 12)
    first_station = block_holder * BLOCK_STATIONS + jax.random.randint(first_key, (BASELINE_COUNT,), 0, BLOCK_STATIONS, dtype=jnp.int32)
    second_station = (first_station + 1 + jax.random.randint(second_key, (BASELINE_COUNT,), 0, STATION_COUNT - 1, dtype=jnp.int32)) % STATION_COUNT
    return jnp.stack([first_station, second_station], axis=0)


def draw_starting_jones_matrices(key, part):
    full_shape = (FREQ_CHANNELS, 8, CALIB_PATHS, STATION_COUNT)
    sub_key = jax.random.fold_in(key, 21)
    jitter_part = jnp.clip(jax.random.normal(sub_key, full_shape, jnp.float32), -4.0, 4.0) * 0.25
    component = jnp.arange(8, dtype=jnp.int32)
    identity = ((component == 0) | (component == 3)).astype(jnp.float32)[None, :, None, None]
    return identity + jitter_part


def draw_starting_polynomial_terms(key, part):
    full_shape = (TERMS, 8, CALIB_PATHS, STATION_COUNT)
    sub_key = jax.random.fold_in(key, 31)
    jitter_part = jnp.clip(jax.random.normal(sub_key, full_shape, jnp.float32), -4.0, 4.0) * 0.25
    component = jnp.arange(8, dtype=jnp.int32)
    degree_ids = jnp.arange(TERMS, dtype=jnp.int32)
    identity = (((component == 0) | (component == 3))[None, :] & (degree_ids == 0)[:, None]).astype(jnp.float32)
    return identity[:, :, None, None] + jitter_part


def block_levels(own_key, shape, cuts, low, top_value):
    level, own = 1.0, jax.random.fold_in(own_key, 6)
    for dim, shards_of in cuts:
        steps = jnp.exp(jax.random.uniform(jax.random.fold_in(own, dim), (shards_of,), jnp.float32, low / len(cuts), top_value / len(cuts)))
        level = level * jnp.repeat(steps, shape[dim] // shards_of).reshape([-1 if axis == dim else 1 for axis in range(len(shape))])
    return level


def different_ones(key, rows, number_of, top, lift):
    ranking = jax.random.permutation(jax.random.fold_in(key, 1), number_of)
    favour = ranking
    for power in range(3):
        favour = favour * favour // number_of
    favour = favour * lift // number_of
    chance = jax.random.randint(jax.random.fold_in(key, 2), (rows, number_of), 0, 4096) + favour
    holders = jax.random.permutation(jax.random.fold_in(key, 3), rows)[jnp.arange(number_of) % rows]
    chance = jnp.where(jnp.arange(rows)[:, None] == holders[None, :], 1 << 14, chance)
    score = chance * number_of + jnp.arange(number_of)
    return lax.top_k(score.astype(jnp.int32), top)[1].astype(jnp.int32)


def scatter_about(own_key, dims, deviation, limit, cuts=(), held_as=jnp.bfloat16):
    drawn = jax.random.normal(own_key, dims, jnp.float32) * deviation
    if len(cuts) > 0:
        drawn = block_levels(own_key, dims, cuts, -0.22, 0.18) * drawn
    return jnp.clip(drawn, min=-limit, max=limit).astype(held_as)


def setup_inputs(seed: int = 0) -> dict:
    arg_keys = jax.random.split(jax.random.key(seed), 9)
    measured_correlation = scatter_about(arg_keys[0], (FREQ_CHANNELS, 8, BASELINE_COUNT), 0.5, 3.0, ((0, 16), (2, 8)), jnp.float32)
    model_correlation = scatter_about(arg_keys[1], (FREQ_CHANNELS, 8, SKY_COMPONENTS, BASELINE_COUNT), (0.5 * STATION_COUNT ** 0.5 * BASELINE_COUNT ** -0.5), 0.75, ((0, 16), (3, 8)), jnp.float32)
    source_pointing = different_ones(arg_keys[2], SKY_COMPONENTS, CALIB_PATHS, 1, 1024)
    antenna_pairs = draw_antenna_pairs(jax.random.fold_in(arg_keys[8], 71), 0)
    starting_jones_matrices = draw_starting_jones_matrices(jax.random.fold_in(arg_keys[8], 71), 0)
    starting_polynomial_terms = draw_starting_polynomial_terms(jax.random.fold_in(arg_keys[8], 71), 0)
    starting_lagrange_scaled = scatter_about(arg_keys[6], (FREQ_CHANNELS, 8, CALIB_PATHS, STATION_COUNT), 0.3, 1.5, ((0, 16),), jnp.float32)
    augmented_lagrange_rhos = jnp.clip(jnp.exp(jax.random.uniform(arg_keys[7], (CALIB_PATHS,), jnp.float32, math.log(0.5), math.log(4.0))), 0.5, 4.0)
    return dict(measured_correlation=measured_correlation, model_correlation=model_correlation, source_pointing=source_pointing, antenna_pairs=antenna_pairs, starting_jones_matrices=starting_jones_matrices, starting_polynomial_terms=starting_polynomial_terms, starting_lagrange_scaled=starting_lagrange_scaled, augmented_lagrange_rhos=augmented_lagrange_rhos)


student_nu = 2.0
squared_tolerance = 1e-06
highest = lax.Precision.HIGHEST

def entries(stacked):
    return [(stacked[slot_idx], stacked[4 + slot_idx]) for slot_idx in range(4)]

def assemble(matrix):
    return jnp.stack([matrix[slot_idx][0] for slot_idx in range(4)] + [matrix[slot_idx][1] for slot_idx in range(4)], axis=0)

def flatten(matrix):
    return [matrix[slot_idx][0] for slot_idx in range(4)] + [matrix[slot_idx][1] for slot_idx in range(4)]

def multiply_pair(first_pair, second_pair):
    return (first_pair[0] * second_pair[0] - first_pair[1] * second_pair[1], first_pair[0] * second_pair[1] + first_pair[1] * second_pair[0])

def add_pair(first_pair, second_pair):
    return (first_pair[0] + second_pair[0], first_pair[1] + second_pair[1])

def conjugate(value_pair):
    return (value_pair[0], -value_pair[1])

def matrix_product(factor_one, factor_two):
    return [add_pair(multiply_pair(factor_one[0], factor_two[0]), multiply_pair(factor_one[1], factor_two[2])), add_pair(multiply_pair(factor_one[0], factor_two[1]), multiply_pair(factor_one[1], factor_two[3])), add_pair(multiply_pair(factor_one[2], factor_two[0]), multiply_pair(factor_one[3], factor_two[2])), add_pair(multiply_pair(factor_one[2], factor_two[1]), multiply_pair(factor_one[3], factor_two[3]))]

def adjoint(matrix):
    return [conjugate(matrix[0]), conjugate(matrix[2]), conjugate(matrix[1]), conjugate(matrix[3])]

def gram_parts(matrix):
    upper_sum = matrix[0][0] * matrix[0][0] + matrix[0][1] * matrix[0][1] + matrix[1][0] * matrix[1][0] + matrix[1][1] * matrix[1][1]
    lower_sum = matrix[2][0] * matrix[2][0] + matrix[2][1] * matrix[2][1] + matrix[3][0] * matrix[3][0] + matrix[3][1] * matrix[3][1]
    cross_term = add_pair(multiply_pair(matrix[0], conjugate(matrix[2])), multiply_pair(matrix[1], conjugate(matrix[3])))
    return [upper_sum, lower_sum, cross_term[0], cross_term[1]]

def basis_table(channel_count):
    frequency = (2.0 * jnp.arange(channel_count, dtype=jnp.float32) + 1.0) / channel_count - 1.0
    columns = []
    for degree in range(TERMS):
        column = frequency ** degree
        for earlier in columns:
            column = column - jnp.sum(earlier * column) / channel_count * earlier
        column = column / jnp.sqrt(jnp.sum(column * column) / channel_count)
        columns.append(column)
    return jnp.stack(columns, axis=1)

def combine_sources(cohere_f, source_pointing):
    member = (source_pointing[:, 0][:, None] == jnp.arange(CALIB_PATHS, dtype=jnp.int32)[None, :]).astype(jnp.float32)
    return jnp.einsum('csb,sk->ckb', cohere_f, member, precision=highest)

def channel_state(vis_f, cohere_dir, spectral_jones_matrices, antenna_pairs):
    coherent = entries(cohere_dir)
    first_gain = entries(spectral_jones_matrices[:, :, antenna_pairs[0]])
    second_gain = entries(spectral_jones_matrices[:, :, antenna_pairs[1]])
    toward_first = matrix_product(coherent, adjoint(second_gain))
    own_terms = matrix_product(first_gain, toward_first)
    observed = entries(vis_f)
    residual = [(observed[slot_idx][0] - lax.optimization_barrier(jnp.sum(own_terms[slot_idx][0], axis=0)), observed[slot_idx][1] - lax.optimization_barrier(jnp.sum(own_terms[slot_idx][1], axis=0))) for slot_idx in range(4)]
    energy = residual[0][0] * residual[0][0] + residual[0][1] * residual[0][1]
    for slot_idx in range(1, 4):
        energy = energy + residual[slot_idx][0] * residual[slot_idx][0] + residual[slot_idx][1] * residual[slot_idx][1]
    return (residual, own_terms, toward_first, first_gain, coherent, energy)

def channel_sums(chan_state, weight, antenna_pairs, station_count):
    residual, own_terms, toward_first, first_gain, coherent, energy = chan_state
    target = [add_pair((residual[slot_idx][0][None], residual[slot_idx][1][None]), own_terms[slot_idx]) for slot_idx in range(4)]
    back_terms = matrix_product(first_gain, coherent)
    first_parts = jnp.stack(gram_parts(toward_first) + flatten(matrix_product(target, adjoint(toward_first))), axis=0) * weight
    second_parts = jnp.stack(gram_parts(adjoint(back_terms)) + flatten(matrix_product(adjoint(target), back_terms)), axis=0) * weight
    zero_sums = jnp.zeros((12, first_parts.shape[1], station_count), jnp.float32)
    return zero_sums.at[:, :, antenna_pairs[0]].add(first_parts).at[:, :, antenna_pairs[1]].add(second_parts)

def jones_estimator(least_squares_equations, pivot_spectral_point, spectral_jones_matrices, augmented_lagrange_rhos):
    augmented_rho_factor = augmented_lagrange_rhos[:, None]
    diag_one = least_squares_equations[0] + augmented_rho_factor
    diag_two = least_squares_equations[1] + augmented_rho_factor
    determinant = diag_one * diag_two - least_squares_equations[2] * least_squares_equations[2] - least_squares_equations[3] * least_squares_equations[3]
    zero_part = jnp.zeros_like(determinant)
    inverse = [(diag_two / determinant, zero_part), (-least_squares_equations[2] / determinant, -least_squares_equations[3] / determinant), (-least_squares_equations[2] / determinant, least_squares_equations[3] / determinant), (diag_one / determinant, zero_part)]
    right_side = entries(least_squares_equations[4:] + augmented_rho_factor[None] * pivot_spectral_point)
    solution = assemble(matrix_product(right_side, inverse))
    return 0.5 * (spectral_jones_matrices + solution)

def plain_python_iterate(measured_correlation, model_correlation, source_pointing, antenna_pairs, present_jones_matrix, pivot_antenna, augmented_lagrange_rhos):

    def energy_of(channel_items):
        vis_f, cohere_f, spectral_jones_matrices = channel_items
        chan_state = channel_state(vis_f, combine_sources(cohere_f, source_pointing), spectral_jones_matrices, antenna_pairs)
        return jnp.sum(chan_state[5])
    summed_energy = jnp.sum(lax.map(energy_of, (measured_correlation, model_correlation, present_jones_matrix)))
    mean_square = summed_energy / (FREQ_CHANNELS * BASELINE_COUNT) + squared_tolerance

    def update_of(channel_items):
        vis_f, cohere_f, spectral_jones_matrices, pivot_spectral_point = channel_items
        chan_state = channel_state(vis_f, combine_sources(cohere_f, source_pointing), spectral_jones_matrices, antenna_pairs)
        weight = (student_nu + 2.0) / (student_nu + chan_state[5] / mean_square)
        least_squares_equations = channel_sums(chan_state, weight, antenna_pairs, STATION_COUNT)
        return jones_estimator(least_squares_equations, pivot_spectral_point, spectral_jones_matrices, augmented_lagrange_rhos)
    return lax.map(update_of, (measured_correlation, model_correlation, present_jones_matrix, pivot_antenna))

def reference(measured_correlation, model_correlation, source_pointing, antenna_pairs, starting_jones_matrices, starting_polynomial_terms, starting_lagrange_scaled, augmented_lagrange_rhos):
    basis = basis_table(FREQ_CHANNELS)
    consensus = jnp.einsum('ft,tcks->fcks', basis, starting_polynomial_terms, precision=highest)
    present_jones_matrix = starting_jones_matrices
    dual_now = starting_lagrange_scaled
    fit_now = starting_polynomial_terms
    for step_idx in range(STEPS):
        pivot_antenna = consensus - dual_now
        for inner_idx in range(INNER):
            present_jones_matrix = plain_python_iterate(measured_correlation, model_correlation, source_pointing, antenna_pairs, present_jones_matrix, pivot_antenna, augmented_lagrange_rhos)
        fit_now = jnp.einsum('ft,fcks->tcks', basis, present_jones_matrix + dual_now, precision=highest) / FREQ_CHANNELS
        consensus = jnp.einsum('ft,tcks->fcks', basis, fit_now, precision=highest)
        dual_now = dual_now + present_jones_matrix - consensus
    return (present_jones_matrix, dual_now, fit_now)
```

```python
import numpy as np
import jax
import jax.numpy as jnp
from jax import lax
from jax.experimental import pallas as pl
from jax.experimental.pallas import tpu as pltpu
from jax.sharding import PartitionSpec as P

PATHS = 8
SOURCES = 16
TERMS = 3
STEPS = 2
INNER = 2
PASSES = STEPS * INNER
NU = 2.0
TINY = 1e-06
MESH = pl.DeviceIdType.MESH
WIDE = 128
PAIRS = ((0, 1), (2, 3), (4, 8), (5, 9), (6, 10), (7, 11))
bf16 = jnp.bfloat16
f32 = jnp.float32


def basis_table(count):
    frequency = (2.0 * np.arange(count, dtype=np.float32) + 1.0) / np.float32(count) - 1.0
    columns = []
    for degree in range(TERMS):
        column = (frequency**degree).astype(np.float32)
        for earlier in columns:
            column = column - np.sum(earlier * column) / np.float32(count) * earlier
        column = column / np.sqrt(np.sum(column * column) / np.float32(count))
        columns.append(column.astype(np.float32))
    return np.stack(columns, axis=1)


def mul(a, b):
    return (a[0] * b[0] - a[1] * b[1], a[0] * b[1] + a[1] * b[0])


def mul_conj(a, b):
    return (a[0] * b[0] + a[1] * b[1], a[1] * b[0] - a[0] * b[1])


def conj_mul(a, b):
    return (a[0] * b[0] + a[1] * b[1], a[0] * b[1] - a[1] * b[0])


def add(a, b):
    return (a[0] + b[0], a[1] + b[1])


def product(a, b):
    return [
        add(mul(a[0], b[0]), mul(a[1], b[2])),
        add(mul(a[0], b[1]), mul(a[1], b[3])),
        add(mul(a[2], b[0]), mul(a[3], b[2])),
        add(mul(a[2], b[1]), mul(a[3], b[3])),
    ]


def product_with_adjoint(a, b):
    return [
        add(mul_conj(a[0], b[0]), mul_conj(a[1], b[1])),
        add(mul_conj(a[0], b[2]), mul_conj(a[1], b[3])),
        add(mul_conj(a[2], b[0]), mul_conj(a[3], b[1])),
        add(mul_conj(a[2], b[2]), mul_conj(a[3], b[3])),
    ]


def adjoint_product(a, b):
    return [
        add(conj_mul(a[0], b[0]), conj_mul(a[2], b[2])),
        add(conj_mul(a[0], b[1]), conj_mul(a[2], b[3])),
        add(conj_mul(a[1], b[0]), conj_mul(a[3], b[2])),
        add(conj_mul(a[1], b[1]), conj_mul(a[3], b[3])),
    ]


def power(a):
    return a[0] * a[0] + a[1] * a[1]


def gram(y):
    cross = add(mul_conj(y[0], y[2]), mul_conj(y[1], y[3]))
    return [power(y[0]) + power(y[1]), power(y[2]) + power(y[3]), cross[0], cross[1]]


def gram_of_adjoint(h):
    cross = add(conj_mul(h[0], h[1]), conj_mul(h[2], h[3]))
    return [power(h[0]) + power(h[2]), power(h[1]) + power(h[3]), cross[0], cross[1]]


def halves(x):
    top = x.astype(bf16)
    return top, (x - top.astype(f32)).astype(bf16)


def swap(x):
    return pltpu.roll(x, 64, 1)


def low(shape):
    return lax.broadcasted_iota(jnp.int32, shape, 1) < 64


def kernel(
    chans,
    blocks,
    table,
    pointing,
    rhos,
    vis_hbm,
    model_hbm,
    pairs_hbm,
    gain_hbm,
    poly_hbm,
    dual_hbm,
    gain_out,
    dual_out,
    fit_out,
    vis,
    model,
    pairs,
    gain_tile,
    poly_tile,
    dual_tile,
    whole,
    coherent,
    spread_q,
    collect_q,
    spread_p,
    collect_p,
    gain_p,
    gain_q,
    back,
    toward,
    target,
    energy,
    parts_p,
    parts_q,
    wide_p,
    wide_q,
    gain,
    dual,
    anchor,
    e_src,
    e_row,
    e_stn,
    e_chan,
    sums_src,
    sums,
    gains_src,
    gains,
    fits_src,
    fits,
    load_sem,
    e_sem,
    s_sem,
    g_sem,
    f_sem,
):
    chan = lax.axis_index("chan")
    stn = lax.axis_index("stn")
    baselines = vis.shape[1]
    stations = whole.shape[1]
    chunks = baselines // WIDE
    samples = float(chans * blocks * baselines)

    def stn_peer(d):
        return lax.rem(stn + d, blocks)

    def chan_peer(d):
        return lax.rem(chan + d, chans)

    barrier = pltpu.get_barrier_semaphore()

    def greet_stn(d, _):
        pl.semaphore_signal(barrier, inc=1, device_id=(chan, stn_peer(d)), device_id_type=MESH)
        return 0

    def greet_chan(d, _):
        pl.semaphore_signal(barrier, inc=1, device_id=(chan_peer(d), stn), device_id_type=MESH)
        return 0

    lax.fori_loop(1, blocks, greet_stn, 0)
    lax.fori_loop(1, chans, greet_chan, 0)

    lane_start = pl.multiple_of(lax.div(stn, 2) * 128, 128)
    loads = [
        pltpu.make_async_copy(pairs_hbm, pairs, load_sem.at[0]),
        pltpu.make_async_copy(model_hbm, model, load_sem.at[1]),
        pltpu.make_async_copy(gain_hbm.at[:, pl.ds(lane_start, 128)], gain_tile, load_sem.at[2]),
        pltpu.make_async_copy(gain_hbm, whole, load_sem.at[3]),
        pltpu.make_async_copy(vis_hbm, vis, load_sem.at[4]),
        pltpu.make_async_copy(poly_hbm.at[:, pl.ds(lane_start, 128)], poly_tile, load_sem.at[5]),
        pltpu.make_async_copy(dual_hbm.at[:, pl.ds(lane_start, 128)], dual_tile, load_sem.at[6]),
    ]
    for copy in loads:
        copy.start()

    loads[0].wait()
    first = pairs[0:1, :] - stn * 64
    second = pairs[1:2, :]
    row = lax.broadcasted_iota(jnp.int32, (128, baselines), 0)
    spread_p[...] = jnp.where(row == first, 1.0, 0.0).astype(bf16)
    for j in range(stations // 128):
        spread_q[128 * j : 128 * j + 128, :] = jnp.where(row + 128 * j == second, 1.0, 0.0).astype(bf16)
    column = lax.broadcasted_iota(jnp.int32, (baselines, 128), 1).astype(f32)
    first_t = jnp.broadcast_to(first.astype(f32), (128, baselines)).T
    second_t = jnp.broadcast_to(second.astype(f32), (128, baselines)).T
    collect_p[...] = jnp.where(column == first_t, 1.0, 0.0).astype(bf16)
    for j in range(stations // 128):
        collect_q[:, 128 * j : 128 * j + 128] = jnp.where(
            column + 128.0 * j == second_t, 1.0, 0.0
        ).astype(bf16)

    lane = lax.broadcasted_iota(jnp.int32, (64, 128), 1)
    high_row = lax.broadcasted_iota(jnp.int32, (64, 128), 0)
    point = jnp.zeros((64, 128), jnp.int32)
    for s in range(SOURCES):
        point = jnp.where(lane % SOURCES == s, pointing[s], point)
    member = jnp.where(
        (high_row // PATHS == lane // SOURCES) & (high_row % PATHS == point), 1.0, 0.0
    ).astype(bf16)
    loads[1].wait()

    def combine(i, _):
        at = pl.ds(pl.multiple_of(i * 256, 256), 256)
        m = model[:, at]
        m0 = m.astype(bf16)
        rest = m - m0.astype(f32)
        m1 = rest.astype(bf16)
        m2 = (rest - m1.astype(f32)).astype(bf16)
        coherent[:, at] = (
            jnp.dot(member, m0, preferred_element_type=f32)
            + jnp.dot(member, m1, preferred_element_type=f32)
            + jnp.dot(member, m2, preferred_element_type=f32)
        )
        return 0

    lax.fori_loop(0, baselines // 256, combine, 0)

    low_32 = low((32, 128))

    def own(re, im):
        return jnp.where(
            lax.rem(stn, 2) == 0,
            jnp.where(low_32, re, swap(im)),
            jnp.where(low_32, swap(re), im),
        )

    def mine(t):
        value = f32(0.0)
        for f in range(chans):
            value = jnp.where(chan == f, f32(table[f, t]), value)
        return value

    my_basis = [mine(t) for t in range(TERMS)]
    for copy in loads[2:]:
        copy.wait()
    gain[...] = own(gain_tile[0:32, :], gain_tile[32:64, :])
    dual[...] = own(dual_tile[0:32, :], dual_tile[32:64, :])
    start = jnp.zeros((32, 128), f32)
    for t in range(TERMS):
        start = start + my_basis[t] * own(
            poly_tile[64 * t : 64 * t + 32, :], poly_tile[64 * t + 32 : 64 * t + 64, :]
        )
    anchor[...] = start - dual[...]

    k_row = lax.broadcasted_iota(jnp.int32, (PATHS, 128), 0)
    rho = jnp.zeros((PATHS, 128), f32)
    for k in range(PATHS):
        rho = jnp.where(k_row == k, rhos[k], rho)
    low_8 = low((8, 128))

    pl.semaphore_wait(barrier, blocks + chans - 2)

    def entries(ref, at):
        return [(ref[8 * i : 8 * i + 8, at], ref[32 + 8 * i : 40 + 8 * i, at]) for i in range(4)]

    def keep(ref, at, values):
        for i in range(4):
            ref[8 * i : 8 * i + 8, at] = values[i][0]
            ref[32 + 8 * i : 40 + 8 * i, at] = values[i][1]

    def chunk(i):
        return pl.ds(pl.multiple_of(i * WIDE, WIDE), WIDE)

    def wait_all(ref, sem):
        pltpu.make_async_copy(ref, ref, sem).wait()

    def to_stn(src, dst, sem):
        def send(d, _):
            pltpu.make_async_remote_copy(
                src_ref=src(stn_peer(d)),
                dst_ref=dst,
                send_sem=sem.at[0],
                recv_sem=sem.at[1],
                device_id=(chan, stn_peer(d)),
                device_id_type=MESH,
            ).start()
            return 0

        lax.fori_loop(1, blocks, send, 0)

    def to_chan(src, dst, sem):
        def send(d, _):
            pltpu.make_async_remote_copy(
                src_ref=src,
                dst_ref=dst,
                send_sem=sem.at[0],
                recv_sem=sem.at[1],
                device_id=(chan_peer(d), stn),
                device_id_type=MESH,
            ).start()
            return 0

        lax.fori_loop(1, chans, send, 0)

    def fit_of(step):
        wait_all(fits.at[step, pl.ds(0, chans - 1)], f_sem.at[step, 1])
        got = [jnp.zeros((32, 128), f32)] * TERMS
        for f in range(chans):
            value = fits[step, f]
            got = [got[t] + f32(table[f, t]) * value for t in range(TERMS)]
        return [g * f32(1.0 / chans) for g in got]

    def consensus_of(fit):
        value = my_basis[0] * fit[0]
        for t in range(1, TERMS):
            value = value + my_basis[t] * fit[t]
        return value

    def one_pass(it, _):
        packed = gain[...]
        top, rest = halves(jnp.concatenate([packed, swap(packed)], axis=0))
        both = jnp.dot(
            jnp.concatenate([top, rest], axis=0), spread_p[...], preferred_element_type=f32
        )
        gain_p[...] = both[0:64] + both[64:128]

        def back_terms(i, _):
            at = chunk(i)
            h = product(entries(gain_p, at), entries(coherent, at))
            keep(back, at, h)
            for n, part in enumerate(gram_of_adjoint(h)):
                parts_q[8 * n : 8 * n + 8, at] = part
            return 0

        lax.fori_loop(0, chunks, back_terms, 0)

        @pl.when(it > 0)
        def _():
            wait_all(gains.at[it - 1, pl.ds(0, blocks - 1)], g_sem.at[it - 1, 1])
            for j in range(blocks // 2):
                a = gains[it - 1, 2 * j]
                b = gains[it - 1, 2 * j + 1]
                whole[0:32, 128 * j : 128 * j + 128] = jnp.where(low_32, a, swap(b))
                whole[32:64, 128 * j : 128 * j + 128] = jnp.where(low_32, swap(a), b)

        top, rest = halves(whole[...])
        both = jnp.dot(
            jnp.concatenate([top, rest], axis=0), spread_q[...], preferred_element_type=f32
        )
        gain_q[...] = both[0:64] + both[64:128]

        def residuals(i, total):
            at = chunk(i)
            y = product_with_adjoint(entries(coherent, at), entries(gain_q, at))
            keep(toward, at, y)
            g = product(entries(gain_p, at), y)
            x = []
            e = None
            for n in range(4):
                pair = []
                for part in range(2):
                    value = g[n][part]
                    left = vis[n + 4 * part : n + 4 * part + 1, at] - jnp.sum(value, axis=0, keepdims=True)
                    e = left * left if e is None else e + left * left
                    pair.append(left + value)
                x.append(tuple(pair))
            keep(target, at, x)
            energy[:, at] = e
            return total + e

        total = lax.fori_loop(0, chunks, residuals, jnp.zeros((1, WIDE), f32))
        e_src[it] = total
        e_stn[it, stn] = total
        to_stn(lambda _: e_src.at[it], e_stn.at[it, stn], e_sem.at[0, it])

        def sums_of(i):
            at = chunk(i)
            y, x, h = entries(toward, at), entries(target, at), entries(back, at)
            b = product_with_adjoint(x, y)
            for n, part in enumerate(gram(y) + [v[0] for v in b] + [v[1] for v in b]):
                parts_p[8 * n : 8 * n + 8, at] = part
            b = adjoint_product(x, h)
            for n, part in enumerate([v[0] for v in b] + [v[1] for v in b]):
                parts_q[32 + 8 * n : 40 + 8 * n, at] = part

        def early(i, _):
            sums_of(i)
            return 0

        lax.fori_loop(0, chunks // 2, early, 0)
        wait_all(e_stn.at[it, pl.ds(0, blocks - 1)], e_sem.at[0, it, 1])
        total = e_stn[it, 0]
        for n in range(1, blocks):
            total = total + e_stn[it, n]
        e_row[it] = total
        e_chan[it, chan] = total
        to_chan(e_row.at[it], e_chan.at[it, chan], e_sem.at[1, it])
        lax.fori_loop(chunks // 2, chunks, early, 0)
        wait_all(e_chan.at[it, pl.ds(0, chans - 1)], e_sem.at[1, it, 1])
        total = e_chan[it, 0]
        for n in range(1, chans):
            total = total + e_chan[it, n]
        noise = jnp.sum(total, axis=1, keepdims=True) * f32(1.0 / samples) + TINY
        scale = jnp.broadcast_to(1.0 / noise, (1, WIDE))

        def weigh(i, _):
            at = chunk(i)
            weight = (NU + 2.0) / (NU + energy[:, at] * scale)
            for n in range(6):
                top, rest = halves(parts_q[16 * n : 16 * n + 16, at] * weight)
                wide_q[16 * n : 16 * n + 16, at] = top
                wide_q[96 + 16 * n : 112 + 16 * n, at] = rest
                top, rest = halves(parts_p[16 * n : 16 * n + 16, at] * weight)
                wide_p[16 * n : 16 * n + 16, at] = top
                wide_p[96 + 16 * n : 112 + 16 * n, at] = rest
            return 0

        lax.fori_loop(0, chunks, weigh, 0)
        for j in range(blocks // 2):
            both = jnp.dot(
                wide_q[...], collect_q[:, 128 * j : 128 * j + 128], preferred_element_type=f32
            )
            both = both[0:96] + both[96:192]
            for n, (a, b) in enumerate(PAIRS):
                a, b = both[8 * a : 8 * a + 8], both[8 * b : 8 * b + 8]
                sums_src[it, 2 * j, 8 * n : 8 * n + 8, :] = jnp.where(low_8, a, swap(b))
                sums_src[it, 2 * j + 1, 8 * n : 8 * n + 8, :] = jnp.where(low_8, swap(a), b)
        to_stn(lambda peer: sums_src.at[it, peer], sums.at[it, stn], s_sem.at[it])
        both = jnp.dot(wide_p[...], collect_p[...], preferred_element_type=f32)
        both = both[0:96] + both[96:192]
        for n, (a, b) in enumerate(PAIRS):
            a, b = both[8 * a : 8 * a + 8], both[8 * b : 8 * b + 8]
            sums[it, stn, 8 * n : 8 * n + 8, :] = (
                jnp.where(low_8, a, swap(b)) + sums_src[it, stn, 8 * n : 8 * n + 8, :]
            )

        @pl.when(it == INNER)
        def _():
            consensus = consensus_of(fit_of(0))
            after = dual[...] + gain[...] - consensus
            dual[...] = after
            anchor[...] = consensus - after

        wait_all(sums.at[it, pl.ds(0, blocks - 1)], s_sem.at[it, 1])
        got = sums[it, 0]
        for n in range(1, blocks):
            got = got + sums[it, n]
        diag, cross = got[0:8], got[8:16]
        d1, d2 = diag + rho, swap(diag) + rho
        cr, ci = cross, swap(cross)
        over = 1.0 / (d1 * d2 - cr * cr - ci * ci)
        right = []
        for n in range(4):
            value = got[16 + 8 * n : 24 + 8 * n] + rho * anchor[8 * n : 8 * n + 8, :]
            right.append((value, swap(value)))
        up = (cr * over, ci * over)
        s1, s2 = d2 * over, d1 * over
        solved = []
        for r in range(2):
            x, y = right[2 * r], right[2 * r + 1]
            one = mul_conj(y, up)
            two = mul(x, up)
            solved.append((x[0] * s1 - one[0], x[1] * s1 - one[1]))
            solved.append((y[0] * s2 - two[0], y[1] * s2 - two[1]))
        for n in range(4):
            value = 0.5 * (gain[8 * n : 8 * n + 8, :] + jnp.where(low_8, solved[n][0], swap(solved[n][1])))
            gain[8 * n : 8 * n + 8, :] = value

        @pl.when(it < PASSES - 1)
        def _():
            gains_src[it] = gain[...]
            gains[it, stn] = gain[...]
            to_stn(lambda _: gains_src.at[it], gains.at[it, stn], g_sem.at[it])

        @pl.when(lax.rem(it, INNER) == INNER - 1)
        def _():
            step = lax.div(it, INNER)
            fits_src[step] = gain[...] + dual[...]
            fits[step, chan] = gain[...] + dual[...]
            to_chan(fits_src.at[step], fits.at[step, chan], f_sem.at[step])

        return 0

    lax.fori_loop(0, PASSES, one_pass, 0)

    fit = fit_of(STEPS - 1)
    consensus = consensus_of(fit)
    final = gain[...]
    after = dual[...] + final - consensus
    gain_out[0:32, :] = final[:, 0:64]
    gain_out[32:64, :] = swap(final)[:, 0:64]
    dual_out[0:32, :] = after[:, 0:64]
    dual_out[32:64, :] = swap(after)[:, 0:64]
    for t in range(TERMS):
        fit_out[64 * t : 64 * t + 32, :] = fit[t][:, 0:64]
        fit_out[64 * t + 32 : 64 * t + 64, :] = swap(fit[t])[:, 0:64]

    def sent(it, _):
        wait_all(e_stn.at[it, pl.ds(0, blocks - 1)], e_sem.at[0, it, 0])
        wait_all(e_chan.at[it, pl.ds(0, chans - 1)], e_sem.at[1, it, 0])
        wait_all(sums.at[it, pl.ds(0, blocks - 1)], s_sem.at[it, 0])
        return 0

    def sent_gains(it, _):
        wait_all(gains.at[it, pl.ds(0, blocks - 1)], g_sem.at[it, 0])
        return 0

    def sent_fits(step, _):
        wait_all(fits.at[step, pl.ds(0, chans - 1)], f_sem.at[step, 0])
        return 0

    lax.fori_loop(0, PASSES, sent, 0)
    lax.fori_loop(0, PASSES - 1, sent_gains, 0)
    lax.fori_loop(0, STEPS, sent_fits, 0)


def solution(mesh):
    chans, blocks = mesh.shape["chan"], mesh.shape["stn"]
    table = basis_table(chans)

    def body(vis, model, pointing, pairs, gains, poly, dual, rhos):
        baselines = vis.shape[2]
        stations = gains.shape[3]

        def run(*refs):
            kernel(chans, blocks, table, *refs)

        any_spec = pl.BlockSpec(memory_space=pl.ANY)
        smem = pl.BlockSpec(memory_space=pltpu.SMEM)
        vmem = pl.BlockSpec(memory_space=pltpu.VMEM)
        dma = pltpu.SemaphoreType.DMA
        big = lambda rows, dtype=f32: pltpu.VMEM((rows, baselines), dtype)
        state = pltpu.VMEM((32, 128), f32)
        out = pl.pallas_call(
            run,
            out_shape=(
                jax.ShapeDtypeStruct((64, 64), f32),
                jax.ShapeDtypeStruct((64, 64), f32),
                jax.ShapeDtypeStruct((64 * TERMS, 64), f32),
            ),
            in_specs=[smem, smem] + [any_spec] * 6,
            out_specs=(vmem, vmem, vmem),
            scratch_shapes=[
                big(8),
                big(128),
                pltpu.VMEM((2, baselines), jnp.int32),
                pltpu.VMEM((64, 128), f32),
                pltpu.VMEM((64 * TERMS, 128), f32),
                pltpu.VMEM((64, 128), f32),
                pltpu.VMEM((64, stations), f32),
                big(64),
                big(stations, bf16),
                pltpu.VMEM((baselines, stations), bf16),
                big(128, bf16),
                pltpu.VMEM((baselines, 128), bf16),
                big(64),
                big(64),
                big(64),
                big(64),
                big(64),
                big(1),
                big(96),
                big(96),
                big(192, bf16),
                big(192, bf16),
                state,
                state,
                state,
                pltpu.VMEM((PASSES, 1, 128), f32),
                pltpu.VMEM((PASSES, 1, 128), f32),
                pltpu.VMEM((PASSES, blocks, 1, 128), f32),
                pltpu.VMEM((PASSES, chans, 1, 128), f32),
                pltpu.VMEM((PASSES, blocks, 48, 128), f32),
                pltpu.VMEM((PASSES, blocks, 48, 128), f32),
                pltpu.VMEM((PASSES - 1, 32, 128), f32),
                pltpu.VMEM((PASSES - 1, blocks, 32, 128), f32),
                pltpu.VMEM((STEPS, 32, 128), f32),
                pltpu.VMEM((STEPS, chans, 32, 128), f32),
                dma((7,)),
                dma((2, PASSES, 2)),
                dma((PASSES, 2)),
                dma((PASSES - 1, 2)),
                dma((STEPS, 2)),
            ],
            compiler_params=pltpu.CompilerParams(
                collective_id=0, has_side_effects=True, vmem_limit_bytes=40 << 20
            ),
            name="calibrate",
        )(
            pointing.reshape(SOURCES),
            rhos,
            vis.reshape(8, baselines),
            model.reshape(8 * SOURCES, baselines),
            pairs,
            gains.reshape(64, stations),
            poly.reshape(64 * TERMS, stations),
            dual.reshape(64, stations),
        )
        return (
            out[0].reshape(1, 8, PATHS, 64),
            out[1].reshape(1, 8, PATHS, 64),
            out[2].reshape(TERMS, 8, PATHS, 64),
        )

    return jax.shard_map(
        body,
        mesh=mesh,
        in_specs=(
            P("chan", None, "stn"),
            P("chan", None, None, "stn"),
            P(),
            P(None, "stn"),
            P("chan", None, None, None),
            P(),
            P("chan", None, None, None),
            P(),
        ),
        out_specs=(
            P("chan", None, None, "stn"),
            P("chan", None, None, "stn"),
            P(None, None, None, "stn"),
        ),
        check_vma=False,
    )
```

```python
import numpy as np
import jax
import jax.numpy as jnp
from jax import lax
from jax.experimental import pallas as pl
from jax.experimental.pallas import tpu as pltpu
from jax.sharding import PartitionSpec as P

PATHS = 8
SOURCES = 16
TERMS = 3
STEPS = 2
INNER = 2
PASSES = STEPS * INNER
NU = 2.0
TINY = 1e-06
MESH = pl.DeviceIdType.MESH
WIDE = 128
PAIRS = ((0, 1), (2, 3), (4, 8), (5, 9), (6, 10), (7, 11))
bf16 = jnp.bfloat16
f32 = jnp.float32


def basis_table(count):
    frequency = (2.0 * np.arange(count, dtype=np.float32) + 1.0) / np.float32(count) - 1.0
    columns = []
    for degree in range(TERMS):
        column = (frequency**degree).astype(np.float32)
        for earlier in columns:
            column = column - np.sum(earlier * column) / np.float32(count) * earlier
        column = column / np.sqrt(np.sum(column * column) / np.float32(count))
        columns.append(column.astype(np.float32))
    return np.stack(columns, axis=1)


def mul(a, b):
    return (a[0] * b[0] - a[1] * b[1], a[0] * b[1] + a[1] * b[0])


def mul_conj(a, b):
    return (a[0] * b[0] + a[1] * b[1], a[1] * b[0] - a[0] * b[1])


def conj_mul(a, b):
    return (a[0] * b[0] + a[1] * b[1], a[0] * b[1] - a[1] * b[0])


def add(a, b):
    return (a[0] + b[0], a[1] + b[1])


def product(a, b):
    return [
        add(mul(a[0], b[0]), mul(a[1], b[2])),
        add(mul(a[0], b[1]), mul(a[1], b[3])),
        add(mul(a[2], b[0]), mul(a[3], b[2])),
        add(mul(a[2], b[1]), mul(a[3], b[3])),
    ]


def product_with_adjoint(a, b):
    return [
        add(mul_conj(a[0], b[0]), mul_conj(a[1], b[1])),
        add(mul_conj(a[0], b[2]), mul_conj(a[1], b[3])),
        add(mul_conj(a[2], b[0]), mul_conj(a[3], b[1])),
        add(mul_conj(a[2], b[2]), mul_conj(a[3], b[3])),
    ]


def adjoint_product(a, b):
    return [
        add(conj_mul(a[0], b[0]), conj_mul(a[2], b[2])),
        add(conj_mul(a[0], b[1]), conj_mul(a[2], b[3])),
        add(conj_mul(a[1], b[0]), conj_mul(a[3], b[2])),
        add(conj_mul(a[1], b[1]), conj_mul(a[3], b[3])),
    ]


def power(a):
    return a[0] * a[0] + a[1] * a[1]


def gram(y):
    cross = add(mul_conj(y[0], y[2]), mul_conj(y[1], y[3]))
    return [power(y[0]) + power(y[1]), power(y[2]) + power(y[3]), cross[0], cross[1]]


def gram_of_adjoint(h):
    cross = add(conj_mul(h[0], h[1]), conj_mul(h[2], h[3]))
    return [power(h[0]) + power(h[2]), power(h[1]) + power(h[3]), cross[0], cross[1]]


def halves(x):
    top = x.astype(bf16)
    return top, (x - top.astype(f32)).astype(bf16)


def swap(x):
    return pltpu.roll(x, 64, 1)


def low(shape):
    return lax.broadcasted_iota(jnp.int32, shape, 1) < 64


def kernel(
    chans,
    blocks,
    table,
    pointing,
    rhos,
    vis_hbm,
    model_hbm,
    pairs_hbm,
    gain_hbm,
    poly_hbm,
    dual_hbm,
    gain_out,
    dual_out,
    fit_out,
    vis,
    model,
    pairs,
    gain_tile,
    poly_tile,
    dual_tile,
    whole,
    coherent,
    spread_q,
    collect_q,
    spread_p,
    collect_p,
    gain_p,
    gain_q,
    back,
    toward,
    target,
    energy,
    parts_p,
    parts_q,
    wide_p,
    wide_q,
    gain,
    dual,
    anchor,
    e_src,
    e_all,
    sums_src,
    sums,
    gains_src,
    gains,
    fits_src,
    fits,
    load_sem,
    e_sem,
    s_sem,
    g_sem,
    f_sem,
):
    chan = lax.axis_index("chan")
    stn = lax.axis_index("stn")
    baselines = vis.shape[1]
    stations = whole.shape[1]
    chunks = baselines // WIDE
    samples = float(chans * blocks * baselines)

    def stn_peer(d):
        return lax.rem(stn + d, blocks)

    def chan_peer(d):
        return lax.rem(chan + d, chans)

    everyone = chans * blocks
    me = chan * blocks + stn

    def any_peer(d):
        peer = lax.rem(me + d, everyone)
        return (lax.div(peer, blocks), lax.rem(peer, blocks))

    barrier = pltpu.get_barrier_semaphore()

    def greet(d, _):
        pl.semaphore_signal(barrier, inc=1, device_id=any_peer(d), device_id_type=MESH)
        return 0

    lax.fori_loop(1, everyone, greet, 0)

    lane_start = pl.multiple_of(lax.div(stn, 2) * 128, 128)
    loads = [
        pltpu.make_async_copy(pairs_hbm, pairs, load_sem.at[0]),
        pltpu.make_async_copy(model_hbm, model, load_sem.at[1]),
        pltpu.make_async_copy(gain_hbm.at[:, pl.ds(lane_start, 128)], gain_tile, load_sem.at[2]),
        pltpu.make_async_copy(gain_hbm, whole, load_sem.at[3]),
        pltpu.make_async_copy(vis_hbm, vis, load_sem.at[4]),
        pltpu.make_async_copy(poly_hbm.at[:, pl.ds(lane_start, 128)], poly_tile, load_sem.at[5]),
        pltpu.make_async_copy(dual_hbm.at[:, pl.ds(lane_start, 128)], dual_tile, load_sem.at[6]),
    ]
    for copy in loads:
        copy.start()

    loads[0].wait()
    first = pairs[0:1, :] - stn * 64
    second = pairs[1:2, :]
    row = lax.broadcasted_iota(jnp.int32, (128, baselines), 0)
    spread_p[...] = jnp.where(row == first, 1.0, 0.0).astype(bf16)
    for j in range(stations // 128):
        spread_q[128 * j : 128 * j + 128, :] = jnp.where(row + 128 * j == second, 1.0, 0.0).astype(bf16)
    column = lax.broadcasted_iota(jnp.int32, (baselines, 128), 1).astype(f32)
    first_t = jnp.broadcast_to(first.astype(f32), (128, baselines)).T
    second_t = jnp.broadcast_to(second.astype(f32), (128, baselines)).T
    collect_p[...] = jnp.where(column == first_t, 1.0, 0.0).astype(bf16)
    for j in range(stations // 128):
        collect_q[:, 128 * j : 128 * j + 128] = jnp.where(
            column + 128.0 * j == second_t, 1.0, 0.0
        ).astype(bf16)

    lane = lax.broadcasted_iota(jnp.int32, (64, 128), 1)
    high_row = lax.broadcasted_iota(jnp.int32, (64, 128), 0)
    point = jnp.zeros((64, 128), jnp.int32)
    for s in range(SOURCES):
        point = jnp.where(lane % SOURCES == s, pointing[s], point)
    member = jnp.where(
        (high_row // PATHS == lane // SOURCES) & (high_row % PATHS == point), 1.0, 0.0
    ).astype(bf16)
    loads[1].wait()

    def combine(i, _):
        at = pl.ds(pl.multiple_of(i * 256, 256), 256)
        m = model[:, at]
        m0 = m.astype(bf16)
        rest = m - m0.astype(f32)
        m1 = rest.astype(bf16)
        m2 = (rest - m1.astype(f32)).astype(bf16)
        coherent[:, at] = (
            jnp.dot(member, m0, preferred_element_type=f32)
            + jnp.dot(member, m1, preferred_element_type=f32)
            + jnp.dot(member, m2, preferred_element_type=f32)
        )
        return 0

    lax.fori_loop(0, baselines // 256, combine, 0)

    low_32 = low((32, 128))

    def own(re, im):
        return jnp.where(
            lax.rem(stn, 2) == 0,
            jnp.where(low_32, re, swap(im)),
            jnp.where(low_32, swap(re), im),
        )

    def mine(t):
        value = f32(0.0)
        for f in range(chans):
            value = jnp.where(chan == f, f32(table[f, t]), value)
        return value

    my_basis = [mine(t) for t in range(TERMS)]
    for copy in loads[2:]:
        copy.wait()
    gain[...] = own(gain_tile[0:32, :], gain_tile[32:64, :])
    dual[...] = own(dual_tile[0:32, :], dual_tile[32:64, :])
    start = jnp.zeros((32, 128), f32)
    for t in range(TERMS):
        start = start + my_basis[t] * own(
            poly_tile[64 * t : 64 * t + 32, :], poly_tile[64 * t + 32 : 64 * t + 64, :]
        )
    anchor[...] = start - dual[...]

    k_row = lax.broadcasted_iota(jnp.int32, (PATHS, 128), 0)
    rho = jnp.zeros((PATHS, 128), f32)
    for k in range(PATHS):
        rho = jnp.where(k_row == k, rhos[k], rho)
    low_8 = low((8, 128))

    pl.semaphore_wait(barrier, everyone - 1)

    def entries(ref, at):
        return [(ref[8 * i : 8 * i + 8, at], ref[32 + 8 * i : 40 + 8 * i, at]) for i in range(4)]

    def keep(ref, at, values):
        for i in range(4):
            ref[8 * i : 8 * i + 8, at] = values[i][0]
            ref[32 + 8 * i : 40 + 8 * i, at] = values[i][1]

    def chunk(i):
        return pl.ds(pl.multiple_of(i * WIDE, WIDE), WIDE)

    def wait_all(ref, sem):
        pltpu.make_async_copy(ref, ref, sem).wait()

    def to_stn(src, dst, sem):
        def send(d, _):
            pltpu.make_async_remote_copy(
                src_ref=src(stn_peer(d)),
                dst_ref=dst,
                send_sem=sem.at[0],
                recv_sem=sem.at[1],
                device_id=(chan, stn_peer(d)),
                device_id_type=MESH,
            ).start()
            return 0

        lax.fori_loop(1, blocks, send, 0)

    def to_chan(src, dst, sem):
        def send(d, _):
            pltpu.make_async_remote_copy(
                src_ref=src,
                dst_ref=dst,
                send_sem=sem.at[0],
                recv_sem=sem.at[1],
                device_id=(chan_peer(d), stn),
                device_id_type=MESH,
            ).start()
            return 0

        lax.fori_loop(1, chans, send, 0)

    def to_all(src, dst, sem):
        def send(d, _):
            pltpu.make_async_remote_copy(
                src_ref=src,
                dst_ref=dst,
                send_sem=sem.at[0],
                recv_sem=sem.at[1],
                device_id=any_peer(d),
                device_id_type=MESH,
            ).start()
            return 0

        lax.fori_loop(1, everyone, send, 0)

    def fit_of(step):
        wait_all(fits.at[step, pl.ds(0, chans - 1)], f_sem.at[step, 1])
        got = [jnp.zeros((32, 128), f32)] * TERMS
        for f in range(chans):
            value = fits[step, f]
            got = [got[t] + f32(table[f, t]) * value for t in range(TERMS)]
        return [g * f32(1.0 / chans) for g in got]

    def consensus_of(fit):
        value = my_basis[0] * fit[0]
        for t in range(1, TERMS):
            value = value + my_basis[t] * fit[t]
        return value

    def one_pass(it, _):
        packed = gain[...]
        top, rest = halves(jnp.concatenate([packed, swap(packed)], axis=0))
        both = jnp.dot(
            jnp.concatenate([top, rest], axis=0), spread_p[...], preferred_element_type=f32
        )
        gain_p[...] = both[0:64] + both[64:128]

        def back_terms(i, _):
            at = chunk(i)
            h = product(entries(gain_p, at), entries(coherent, at))
            keep(back, at, h)
            for n, part in enumerate(gram_of_adjoint(h)):
                parts_q[8 * n : 8 * n + 8, at] = part
            return 0

        lax.fori_loop(0, chunks, back_terms, 0)

        @pl.when(it > 0)
        def _():
            wait_all(gains.at[it - 1, pl.ds(0, blocks - 1)], g_sem.at[it - 1, 1])
            for j in range(blocks // 2):
                a = gains[it - 1, 2 * j]
                b = gains[it - 1, 2 * j + 1]
                whole[0:32, 128 * j : 128 * j + 128] = jnp.where(low_32, a, swap(b))
                whole[32:64, 128 * j : 128 * j + 128] = jnp.where(low_32, swap(a), b)

        top, rest = halves(whole[...])
        both = jnp.dot(
            jnp.concatenate([top, rest], axis=0), spread_q[...], preferred_element_type=f32
        )
        gain_q[...] = both[0:64] + both[64:128]

        def residuals(i, total):
            at = chunk(i)
            y = product_with_adjoint(entries(coherent, at), entries(gain_q, at))
            keep(toward, at, y)
            g = product(entries(gain_p, at), y)
            x = []
            e = None
            for n in range(4):
                pair = []
                for part in range(2):
                    value = g[n][part]
                    left = vis[n + 4 * part : n + 4 * part + 1, at] - jnp.sum(value, axis=0, keepdims=True)
                    e = left * left if e is None else e + left * left
                    pair.append(left + value)
                x.append(tuple(pair))
            keep(target, at, x)
            energy[:, at] = e
            return total + e

        total = lax.fori_loop(0, chunks, residuals, jnp.zeros((1, WIDE), f32))
        e_src[it] = total
        e_all[it, me] = total
        to_all(e_src.at[it], e_all.at[it, me], e_sem.at[it])

        def sums_of(i):
            at = chunk(i)
            y, x, h = entries(toward, at), entries(target, at), entries(back, at)
            b = product_with_adjoint(x, y)
            for n, part in enumerate(gram(y) + [v[0] for v in b] + [v[1] for v in b]):
                parts_p[8 * n : 8 * n + 8, at] = part
            b = adjoint_product(x, h)
            for n, part in enumerate([v[0] for v in b] + [v[1] for v in b]):
                parts_q[32 + 8 * n : 40 + 8 * n, at] = part

        def early(i, _):
            sums_of(i)
            return 0

        lax.fori_loop(0, chunks, early, 0)
        wait_all(e_all.at[it, pl.ds(0, chans * blocks - 1)], e_sem.at[it, 1])
        total = jnp.sum(e_all[it], axis=0)
        noise = jnp.sum(total, axis=1, keepdims=True) * f32(1.0 / samples) + TINY
        scale = jnp.broadcast_to(1.0 / noise, (1, WIDE))

        def weigh(i, _):
            at = chunk(i)
            weight = (NU + 2.0) / (NU + energy[:, at] * scale)
            for n in range(6):
                top, rest = halves(parts_q[16 * n : 16 * n + 16, at] * weight)
                wide_q[16 * n : 16 * n + 16, at] = top
                wide_q[96 + 16 * n : 112 + 16 * n, at] = rest
                top, rest = halves(parts_p[16 * n : 16 * n + 16, at] * weight)
                wide_p[16 * n : 16 * n + 16, at] = top
                wide_p[96 + 16 * n : 112 + 16 * n, at] = rest
            return 0

        lax.fori_loop(0, chunks, weigh, 0)
        for j in range(blocks // 2):
            both = jnp.dot(
                wide_q[...], collect_q[:, 128 * j : 128 * j + 128], preferred_element_type=f32
            )
            both = both[0:96] + both[96:192]
            for n, (a, b) in enumerate(PAIRS):
                a, b = both[8 * a : 8 * a + 8], both[8 * b : 8 * b + 8]
                sums_src[it, 2 * j, 8 * n : 8 * n + 8, :] = jnp.where(low_8, a, swap(b))
                sums_src[it, 2 * j + 1, 8 * n : 8 * n + 8, :] = jnp.where(low_8, swap(a), b)
        to_stn(lambda peer: sums_src.at[it, peer], sums.at[it, stn], s_sem.at[it])
        both = jnp.dot(wide_p[...], collect_p[...], preferred_element_type=f32)
        both = both[0:96] + both[96:192]
        for n, (a, b) in enumerate(PAIRS):
            a, b = both[8 * a : 8 * a + 8], both[8 * b : 8 * b + 8]
            sums[it, stn, 8 * n : 8 * n + 8, :] = (
                jnp.where(low_8, a, swap(b)) + sums_src[it, stn, 8 * n : 8 * n + 8, :]
            )

        @pl.when(it == INNER)
        def _():
            consensus = consensus_of(fit_of(0))
            after = dual[...] + gain[...] - consensus
            dual[...] = after
            anchor[...] = consensus - after

        wait_all(sums.at[it, pl.ds(0, blocks - 1)], s_sem.at[it, 1])
        got = sums[it, 0]
        for n in range(1, blocks):
            got = got + sums[it, n]
        diag, cross = got[0:8], got[8:16]
        d1, d2 = diag + rho, swap(diag) + rho
        cr, ci = cross, swap(cross)
        over = 1.0 / (d1 * d2 - cr * cr - ci * ci)
        right = []
        for n in range(4):
            value = got[16 + 8 * n : 24 + 8 * n] + rho * anchor[8 * n : 8 * n + 8, :]
            right.append((value, swap(value)))
        up = (cr * over, ci * over)
        s1, s2 = d2 * over, d1 * over
        solved = []
        for r in range(2):
            x, y = right[2 * r], right[2 * r + 1]
            one = mul_conj(y, up)
            two = mul(x, up)
            solved.append((x[0] * s1 - one[0], x[1] * s1 - one[1]))
            solved.append((y[0] * s2 - two[0], y[1] * s2 - two[1]))
        for n in range(4):
            value = 0.5 * (gain[8 * n : 8 * n + 8, :] + jnp.where(low_8, solved[n][0], swap(solved[n][1])))
            gain[8 * n : 8 * n + 8, :] = value

        @pl.when(it < PASSES - 1)
        def _():
            gains_src[it] = gain[...]
            gains[it, stn] = gain[...]
            to_stn(lambda _: gains_src.at[it], gains.at[it, stn], g_sem.at[it])

        @pl.when(lax.rem(it, INNER) == INNER - 1)
        def _():
            step = lax.div(it, INNER)
            fits_src[step] = gain[...] + dual[...]
            fits[step, chan] = gain[...] + dual[...]
            to_chan(fits_src.at[step], fits.at[step, chan], f_sem.at[step])

        return 0

    lax.fori_loop(0, PASSES, one_pass, 0)

    fit = fit_of(STEPS - 1)
    consensus = consensus_of(fit)
    final = gain[...]
    after = dual[...] + final - consensus
    gain_out[0:32, :] = final[:, 0:64]
    gain_out[32:64, :] = swap(final)[:, 0:64]
    dual_out[0:32, :] = after[:, 0:64]
    dual_out[32:64, :] = swap(after)[:, 0:64]
    for t in range(TERMS):
        fit_out[64 * t : 64 * t + 32, :] = fit[t][:, 0:64]
        fit_out[64 * t + 32 : 64 * t + 64, :] = swap(fit[t])[:, 0:64]

    def sent(it, _):
        wait_all(e_all.at[it, pl.ds(0, chans * blocks - 1)], e_sem.at[it, 0])
        wait_all(sums.at[it, pl.ds(0, blocks - 1)], s_sem.at[it, 0])
        return 0

    def sent_gains(it, _):
        wait_all(gains.at[it, pl.ds(0, blocks - 1)], g_sem.at[it, 0])
        return 0

    def sent_fits(step, _):
        wait_all(fits.at[step, pl.ds(0, chans - 1)], f_sem.at[step, 0])
        return 0

    lax.fori_loop(0, PASSES, sent, 0)
    lax.fori_loop(0, PASSES - 1, sent_gains, 0)
    lax.fori_loop(0, STEPS, sent_fits, 0)


def solution(mesh):
    chans, blocks = mesh.shape["chan"], mesh.shape["stn"]
    table = basis_table(chans)

    def body(vis, model, pointing, pairs, gains, poly, dual, rhos):
        baselines = vis.shape[2]
        stations = gains.shape[3]

        def run(*refs):
            kernel(chans, blocks, table, *refs)

        any_spec = pl.BlockSpec(memory_space=pltpu.HBM)
        smem = pl.BlockSpec(memory_space=pltpu.SMEM)
        vmem = pl.BlockSpec(memory_space=pltpu.VMEM)
        dma = pltpu.SemaphoreType.DMA
        big = lambda rows, dtype=f32: pltpu.VMEM((rows, baselines), dtype)
        state = pltpu.VMEM((32, 128), f32)
        out = pl.pallas_call(
            run,
            out_shape=(
                jax.ShapeDtypeStruct((64, 64), f32),
                jax.ShapeDtypeStruct((64, 64), f32),
                jax.ShapeDtypeStruct((64 * TERMS, 64), f32),
            ),
            in_specs=[smem, smem] + [any_spec] * 6,
            out_specs=(vmem, vmem, vmem),
            scratch_shapes=[
                big(8),
                big(128),
                pltpu.VMEM((2, baselines), jnp.int32),
                pltpu.VMEM((64, 128), f32),
                pltpu.VMEM((64 * TERMS, 128), f32),
                pltpu.VMEM((64, 128), f32),
                pltpu.VMEM((64, stations), f32),
                big(64),
                big(stations, bf16),
                pltpu.VMEM((baselines, stations), bf16),
                big(128, bf16),
                pltpu.VMEM((baselines, 128), bf16),
                big(64),
                big(64),
                big(64),
                big(64),
                big(64),
                big(1),
                big(96),
                big(96),
                big(192, bf16),
                big(192, bf16),
                state,
                state,
                state,
                pltpu.VMEM((PASSES, 1, 128), f32),
                pltpu.VMEM((PASSES, chans * blocks, 1, 128), f32),
                pltpu.VMEM((PASSES, blocks, 48, 128), f32),
                pltpu.VMEM((PASSES, blocks, 48, 128), f32),
                pltpu.VMEM((PASSES - 1, 32, 128), f32),
                pltpu.VMEM((PASSES - 1, blocks, 32, 128), f32),
                pltpu.VMEM((STEPS, 32, 128), f32),
                pltpu.VMEM((STEPS, chans, 32, 128), f32),
                dma((7,)),
                dma((PASSES, 2)),
                dma((PASSES, 2)),
                dma((PASSES - 1, 2)),
                dma((STEPS, 2)),
            ],
            compiler_params=pltpu.CompilerParams(
                collective_id=0, has_side_effects=True, vmem_limit_bytes=62 << 20
            ),
            name="calibrate",
        )(
            pointing.reshape(SOURCES),
            rhos,
            vis.reshape(8, baselines),
            model.reshape(8 * SOURCES, baselines),
            pairs,
            gains.reshape(64, stations),
            poly.reshape(64 * TERMS, stations),
            dual.reshape(64, stations),
        )
        return (
            out[0].reshape(1, 8, PATHS, 64),
            out[1].reshape(1, 8, PATHS, 64),
            out[2].reshape(TERMS, 8, PATHS, 64),
        )

    return jax.shard_map(
        body,
        mesh=mesh,
        in_specs=(
            P("chan", None, "stn"),
            P("chan", None, None, "stn"),
            P(),
            P(None, "stn"),
            P("chan", None, None, None),
            P(),
            P("chan", None, None, None),
            P(),
        ),
        out_specs=(
            P("chan", None, None, "stn"),
            P("chan", None, None, "stn"),
            P(None, None, None, "stn"),
        ),
        check_vma=False,
    )
```

```python
import numpy as np
import jax
import jax.numpy as jnp
from jax import lax
from jax.experimental import pallas as pl
from jax.experimental.pallas import tpu as pltpu
from jax.sharding import PartitionSpec as P

PATHS = 8
SOURCES = 16
TERMS = 3
STEPS = 2
INNER = 2
PASSES = STEPS * INNER
NU = 2.0
TINY = 1e-06
LOGICAL = pl.DeviceIdType.LOGICAL
WIDE = 128
bf16 = jnp.bfloat16
f32 = jnp.float32


def basis_table(count):
    frequency = (2.0 * np.arange(count, dtype=np.float32) + 1.0) / np.float32(count) - 1.0
    columns = []
    for degree in range(TERMS):
        column = (frequency**degree).astype(np.float32)
        for earlier in columns:
            column = column - np.sum(earlier * column) / np.float32(count) * earlier
        column = column / np.sqrt(np.sum(column * column) / np.float32(count))
        columns.append(column.astype(np.float32))
    return np.stack(columns, axis=1)


def mul(a, b):
    return (a[0] * b[0] - a[1] * b[1], a[0] * b[1] + a[1] * b[0])


def mul_conj(a, b):
    return (a[0] * b[0] + a[1] * b[1], a[1] * b[0] - a[0] * b[1])


def conj_mul(a, b):
    return (a[0] * b[0] + a[1] * b[1], a[0] * b[1] - a[1] * b[0])


def add(a, b):
    return (a[0] + b[0], a[1] + b[1])


def product(a, b):
    return [
        add(mul(a[0], b[0]), mul(a[1], b[2])),
        add(mul(a[0], b[1]), mul(a[1], b[3])),
        add(mul(a[2], b[0]), mul(a[3], b[2])),
        add(mul(a[2], b[1]), mul(a[3], b[3])),
    ]


def product_with_adjoint(a, b):
    return [
        add(mul_conj(a[0], b[0]), mul_conj(a[1], b[1])),
        add(mul_conj(a[0], b[2]), mul_conj(a[1], b[3])),
        add(mul_conj(a[2], b[0]), mul_conj(a[3], b[1])),
        add(mul_conj(a[2], b[2]), mul_conj(a[3], b[3])),
    ]


def adjoint_product(a, b):
    return [
        add(conj_mul(a[0], b[0]), conj_mul(a[2], b[2])),
        add(conj_mul(a[0], b[1]), conj_mul(a[2], b[3])),
        add(conj_mul(a[1], b[0]), conj_mul(a[3], b[2])),
        add(conj_mul(a[1], b[1]), conj_mul(a[3], b[3])),
    ]


def power(a):
    return a[0] * a[0] + a[1] * a[1]


def gram(y):
    cross = add(mul_conj(y[0], y[2]), mul_conj(y[1], y[3]))
    return [power(y[0]) + power(y[1]), power(y[2]) + power(y[3]), cross[0], cross[1]]


def gram_of_adjoint(h):
    cross = add(conj_mul(h[0], h[1]), conj_mul(h[2], h[3]))
    return [power(h[0]) + power(h[2]), power(h[1]) + power(h[3]), cross[0], cross[1]]


def halves(x):
    top = x.astype(bf16)
    return top, (x - top.astype(f32)).astype(bf16)


def swap(x):
    return pltpu.roll(x, 64, 1)


def take(table, index):
    return jnp.take_along_axis(table, index, axis=1, mode="promise_in_bounds")


def masks_by_hops(everyone):
    hop = (0, 1, 2, 1)
    hops = lambda m: hop[m >> 1 & 3] + hop[m >> 3 & 3] + hop[m >> 5 & 3]
    return sorted(range(1, everyone), key=lambda m: (-hops(m), m))


SCRATCH = []


def scratch(name, *shape, dtype=f32):
    SCRATCH.append((name, pltpu.VMEM(shape, dtype)))


def lay_out(chans, blocks, baselines, stations):
    SCRATCH.clear()
    everyone = chans * blocks
    scratch("vis", 8, baselines)
    scratch("model", 8 * SOURCES, baselines)
    scratch("pairs", 2, baselines, dtype=jnp.int32)
    scratch("whole", 64 * stations // 128, 128)
    scratch("poly", 64 * TERMS * stations // 128, 128)
    scratch("dual_in", 64 * stations // 128, 128)
    scratch("coherent", 64, baselines)
    scratch("d_src", baselines // 128 * 64, 128)
    scratch("d_all", baselines // 128 * 64, 128)
    scratch("d_own", 64, baselines)
    scratch("pairs_all", blocks, 2, baselines, dtype=jnp.int32)
    scratch("index_p", blocks, baselines, dtype=jnp.int32)
    scratch("index_q", blocks, baselines, dtype=jnp.int32)
    scratch("table_q", 8 * stations // 128 * 8, 128)
    scratch("table_p", 64, 128)
    scratch("collect_p", blocks * 128, baselines, dtype=bf16)
    scratch("collect_q", blocks * 128, baselines, dtype=bf16)
    scratch("in_tile", blocks * 4 * 16, baselines, dtype=bf16)
    scratch("toward", 64, baselines)
    scratch("terms", 64, baselines)
    scratch("back", 64, baselines)
    scratch("parts_p", baselines // 128 * 16 * blocks, 128)
    scratch("parts_q", baselines // 128 * 16 * blocks, 128)
    scratch("weights", blocks, baselines)
    scratch("sums", 128, 128)
    scratch("gain", 64, 128)
    scratch("anchor", 64, 128)
    scratch("dual", stations // 16, 128)
    scratch("e_src", PASSES, 1, 128)
    scratch("e_all", PASSES, everyone, 1, 128)
    scratch("r_src", PASSES, baselines // 16, 128)
    scratch("r_all", PASSES, blocks * baselines // 16, 128)
    scratch("g_src", PASSES, stations // 16, 128)
    scratch("g_all", PASSES, blocks * stations // 16, 128)
    scratch("f_src", stations // 16, 128)
    scratch("f_all", chans, stations // 16, 128)
    scratch("s_src", blocks, 4, 128)
    scratch("s_all", everyone, 4, 128)
    scratch("j_src", blocks, 4, 128)
    scratch("j_all", blocks, 4, 128)
    scratch("unpack", 32, 128)
    dma = pltpu.SemaphoreType.DMA
    SCRATCH.append(("load_sem", dma((3 + 3 * stations // 128,))))
    for name, *shape in (
        ("p_sem", 2),
        ("d_sem", 2),
        ("e_sem", PASSES, 2),
        ("r_sem", PASSES, 2),
        ("g_sem", PASSES, 2),
        ("f_sem", 2),
        ("s_sem", 2),
        ("j_sem", 2),
    ):
        SCRATCH.append((name, dma(tuple(shape))))


class Held:
    def __init__(self, refs):
        for (name, _), ref in zip(SCRATCH, refs, strict=True):
            setattr(self, name, ref)


def kernel(
    chans,
    blocks,
    table,
    pointing,
    rhos,
    vis_hbm,
    model_hbm,
    pairs_hbm,
    gain_hbm,
    poly_hbm,
    dual_hbm,
    gain_out,
    dual_out,
    fit_out,
    *refs,
):
    v = Held(refs)
    stations = gain_hbm.shape[1]
    chan = lax.axis_index("chan")
    stn = lax.axis_index("stn")
    everyone = chans * blocks
    me = chan * blocks + stn
    baselines = v.vis.shape[1]
    tiles = stations // 128
    chunks = baselines // WIDE
    samples = float(everyone * baselines)

    flips = [(1 - 2 * lax.rem(lax.div(me, 1 << n), 2)) * (1 << n) for n in range(7)]

    def flipped(mask, start, count, base):
        for n in range(count):
            if mask >> n & 1:
                base = base + flips[start + n]
        return base

    uppers = [flipped(m, 4, 3, me) for m in range(8)]
    lowers = [flipped(m, 0, 4, 0) for m in range(16)]
    masks = masks_by_hops(everyone)

    def peer_of(mask):
        return uppers[mask >> 4] + lowers[mask & 15]

    stn_masks = [m for m in masks if m < blocks]
    chan_masks = [m for m in masks if m % blocks == 0]

    barrier = pltpu.get_barrier_semaphore()
    for mask in masks:
        pl.semaphore_signal(barrier, inc=1, device_id=peer_of(mask), device_id_type=LOGICAL)

    moves = [(model_hbm, v.model), (pairs_hbm, v.pairs), (vis_hbm, v.vis)]
    for src, dst in ((gain_hbm, v.whole), (dual_hbm, v.dual_in), (poly_hbm, v.poly)):
        rows = src.shape[0]
        moves += [
            (src.at[:, pl.ds(128 * j, 128)], dst.at[pl.ds(rows * j, rows)]) for j in range(tiles)
        ]
    loads = [pltpu.make_async_copy(a, b, v.load_sem.at[n]) for n, (a, b) in enumerate(moves)]
    for copy in loads:
        copy.start()

    def remote(src, dst, sem, peer):
        pltpu.make_async_remote_copy(
            src_ref=src,
            dst_ref=dst,
            send_sem=sem.at[0],
            recv_sem=sem.at[1],
            device_id=peer,
            device_id_type=LOGICAL,
        ).start()

    def to_stn(src, dst, sem):
        for mask in stn_masks:
            remote(src(stn + lowers[mask]), dst, sem, peer_of(mask))

    def wait_all(ref, sem):
        pltpu.make_async_copy(ref, ref, sem).wait()

    def chunk(i):
        return pl.ds(pl.multiple_of(i * WIDE, WIDE), WIDE)

    def entries(ref, at):
        return [(ref[8 * i : 8 * i + 8, at], ref[32 + 8 * i : 40 + 8 * i, at]) for i in range(4)]

    def keep(ref, at, values):
        for i in range(4):
            ref[8 * i : 8 * i + 8, at] = values[i][0]
            ref[32 + 8 * i : 40 + 8 * i, at] = values[i][1]

    def as_entries(values):
        return [(values[i], values[4 + i]) for i in range(4)]

    def picked(tile_of, index):
        within, tile = index & 127, index >> 7
        out = []
        for c in range(8):
            value = take(tile_of(c, 0), within)
            for j in range(1, tiles):
                value = jnp.where(tile == j, take(tile_of(c, j), within), value)
            out.append(value)
        return as_entries(out)

    lane = lax.broadcasted_iota(jnp.int32, (128, 128), 1)
    high = lax.broadcasted_iota(jnp.int32, (128, 128), 0)
    point = jnp.zeros((128, 128), jnp.int32)
    for s in range(SOURCES):
        point = jnp.where(lane % SOURCES == s, pointing[s], point)
    left, right = high % 64 // PATHS, high % PATHS
    component = jnp.where(high < 64, left, right)
    direction = jnp.where(high < 64, right, left)
    member = jnp.where((component == lane // SOURCES) & (direction == point), 1.0, 0.0).astype(bf16)
    loads[0].wait()

    def combine(i, _):
        at = pl.ds(pl.multiple_of(i * 256, 256), 256)
        m = v.model[:, at]
        m0 = m.astype(bf16)
        rest = m - m0.astype(f32)
        m1 = rest.astype(bf16)
        m2 = (rest - m1.astype(f32)).astype(bf16)
        both = (
            jnp.dot(member, m0, preferred_element_type=f32)
            + jnp.dot(member, m1, preferred_element_type=f32)
            + jnp.dot(member, m2, preferred_element_type=f32)
        )
        v.coherent[:, at] = both[0:64]
        for k in range(PATHS):
            for j in range(2):
                rows = pl.ds(pl.multiple_of(64 * k + 8 * (2 * i + j), 8), 8)
                v.d_src[rows] = both[64 + 8 * k : 72 + 8 * k, 128 * j : 128 * j + 128]
        return 0

    lax.fori_loop(0, baselines // 256, combine, 0)

    def mine(t):
        value = f32(0.0)
        for f in range(chans):
            value = jnp.where(chan == f, f32(table[f, t]), value)
        return value

    my_basis = [mine(t) for t in range(TERMS)]
    for copy in loads[1:]:
        copy.wait()

    def consensus_of(fit):
        value = my_basis[0] * fit[0]
        for t in range(1, TERMS):
            value = value + my_basis[t] * fit[t]
        return value

    def to_tiles(ref, rows):
        for j in range(tiles):
            ref[pl.ds(j, 8, stride=8), :] = rows[8 * j : 8 * j + 8]

    def own_of(ref, rows, start):
        return jnp.concatenate(
            [ref[pl.ds(rows * j + start + stn, 8, stride=8), :] for j in range(tiles)], axis=0
        )

    v.gain[...] = jnp.zeros((64, 128), f32)
    v.anchor[...] = jnp.zeros((64, 128), f32)
    v.sums[...] = jnp.zeros((128, 128), f32)
    to_tiles(v.gain, own_of(v.whole, 64, 0))
    dual_rows = own_of(v.dual_in, 64, 0)
    v.dual[...] = dual_rows
    to_tiles(v.anchor, consensus_of([own_of(v.poly, 64 * TERMS, 64 * t) for t in range(TERMS)]) - dual_rows)
    rho = rhos[stn]

    def keep_part(ref, i, n, value):
        ref[pl.ds(16 * blocks * i + n, blocks, stride=16), :] = value

    zeros = jnp.zeros((8, WIDE), f32)
    for n in range(12, 16):
        for i in range(chunks):
            keep_part(v.parts_p, i, n, zeros)
            keep_part(v.parts_q, i, n, zeros)
    sub = lax.broadcasted_iota(jnp.int32, (8, 128), 0)
    own_tile = pl.multiple_of(lax.div(stn, 2) * 64, 64)

    def spread_tables():
        rows = [v.gain[pl.ds(j, 8, stride=8), :] for j in range(tiles)]
        for c in range(8):
            per_block = None
            for j in range(tiles):
                value = jnp.broadcast_to(rows[j][c : c + 1], (8, 128))
                at = 8 * (c * tiles + j)
                v.table_q[at : at + 8, :] = value
                per_block = value if j == 0 else jnp.where(sub // 2 == j, value, per_block)
            v.table_p[8 * c : 8 * c + 8, :] = per_block

    def own_terms(i, _):
        at = chunk(i)
        d = entries(v.d_own, at)
        p = v.index_p[:, at]
        gain_p = as_entries([take(v.table_p[8 * c : 8 * c + 8, :], p) for c in range(8)])
        h = product(gain_p, d)
        keep(v.back, at, h)
        for n, part in enumerate(gram_of_adjoint(h)):
            keep_part(v.parts_q, i, n, part)

        def tile_of(c, j):
            return v.table_q[8 * (c * tiles + j) : 8 * (c * tiles + j) + 8, :]

        y = product_with_adjoint(d, picked(tile_of, v.index_q[:, at]))
        keep(v.toward, at, y)
        for n, part in enumerate(gram(y)):
            keep_part(v.parts_p, i, n, part)
        keep(v.terms, at, product(gain_p, y))
        return 0

    own_g, own_r = stations // 16, baselines // 16
    g_rows = pl.ds(pl.multiple_of(own_g * stn, own_g), own_g)
    r_rows = pl.ds(pl.multiple_of(own_r * stn, own_r), own_r)

    def one_pass(it, _):
        spread_tables()

        @pl.when(it > 0)
        def _():
            lax.fori_loop(0, chunks, own_terms, 0)
            wait_all(v.g_all.at[it - 1, pl.ds(0, (blocks - 1) * own_g)], v.g_sem.at[it - 1, 1])
            for j in range(tiles):
                for c in range(8):
                    v.whole[64 * j + 8 * c : 64 * j + 8 * c + 8] = v.g_all[
                        it - 1, pl.ds(8 * j + c, blocks, stride=own_g), :
                    ]

        def residuals(i, total):
            at = chunk(i)
            first = jnp.broadcast_to(v.pairs[0:1, at], (8, WIDE)) & 127
            second = jnp.broadcast_to(v.pairs[1:2, at], (8, WIDE))

            def tile_of(c, j):
                return v.whole[64 * j + 8 * c : 64 * j + 8 * c + 8]

            y = product_with_adjoint(entries(v.coherent, at), picked(tile_of, second))
            gain_p = as_entries(
                [take(v.whole[pl.ds(own_tile + 8 * c, 8)], first) for c in range(8)]
            )
            g = product(gain_p, y)
            e = None
            for n in range(4):
                for part in range(2):
                    c = n + 4 * part
                    left = v.vis[c : c + 1, at] - jnp.sum(g[n][part], axis=0, keepdims=True)
                    e = left * left if e is None else e + left * left
                    v.r_src[it, pl.ds(8 * i + c, 1)] = left
            return total + e

        total = lax.fori_loop(0, chunks, residuals, jnp.zeros((1, WIDE), f32))
        v.e_src[it] = total
        v.e_all[it, me] = total
        v.r_all[it, r_rows] = v.r_src[it]

        @pl.when(it == 0)
        def _():
            pl.semaphore_wait(barrier, everyone - 1)

        to_stn(lambda _: v.r_src.at[it], v.r_all.at[it, r_rows], v.r_sem.at[it])
        for mask in masks:
            remote(v.e_src.at[it], v.e_all.at[it, me], v.e_sem.at[it], peer_of(mask))

        @pl.when(it == 0)
        def _():
            to_stn(lambda _: v.pairs, v.pairs_all.at[stn], v.p_sem)
            to_stn(
                lambda peer: v.d_src.at[pl.ds(pl.multiple_of(own_r * peer, own_r), own_r)],
                v.d_all.at[r_rows],
                v.d_sem,
            )
            v.pairs_all[stn] = v.pairs[...]
            v.d_all[r_rows] = v.d_src[r_rows]
            wait_all(v.pairs_all.at[pl.ds(0, blocks - 1)], v.p_sem.at[1])
            row = lax.broadcasted_iota(jnp.int32, (128, baselines), 0)
            for i in range(blocks):
                first = v.pairs_all[i, 0:1, :]
                second = v.pairs_all[i, 1:2, :]
                v.index_p[i : i + 1, :] = first & 127
                v.index_q[i : i + 1, :] = second
                v.collect_p[128 * i : 128 * i + 128, :] = jnp.where(row == (first & 127), 1.0, 0.0).astype(bf16)
                v.collect_q[128 * i : 128 * i + 128, :] = jnp.where(row == (second & 127), 1.0, 0.0).astype(bf16)
                for j in range(tiles):
                    inside = jnp.where((second >> 7) == j, 1.0, 0.0)
                    at = 16 * (4 * i + j)
                    v.in_tile[at : at + 16, :] = jnp.broadcast_to(inside, (16, baselines)).astype(bf16)
            wait_all(v.d_all.at[pl.ds(0, (blocks - 1) * own_r)], v.d_sem.at[1])
            for i in range(chunks):
                at = slice(WIDE * i, WIDE * i + WIDE)
                for c in range(8):
                    v.d_own[8 * c : 8 * c + 8, at] = v.d_all[pl.ds(8 * i + c, blocks, stride=own_r), :]
            lax.fori_loop(0, chunks, own_terms, 0)

        wait_all(v.r_all.at[it, pl.ds(0, (blocks - 1) * own_r)], v.r_sem.at[it, 1])

        def products(i, _):
            at = chunk(i)
            y, h, g = entries(v.toward, at), entries(v.back, at), entries(v.terms, at)
            r = as_entries([v.r_all[it, pl.ds(8 * i + c, blocks, stride=own_r), :] for c in range(8)])
            v.weights[:, at] = power(r[0]) + power(r[1]) + power(r[2]) + power(r[3])
            x = [add(a, b) for a, b in zip(r, g)]
            b = product_with_adjoint(x, y)
            for n, part in enumerate([z[0] for z in b] + [z[1] for z in b]):
                keep_part(v.parts_p, i, 4 + n, part)
            b = adjoint_product(x, h)
            for n, part in enumerate([z[0] for z in b] + [z[1] for z in b]):
                keep_part(v.parts_q, i, 4 + n, part)
            return 0

        lax.fori_loop(0, chunks, products, 0)

        @pl.when(it == INNER)
        def _():
            wait_all(v.f_all.at[pl.ds(0, chans - 1)], v.f_sem.at[1])
            fit = [jnp.zeros((own_g, 128), f32)] * TERMS
            for f in range(chans):
                value = v.f_all[f]
                fit = [fit[t] + f32(table[f, t]) * value for t in range(TERMS)]
            consensus = consensus_of([z * f32(1.0 / chans) for z in fit])
            after = v.f_src[...] - consensus
            v.dual[...] = after
            to_tiles(v.anchor, consensus - after)

        wait_all(v.e_all.at[it, pl.ds(0, everyone - 1)], v.e_sem.at[it, 1])
        total = jnp.sum(v.e_all[it], axis=0)
        noise = jnp.sum(total, axis=1, keepdims=True) * f32(1.0 / samples) + TINY
        scale = jnp.broadcast_to(1.0 / noise, (1, 128))
        scale = jnp.concatenate([scale] * (baselines // 128), axis=1)
        v.weights[...] = (NU + 2.0) / (NU + v.weights[...] * scale)

        def collected(left, right):
            return lax.dot_general(left, right, (((1,), (1,)), ((), ())), preferred_element_type=f32)

        def block_of(ref, i):
            return jnp.concatenate(
                [ref[16 * (blocks * n + i) : 16 * (blocks * n + i) + 16, :] for n in range(chunks)], axis=1
            )

        got = [jnp.zeros((32, 128), f32) for _ in range(tiles)]
        for i in range(blocks):
            weight = v.weights[i : i + 1, :]
            wide = jnp.concatenate(halves(block_of(v.parts_p, i) * weight), axis=0)
            got[i // 2] = got[i // 2] + collected(wide, v.collect_p[128 * i : 128 * i + 128, :])
            top, rest = halves(block_of(v.parts_q, i) * weight)
            pieces = []
            for j in range(tiles):
                inside = v.in_tile[16 * (4 * i + j) : 16 * (4 * i + j) + 16, :]
                pieces += [top * inside, rest * inside]
            both = collected(jnp.concatenate(pieces, axis=0), v.collect_q[128 * i : 128 * i + 128, :])
            for j in range(tiles):
                got[j] = got[j] + both[32 * j : 32 * j + 32]
        for j in range(tiles):
            v.sums[pl.ds(j, 16, stride=8), :] = got[j][0:16] + got[j][16:32]

        def part(n):
            return v.sums[8 * n : 8 * n + 8, :]

        d1, d2, cr, ci = part(0) + rho, part(1) + rho, part(2), part(3)
        over = 1.0 / (d1 * d2 - cr * cr - ci * ci)
        right = as_entries([part(4 + n) + rho * v.anchor[8 * n : 8 * n + 8, :] for n in range(8)])
        up = (cr * over, ci * over)
        s1, s2 = d2 * over, d1 * over
        solved = []
        for r in range(2):
            x, y = right[2 * r], right[2 * r + 1]
            one = mul_conj(y, up)
            two = mul(x, up)
            solved.append((x[0] * s1 - one[0], x[1] * s1 - one[1]))
            solved.append((y[0] * s2 - two[0], y[1] * s2 - two[1]))
        for n in range(4):
            for k in range(2):
                at = 8 * (n + 4 * k)
                v.gain[at : at + 8, :] = 0.5 * (v.gain[at : at + 8, :] + solved[n][k])
        for j in range(tiles):
            v.g_src[it, 8 * j : 8 * j + 8, :] = v.gain[pl.ds(j, 8, stride=8), :]

        @pl.when(it < PASSES - 1)
        def _():
            to_stn(lambda _: v.g_src.at[it], v.g_all.at[it, g_rows], v.g_sem.at[it])
            v.g_all[it, g_rows] = v.g_src[it]

        @pl.when(it == INNER - 1)
        def _():
            v.f_src[...] = v.g_src[it] + v.dual[...]
            v.f_all[chan] = v.f_src[...]
            for mask in chan_masks:
                remote(v.f_src, v.f_all.at[chan], v.f_sem, peer_of(mask))

        return 0

    lax.fori_loop(0, PASSES, one_pass, 0)

    low = lax.broadcasted_iota(jnp.int32, (8, 128), 1) < 64

    def slices(ref, rows):
        for j in range(tiles):
            a = rows[8 * j : 8 * j + 8]
            under = pltpu.roll(a, 4, 0)
            ref[2 * j] = jnp.where(low, a, swap(under))[0:4]
            ref[2 * j + 1] = jnp.where(low, swap(a), under)[0:4]

    last = v.g_src[PASSES - 1]
    slices(v.s_src, last + v.dual[...])
    slices(v.j_src, last)
    for mask in masks:
        block = stn + lowers[mask & 7]
        remote(v.s_src.at[block], v.s_all.at[me], v.s_sem, peer_of(mask))
    to_stn(lambda peer: v.j_src.at[peer], v.j_all.at[stn], v.j_sem)
    v.s_all[me] = v.s_src[stn]
    v.j_all[stn] = v.j_src[stn]
    wait_all(v.j_all.at[pl.ds(0, blocks - 1)], v.j_sem.at[1])

    def give(ref, start, value):
        v.unpack[...] = value
        for n in range(4):
            rows = v.unpack[pl.ds(n, 8, stride=4), :]
            ref[start + 8 * n : start + 8 * n + 8, :] = rows[:, 0:64]
            ref[start + 32 + 8 * n : start + 40 + 8 * n, :] = swap(rows)[:, 0:64]

    give(gain_out, 0, v.j_all[...].reshape(32, 128))
    wait_all(v.s_all.at[pl.ds(0, everyone - 1)], v.s_sem.at[1])
    fit = [jnp.zeros((32, 128), f32)] * TERMS
    for f in range(chans):
        value = v.s_all[blocks * f : blocks * f + blocks].reshape(32, 128)
        fit = [fit[t] + f32(table[f, t]) * value for t in range(TERMS)]
    fit = [z * f32(1.0 / chans) for z in fit]
    for t in range(TERMS):
        give(fit_out, 64 * t, fit[t])
    give(dual_out, 0, v.s_all[pl.ds(blocks * chan, blocks)].reshape(32, 128) - consensus_of(fit))

    wait_all(v.pairs_all.at[pl.ds(0, blocks - 1)], v.p_sem.at[0])
    wait_all(v.d_all.at[pl.ds(0, (blocks - 1) * own_r)], v.d_sem.at[0])
    wait_all(v.f_all.at[pl.ds(0, chans - 1)], v.f_sem.at[0])
    wait_all(v.s_all.at[pl.ds(0, everyone - 1)], v.s_sem.at[0])
    wait_all(v.j_all.at[pl.ds(0, blocks - 1)], v.j_sem.at[0])
    for it in range(PASSES):
        wait_all(v.e_all.at[it, pl.ds(0, everyone - 1)], v.e_sem.at[it, 0])
        wait_all(v.r_all.at[it, pl.ds(0, (blocks - 1) * own_r)], v.r_sem.at[it, 0])
        if it < PASSES - 1:
            wait_all(v.g_all.at[it, pl.ds(0, (blocks - 1) * own_g)], v.g_sem.at[it, 0])


def solution(mesh):
    chans, blocks = mesh.shape["chan"], mesh.shape["stn"]
    table = basis_table(chans)

    def body(vis, model, pointing, pairs, gains, poly, dual, rhos):
        baselines = vis.shape[2]
        stations = gains.shape[3]

        def run(*refs):
            kernel(chans, blocks, table, *refs)

        any_spec = pl.BlockSpec(memory_space=pltpu.HBM)
        smem = pl.BlockSpec(memory_space=pltpu.SMEM)
        vmem = pl.BlockSpec(memory_space=pltpu.VMEM)
        lay_out(chans, blocks, baselines, stations)
        out = pl.pallas_call(
            run,
            out_shape=(
                jax.ShapeDtypeStruct((64, 64), f32),
                jax.ShapeDtypeStruct((64, 64), f32),
                jax.ShapeDtypeStruct((64 * TERMS, 64), f32),
            ),
            in_specs=[smem, smem] + [any_spec] * 6,
            out_specs=(vmem, vmem, vmem),
            scratch_shapes=[shape for _, shape in SCRATCH],
            compiler_params=pltpu.CompilerParams(
                collective_id=0, has_side_effects=True, vmem_limit_bytes=62 << 20
            ),
            name="calibrate",
        )(
            pointing.reshape(SOURCES),
            rhos,
            vis.reshape(8, baselines),
            model.reshape(8 * SOURCES, baselines),
            pairs,
            gains.reshape(64, stations),
            poly.reshape(64 * TERMS, stations),
            dual.reshape(64, stations),
        )
        return (
            out[0].reshape(1, 8, PATHS, 64),
            out[1].reshape(1, 8, PATHS, 64),
            out[2].reshape(TERMS, 8, PATHS, 64),
        )

    return jax.shard_map(
        body,
        mesh=mesh,
        in_specs=(
            P("chan", None, "stn"),
            P("chan", None, None, "stn"),
            P(),
            P(None, "stn"),
            P("chan", None, None, None),
            P(),
            P("chan", None, None, None),
            P(),
        ),
        out_specs=(
            P("chan", None, None, "stn"),
            P("chan", None, None, "stn"),
            P(None, None, None, "stn"),
        ),
        check_vma=False,
    )
```

```python
import numpy as np
import jax
import jax.numpy as jnp
from jax import lax
from jax.experimental import pallas as pl
from jax.experimental.pallas import tpu as pltpu
from jax.sharding import PartitionSpec as P

PATHS = 8
SOURCES = 16
TERMS = 3
STEPS = 2
INNER = 2
PASSES = STEPS * INNER
NU = 2.0
TINY = 1e-06
LOGICAL = pl.DeviceIdType.LOGICAL
WIDE = 128
bf16 = jnp.bfloat16
f32 = jnp.float32


def basis_table(count):
    frequency = (2.0 * np.arange(count, dtype=np.float32) + 1.0) / np.float32(count) - 1.0
    columns = []
    for degree in range(TERMS):
        column = (frequency**degree).astype(np.float32)
        for earlier in columns:
            column = column - np.sum(earlier * column) / np.float32(count) * earlier
        column = column / np.sqrt(np.sum(column * column) / np.float32(count))
        columns.append(column.astype(np.float32))
    return np.stack(columns, axis=1)


def mul(a, b):
    return (a[0] * b[0] - a[1] * b[1], a[0] * b[1] + a[1] * b[0])


def mul_conj(a, b):
    return (a[0] * b[0] + a[1] * b[1], a[1] * b[0] - a[0] * b[1])


def conj_mul(a, b):
    return (a[0] * b[0] + a[1] * b[1], a[0] * b[1] - a[1] * b[0])


def add(a, b):
    return (a[0] + b[0], a[1] + b[1])


def product(a, b):
    return [
        add(mul(a[0], b[0]), mul(a[1], b[2])),
        add(mul(a[0], b[1]), mul(a[1], b[3])),
        add(mul(a[2], b[0]), mul(a[3], b[2])),
        add(mul(a[2], b[1]), mul(a[3], b[3])),
    ]


def product_with_adjoint(a, b):
    return [
        add(mul_conj(a[0], b[0]), mul_conj(a[1], b[1])),
        add(mul_conj(a[0], b[2]), mul_conj(a[1], b[3])),
        add(mul_conj(a[2], b[0]), mul_conj(a[3], b[1])),
        add(mul_conj(a[2], b[2]), mul_conj(a[3], b[3])),
    ]


def adjoint_product(a, b):
    return [
        add(conj_mul(a[0], b[0]), conj_mul(a[2], b[2])),
        add(conj_mul(a[0], b[1]), conj_mul(a[2], b[3])),
        add(conj_mul(a[1], b[0]), conj_mul(a[3], b[2])),
        add(conj_mul(a[1], b[1]), conj_mul(a[3], b[3])),
    ]


def power(a):
    return a[0] * a[0] + a[1] * a[1]


def gram(y):
    cross = add(mul_conj(y[0], y[2]), mul_conj(y[1], y[3]))
    return [power(y[0]) + power(y[1]), power(y[2]) + power(y[3]), cross[0], cross[1]]


def gram_of_adjoint(h):
    cross = add(conj_mul(h[0], h[1]), conj_mul(h[2], h[3]))
    return [power(h[0]) + power(h[2]), power(h[1]) + power(h[3]), cross[0], cross[1]]


def halves(x):
    top = x.astype(bf16)
    return top, (x - top.astype(f32)).astype(bf16)


def swap(x):
    return pltpu.roll(x, 64, 1)


def take(table, index):
    return jnp.take_along_axis(table, index, axis=1, mode="promise_in_bounds")


def masks_by_hops(everyone):
    hop = (0, 1, 2, 1)
    hops = lambda m: hop[m >> 1 & 3] + hop[m >> 3 & 3] + hop[m >> 5 & 3]
    return sorted(range(1, everyone), key=lambda m: (-hops(m), m))


SCRATCH = []


def scratch(name, *shape, dtype=f32):
    SCRATCH.append((name, pltpu.VMEM(shape, dtype)))


def lay_out(chans, blocks, baselines, stations):
    SCRATCH.clear()
    everyone = chans * blocks
    scratch("vis", 8, baselines)
    scratch("model", 8 * SOURCES, baselines)
    scratch("pairs", 2, baselines, dtype=jnp.int32)
    scratch("whole", 64 * stations // 128, 128)
    scratch("poly", 64 * TERMS * stations // 128, 128)
    scratch("dual_in", 64 * stations // 128, 128)
    scratch("coherent", 64, baselines)
    scratch("d_src", baselines // 128 * 64, 128)
    scratch("d_all", baselines // 128 * 64, 128)
    scratch("d_own", 64, baselines)
    scratch("pairs_all", blocks, 2, baselines, dtype=jnp.int32)
    scratch("index_p", blocks, baselines, dtype=jnp.int32)
    scratch("index_q", blocks, baselines, dtype=jnp.int32)
    scratch("table_q", 8 * stations // 128 * 8, 128)
    scratch("table_p", 64, 128)
    scratch("collect", blocks * baselines, 256, dtype=bf16)
    scratch("wide", 160, blocks * baselines, dtype=bf16)
    scratch("in_tile", blocks * 4 * 16, baselines, dtype=bf16)
    scratch("toward", 64, baselines)
    scratch("terms", 64, baselines)
    scratch("back", 64, baselines)
    scratch("parts_p", baselines // 128 * 16 * blocks, 128)
    scratch("parts_q", baselines // 128 * 16 * blocks, 128)
    scratch("weights", blocks, baselines)
    scratch("sums", 128, 128)
    scratch("gain", 64, 128)
    scratch("anchor", 64, 128)
    scratch("dual", stations // 16, 128)
    scratch("e_src", PASSES, 1, 128)
    scratch("e_all", PASSES, everyone, 1, 128)
    scratch("r_src", PASSES, baselines // 16, 128)
    scratch("r_all", PASSES, blocks * baselines // 16, 128)
    scratch("g_src", PASSES, stations // 16, 128)
    scratch("g_all", PASSES, blocks * stations // 16, 128)
    scratch("f_src", stations // 16, 128)
    scratch("f_all", chans, stations // 16, 128)
    scratch("s_src", blocks, 4, 128)
    scratch("s_all", everyone, 4, 128)
    scratch("j_src", blocks, 4, 128)
    scratch("j_all", blocks, 4, 128)
    dma = pltpu.SemaphoreType.DMA
    SCRATCH.append(("load_sem", dma((3 + 3 * stations // 128,))))
    for name, *shape in (
        ("p_sem", 2),
        ("d_sem", 2),
        ("e_sem", PASSES, 2),
        ("r_sem", PASSES, 2),
        ("g_sem", PASSES, 2),
        ("f_sem", 2),
        ("s_sem", 2),
        ("j_sem", 2),
    ):
        SCRATCH.append((name, dma(tuple(shape))))


class Held:
    def __init__(self, refs):
        for (name, _), ref in zip(SCRATCH, refs, strict=True):
            setattr(self, name, ref)


def kernel(
    chans,
    blocks,
    table,
    pointing,
    rhos,
    vis_hbm,
    model_hbm,
    pairs_hbm,
    gain_hbm,
    poly_hbm,
    dual_hbm,
    packed,
    *refs,
):
    v = Held(refs)
    stations = gain_hbm.shape[1]
    chan = lax.axis_index("chan")
    stn = lax.axis_index("stn")
    everyone = chans * blocks
    me = chan * blocks + stn
    baselines = v.vis.shape[1]
    tiles = stations // 128
    chunks = baselines // WIDE
    samples = float(everyone * baselines)

    flips = [(1 - 2 * lax.rem(lax.div(me, 1 << n), 2)) * (1 << n) for n in range(7)]

    def flipped(mask, start, count, base):
        for n in range(count):
            if mask >> n & 1:
                base = base + flips[start + n]
        return base

    uppers = [flipped(m, 4, 3, me) for m in range(8)]
    lowers = [flipped(m, 0, 4, 0) for m in range(16)]
    masks = masks_by_hops(everyone)

    def peer_of(mask):
        return uppers[mask >> 4] + lowers[mask & 15]

    stn_masks = [m for m in masks if m < blocks]
    chan_masks = [m for m in masks if m % blocks == 0]

    barrier = pltpu.get_barrier_semaphore()
    for mask in masks:
        pl.semaphore_signal(barrier, inc=1, device_id=peer_of(mask), device_id_type=LOGICAL)

    moves = [(model_hbm, v.model), (pairs_hbm, v.pairs), (vis_hbm, v.vis)]
    for src, dst in ((gain_hbm, v.whole), (dual_hbm, v.dual_in), (poly_hbm, v.poly)):
        rows = src.shape[0]
        moves += [
            (src.at[:, pl.ds(128 * j, 128)], dst.at[pl.ds(rows * j, rows)]) for j in range(tiles)
        ]
    loads = [pltpu.make_async_copy(a, b, v.load_sem.at[n]) for n, (a, b) in enumerate(moves)]
    for copy in loads:
        copy.start()

    def remote(src, dst, sem, peer):
        pltpu.make_async_remote_copy(
            src_ref=src,
            dst_ref=dst,
            send_sem=sem.at[0],
            recv_sem=sem.at[1],
            device_id=peer,
            device_id_type=LOGICAL,
        ).start()

    def to_stn(src, dst, sem):
        for mask in stn_masks:
            remote(src(stn + lowers[mask]), dst, sem, peer_of(mask))

    def wait_all(ref, sem):
        pltpu.make_async_copy(ref, ref, sem).wait()

    def chunk(i):
        return pl.ds(pl.multiple_of(i * WIDE, WIDE), WIDE)

    def entries(ref, at):
        return [(ref[8 * i : 8 * i + 8, at], ref[32 + 8 * i : 40 + 8 * i, at]) for i in range(4)]

    def keep(ref, at, values):
        for i in range(4):
            ref[8 * i : 8 * i + 8, at] = values[i][0]
            ref[32 + 8 * i : 40 + 8 * i, at] = values[i][1]

    def as_entries(values):
        return [(values[i], values[4 + i]) for i in range(4)]

    def picked(tile_of, index):
        within, tile = index & 127, index >> 7
        out = []
        for c in range(8):
            value = take(tile_of(c, 0), within)
            for j in range(1, tiles):
                value = jnp.where(tile == j, take(tile_of(c, j), within), value)
            out.append(value)
        return as_entries(out)

    lane = lax.broadcasted_iota(jnp.int32, (128, 128), 1)
    high = lax.broadcasted_iota(jnp.int32, (128, 128), 0)
    point = jnp.zeros((128, 128), jnp.int32)
    for s in range(SOURCES):
        point = jnp.where(lane % SOURCES == s, pointing[s], point)
    left, right = high % 64 // PATHS, high % PATHS
    component = jnp.where(high < 64, left, right)
    direction = jnp.where(high < 64, right, left)
    member = jnp.where((component == lane // SOURCES) & (direction == point), 1.0, 0.0).astype(bf16)
    loads[0].wait()

    def combine(i, _):
        at = pl.ds(pl.multiple_of(i * 256, 256), 256)
        m = v.model[:, at]
        m0 = m.astype(bf16)
        rest = m - m0.astype(f32)
        m1 = rest.astype(bf16)
        m2 = (rest - m1.astype(f32)).astype(bf16)
        both = (
            jnp.dot(member, m0, preferred_element_type=f32)
            + jnp.dot(member, m1, preferred_element_type=f32)
            + jnp.dot(member, m2, preferred_element_type=f32)
        )
        v.coherent[:, at] = both[0:64]
        for k in range(PATHS):
            for j in range(2):
                rows = pl.ds(pl.multiple_of(64 * k + 8 * (2 * i + j), 8), 8)
                v.d_src[rows] = both[64 + 8 * k : 72 + 8 * k, 128 * j : 128 * j + 128]
        return 0

    lax.fori_loop(0, baselines // 256, combine, 0)

    def mine(t):
        value = f32(0.0)
        for f in range(chans):
            value = jnp.where(chan == f, f32(table[f, t]), value)
        return value

    my_basis = [mine(t) for t in range(TERMS)]
    for copy in loads[1:]:
        copy.wait()

    def consensus_of(fit):
        value = my_basis[0] * fit[0]
        for t in range(1, TERMS):
            value = value + my_basis[t] * fit[t]
        return value

    def to_tiles(ref, rows):
        for j in range(tiles):
            ref[pl.ds(j, 8, stride=8), :] = rows[8 * j : 8 * j + 8]

    def own_of(ref, rows, start):
        return jnp.concatenate(
            [ref[pl.ds(rows * j + start + stn, 8, stride=8), :] for j in range(tiles)], axis=0
        )

    v.gain[...] = jnp.zeros((64, 128), f32)
    v.anchor[...] = jnp.zeros((64, 128), f32)
    v.sums[...] = jnp.zeros((128, 128), f32)
    to_tiles(v.gain, own_of(v.whole, 64, 0))
    dual_rows = own_of(v.dual_in, 64, 0)
    v.dual[...] = dual_rows
    to_tiles(v.anchor, consensus_of([own_of(v.poly, 64 * TERMS, 64 * t) for t in range(TERMS)]) - dual_rows)
    rho = rhos[stn]

    def keep_part(ref, i, n, value):
        ref[pl.ds(16 * blocks * i + n, blocks, stride=16), :] = value

    zeros = jnp.zeros((8, WIDE), f32)
    for n in range(12, 16):
        for i in range(chunks):
            keep_part(v.parts_p, i, n, zeros)
            keep_part(v.parts_q, i, n, zeros)
    sub = lax.broadcasted_iota(jnp.int32, (8, 128), 0)
    own_tile = pl.multiple_of(lax.div(stn, 2) * 64, 64)

    def spread_tables():
        rows = [v.gain[pl.ds(j, 8, stride=8), :] for j in range(tiles)]
        for c in range(8):
            per_block = None
            for j in range(tiles):
                value = jnp.broadcast_to(rows[j][c : c + 1], (8, 128))
                at = 8 * (c * tiles + j)
                v.table_q[at : at + 8, :] = value
                per_block = value if j == 0 else jnp.where(sub // 2 == j, value, per_block)
            v.table_p[8 * c : 8 * c + 8, :] = per_block

    def own_terms(i, _):
        at = chunk(i)
        d = entries(v.d_own, at)
        p = v.index_p[:, at]
        gain_p = as_entries([take(v.table_p[8 * c : 8 * c + 8, :], p) for c in range(8)])
        h = product(gain_p, d)
        keep(v.back, at, h)
        for n, part in enumerate(gram_of_adjoint(h)):
            keep_part(v.parts_q, i, n, part)

        def tile_of(c, j):
            return v.table_q[8 * (c * tiles + j) : 8 * (c * tiles + j) + 8, :]

        y = product_with_adjoint(d, picked(tile_of, v.index_q[:, at]))
        keep(v.toward, at, y)
        for n, part in enumerate(gram(y)):
            keep_part(v.parts_p, i, n, part)
        keep(v.terms, at, product(gain_p, y))
        return 0

    own_g, own_r = stations // 16, baselines // 16
    g_rows = pl.ds(pl.multiple_of(own_g * stn, own_g), own_g)
    r_rows = pl.ds(pl.multiple_of(own_r * stn, own_r), own_r)

    def one_pass(it, _):
        spread_tables()

        @pl.when(it > 0)
        def _():
            lax.fori_loop(0, chunks, own_terms, 0, unroll=True)
            wait_all(v.g_all.at[it - 1, pl.ds(0, (blocks - 1) * own_g)], v.g_sem.at[it - 1, 1])
            for j in range(tiles):
                for c in range(8):
                    v.whole[64 * j + 8 * c : 64 * j + 8 * c + 8] = v.g_all[
                        it - 1, pl.ds(8 * j + c, blocks, stride=own_g), :
                    ]

        def residuals(i, total):
            at = chunk(i)
            first = jnp.broadcast_to(v.pairs[0:1, at], (8, WIDE)) & 127
            second = jnp.broadcast_to(v.pairs[1:2, at], (8, WIDE))

            def tile_of(c, j):
                return v.whole[64 * j + 8 * c : 64 * j + 8 * c + 8]

            y = product_with_adjoint(entries(v.coherent, at), picked(tile_of, second))
            gain_p = as_entries(
                [take(v.whole[pl.ds(own_tile + 8 * c, 8)], first) for c in range(8)]
            )
            g = product(gain_p, y)
            e = None
            for n in range(4):
                for part in range(2):
                    c = n + 4 * part
                    left = v.vis[c : c + 1, at] - jnp.sum(g[n][part], axis=0, keepdims=True)
                    e = left * left if e is None else e + left * left
                    v.r_src[it, pl.ds(8 * i + c, 1)] = left
            return total + e

        total = lax.fori_loop(0, chunks, residuals, jnp.zeros((1, WIDE), f32), unroll=True)
        v.e_src[it] = total
        v.e_all[it, me] = total
        v.r_all[it, r_rows] = v.r_src[it]

        @pl.when(it == 0)
        def _():
            pl.semaphore_wait(barrier, everyone - 1)
            to_stn(lambda _: v.pairs, v.pairs_all.at[stn], v.p_sem)
            to_stn(
                lambda peer: v.d_src.at[pl.ds(pl.multiple_of(own_r * peer, own_r), own_r)],
                v.d_all.at[r_rows],
                v.d_sem,
            )

        to_stn(lambda _: v.r_src.at[it], v.r_all.at[it, r_rows], v.r_sem.at[it])
        for mask in masks:
            remote(v.e_src.at[it], v.e_all.at[it, me], v.e_sem.at[it], peer_of(mask))

        @pl.when(it == 0)
        def _():
            v.pairs_all[stn] = v.pairs[...]
            v.d_all[r_rows] = v.d_src[r_rows]
            wait_all(v.pairs_all.at[pl.ds(0, blocks - 1)], v.p_sem.at[1])
            column = lax.broadcasted_iota(jnp.int32, (baselines, 128), 1).astype(f32)
            for i in range(blocks):
                first = v.pairs_all[i, 0:1, :] & 127
                second = v.pairs_all[i, 1:2, :]
                v.index_p[i : i + 1, :] = first
                v.index_q[i : i + 1, :] = second
                for start, index in ((0, second & 127), (128, first)):
                    across = jnp.broadcast_to(index.astype(f32), (128, baselines)).T
                    v.collect[baselines * i : baselines * i + baselines, start : start + 128] = jnp.where(
                        column == across, 1.0, 0.0
                    ).astype(bf16)
                for j in range(tiles):
                    inside = jnp.where((second >> 7) == j, 1.0, 0.0)
                    at = 16 * (4 * i + j)
                    v.in_tile[at : at + 16, :] = jnp.broadcast_to(inside, (16, baselines)).astype(bf16)
            wait_all(v.d_all.at[pl.ds(0, (blocks - 1) * own_r)], v.d_sem.at[1])
            for i in range(chunks):
                at = slice(WIDE * i, WIDE * i + WIDE)
                for c in range(8):
                    v.d_own[8 * c : 8 * c + 8, at] = v.d_all[pl.ds(8 * i + c, blocks, stride=own_r), :]
            lax.fori_loop(0, chunks, own_terms, 0, unroll=True)

        wait_all(v.r_all.at[it, pl.ds(0, (blocks - 1) * own_r)], v.r_sem.at[it, 1])

        def products(i, _):
            at = chunk(i)
            y, h, g = entries(v.toward, at), entries(v.back, at), entries(v.terms, at)
            r = as_entries([v.r_all[it, pl.ds(8 * i + c, blocks, stride=own_r), :] for c in range(8)])
            v.weights[:, at] = power(r[0]) + power(r[1]) + power(r[2]) + power(r[3])
            x = [add(a, b) for a, b in zip(r, g)]
            b = product_with_adjoint(x, y)
            for n, part in enumerate([z[0] for z in b] + [z[1] for z in b]):
                keep_part(v.parts_p, i, 4 + n, part)
            b = adjoint_product(x, h)
            for n, part in enumerate([z[0] for z in b] + [z[1] for z in b]):
                keep_part(v.parts_q, i, 4 + n, part)
            return 0

        lax.fori_loop(0, chunks, products, 0, unroll=True)

        @pl.when(it == INNER)
        def _():
            wait_all(v.f_all.at[pl.ds(0, chans - 1)], v.f_sem.at[1])
            fit = [jnp.zeros((own_g, 128), f32)] * TERMS
            for f in range(chans):
                value = v.f_all[f]
                fit = [fit[t] + f32(table[f, t]) * value for t in range(TERMS)]
            consensus = consensus_of([z * f32(1.0 / chans) for z in fit])
            after = v.f_src[...] - consensus
            v.dual[...] = after
            to_tiles(v.anchor, consensus - after)

        wait_all(v.e_all.at[it, pl.ds(0, everyone - 1)], v.e_sem.at[it, 1])
        total = jnp.sum(v.e_all[it], axis=0)
        noise = jnp.sum(total, axis=1, keepdims=True) * f32(1.0 / samples) + TINY
        scale = jnp.broadcast_to(1.0 / noise, (1, 128))
        scale = jnp.concatenate([scale] * (baselines // 128), axis=1)
        v.weights[...] = (NU + 2.0) / (NU + v.weights[...] * scale)

        def block_of(ref, i):
            return jnp.concatenate(
                [ref[16 * (blocks * n + i) : 16 * (blocks * n + i) + 16, :] for n in range(chunks)], axis=1
            )

        for i in range(blocks):
            weight = v.weights[i : i + 1, :]
            at = slice(baselines * i, baselines * i + baselines)
            top, rest = halves(block_of(v.parts_p, i) * weight)
            v.wide[128:144, at] = top
            v.wide[144:160, at] = rest
            top, rest = halves(block_of(v.parts_q, i) * weight)
            for j in range(tiles):
                inside = v.in_tile[16 * (4 * i + j) : 16 * (4 * i + j) + 16, :]
                v.wide[32 * j : 32 * j + 16, at] = top * inside
                v.wide[32 * j + 16 : 32 * j + 32, at] = rest * inside
        got = [jnp.zeros((32, 128), f32) for _ in range(tiles)]
        for n in range(8):
            at = slice(1 * baselines * n, 1 * baselines * (n + 1))
            every = jnp.dot(v.wide[:, at], v.collect[at, :], preferred_element_type=f32)
            got[1 * n // 2] = got[1 * n // 2] + every[128:160, 128:256]
            for j in range(tiles):
                got[j] = got[j] + every[32 * j : 32 * j + 32, 0:128]
        for j in range(tiles):
            v.sums[pl.ds(j, 16, stride=8), :] = got[j][0:16] + got[j][16:32]

        def part(n):
            return v.sums[8 * n : 8 * n + 8, :]

        d1, d2, cr, ci = part(0) + rho, part(1) + rho, part(2), part(3)
        over = 1.0 / (d1 * d2 - cr * cr - ci * ci)
        right = as_entries([part(4 + n) + rho * v.anchor[8 * n : 8 * n + 8, :] for n in range(8)])
        up = (cr * over, ci * over)
        s1, s2 = d2 * over, d1 * over
        solved = []
        for r in range(2):
            x, y = right[2 * r], right[2 * r + 1]
            one = mul_conj(y, up)
            two = mul(x, up)
            solved.append((x[0] * s1 - one[0], x[1] * s1 - one[1]))
            solved.append((y[0] * s2 - two[0], y[1] * s2 - two[1]))
        for n in range(4):
            for k in range(2):
                at = 8 * (n + 4 * k)
                v.gain[at : at + 8, :] = 0.5 * (v.gain[at : at + 8, :] + solved[n][k])
        for j in range(tiles):
            v.g_src[it, 8 * j : 8 * j + 8, :] = v.gain[pl.ds(j, 8, stride=8), :]

        @pl.when(it < PASSES - 1)
        def _():
            to_stn(lambda _: v.g_src.at[it], v.g_all.at[it, g_rows], v.g_sem.at[it])
            v.g_all[it, g_rows] = v.g_src[it]

        @pl.when(it == INNER - 1)
        def _():
            v.f_src[...] = v.g_src[it] + v.dual[...]
            v.f_all[chan] = v.f_src[...]
            for mask in chan_masks:
                remote(v.f_src, v.f_all.at[chan], v.f_sem, peer_of(mask))

        return 0

    lax.fori_loop(0, PASSES, one_pass, 0)

    low = lax.broadcasted_iota(jnp.int32, (8, 128), 1) < 64

    def slices(ref, rows):
        for j in range(tiles):
            a = rows[8 * j : 8 * j + 8]
            under = pltpu.roll(a, 4, 0)
            ref[2 * j] = jnp.where(low, a, swap(under))[0:4]
            ref[2 * j + 1] = jnp.where(low, swap(a), under)[0:4]

    last = v.g_src[PASSES - 1]
    slices(v.s_src, last + v.dual[...])
    slices(v.j_src, last)
    for mask in masks:
        block = stn + lowers[mask & 7]
        remote(v.s_src.at[block], v.s_all.at[me], v.s_sem, peer_of(mask))
    to_stn(lambda peer: v.j_src.at[peer], v.j_all.at[stn], v.j_sem)
    v.s_all[me] = v.s_src[stn]
    v.j_all[stn] = v.j_src[stn]
    wait_all(v.j_all.at[pl.ds(0, blocks - 1)], v.j_sem.at[1])

    packed[0:32, :] = v.j_all[...].reshape(32, 128)
    wait_all(v.s_all.at[pl.ds(0, everyone - 1)], v.s_sem.at[1])
    fit = [jnp.zeros((32, 128), f32)] * TERMS
    for f in range(chans):
        value = v.s_all[blocks * f : blocks * f + blocks].reshape(32, 128)
        fit = [fit[t] + f32(table[f, t]) * value for t in range(TERMS)]
    fit = [z * f32(1.0 / chans) for z in fit]
    packed[32:64, :] = v.s_all[pl.ds(blocks * chan, blocks)].reshape(32, 128) - consensus_of(fit)
    for t in range(TERMS):
        packed[64 + 32 * t : 96 + 32 * t, :] = fit[t]

    wait_all(v.pairs_all.at[pl.ds(0, blocks - 1)], v.p_sem.at[0])
    wait_all(v.d_all.at[pl.ds(0, (blocks - 1) * own_r)], v.d_sem.at[0])
    wait_all(v.f_all.at[pl.ds(0, chans - 1)], v.f_sem.at[0])
    wait_all(v.s_all.at[pl.ds(0, everyone - 1)], v.s_sem.at[0])
    wait_all(v.j_all.at[pl.ds(0, blocks - 1)], v.j_sem.at[0])
    for it in range(PASSES):
        wait_all(v.e_all.at[it, pl.ds(0, everyone - 1)], v.e_sem.at[it, 0])
        wait_all(v.r_all.at[it, pl.ds(0, (blocks - 1) * own_r)], v.r_sem.at[it, 0])
        if it < PASSES - 1:
            wait_all(v.g_all.at[it, pl.ds(0, (blocks - 1) * own_g)], v.g_sem.at[it, 0])


def unpack(packed, gain_out, dual_out, fit_out):
    spots = [(gain_out, 0), (dual_out, 0)] + [(fit_out, 64 * t) for t in range(TERMS)]
    for m, (ref, start) in enumerate(spots):
        for n in range(4):
            rows = packed[pl.ds(32 * m + n, PATHS, stride=4), :]
            ref[start + 8 * n : start + 8 * n + 8, :] = rows[:, 0:64]
            ref[start + 32 + 8 * n : start + 40 + 8 * n, :] = swap(rows)[:, 0:64]


def solution(mesh):
    chans, blocks = mesh.shape["chan"], mesh.shape["stn"]
    table = basis_table(chans)

    def body(vis, model, pointing, pairs, gains, poly, dual, rhos):
        baselines = vis.shape[2]
        stations = gains.shape[3]

        def run(*refs):
            kernel(chans, blocks, table, *refs)

        any_spec = pl.BlockSpec(memory_space=pltpu.HBM)
        smem = pl.BlockSpec(memory_space=pltpu.SMEM)
        vmem = pl.BlockSpec(memory_space=pltpu.VMEM)
        lay_out(chans, blocks, baselines, stations)
        packed = pl.pallas_call(
            run,
            out_shape=jax.ShapeDtypeStruct((32 * (2 + TERMS), 128), f32),
            in_specs=[smem, smem] + [any_spec] * 6,
            out_specs=vmem,
            scratch_shapes=[shape for _, shape in SCRATCH],
            compiler_params=pltpu.CompilerParams(
                collective_id=0, has_side_effects=True, vmem_limit_bytes=62 << 20
            ),
            name="calibrate",
        )(
            pointing.reshape(SOURCES),
            rhos,
            vis.reshape(8, baselines),
            model.reshape(8 * SOURCES, baselines),
            pairs,
            gains.reshape(64, stations),
            poly.reshape(64 * TERMS, stations),
            dual.reshape(64, stations),
        )
        out = pl.pallas_call(
            unpack,
            out_shape=(
                jax.ShapeDtypeStruct((64, 64), f32),
                jax.ShapeDtypeStruct((64, 64), f32),
                jax.ShapeDtypeStruct((64 * TERMS, 64), f32),
            ),
            in_specs=[vmem],
            out_specs=(vmem, vmem, vmem),
            compiler_params=pltpu.CompilerParams(vmem_limit_bytes=62 << 20),
            name="unpack",
        )(packed)
        return (
            out[0].reshape(1, 8, PATHS, 64),
            out[1].reshape(1, 8, PATHS, 64),
            out[2].reshape(TERMS, 8, PATHS, 64),
        )

    return jax.shard_map(
        body,
        mesh=mesh,
        in_specs=(
            P("chan", None, "stn"),
            P("chan", None, None, "stn"),
            P(),
            P(None, "stn"),
            P("chan", None, None, None),
            P(),
            P("chan", None, None, None),
            P(),
        ),
        out_specs=(
            P("chan", None, None, "stn"),
            P("chan", None, None, "stn"),
            P(None, None, None, "stn"),
        ),
        check_vma=False,
    )
```

```python
import numpy as np
import jax
import jax.numpy as jnp
from jax import lax
from jax.experimental import pallas as pl
from jax.experimental.pallas import tpu as pltpu
from jax.sharding import PartitionSpec as P

PATHS = 8
SOURCES = 16
TERMS = 3
STEPS = 2
INNER = 2
PASSES = STEPS * INNER
NU = 2.0
TINY = 1e-06
LOGICAL = pl.DeviceIdType.LOGICAL
WIDE = 128
bf16 = jnp.bfloat16
f32 = jnp.float32


def basis_table(count):
    frequency = (2.0 * np.arange(count, dtype=np.float32) + 1.0) / np.float32(count) - 1.0
    columns = []
    for degree in range(TERMS):
        column = (frequency**degree).astype(np.float32)
        for earlier in columns:
            column = column - np.sum(earlier * column) / np.float32(count) * earlier
        column = column / np.sqrt(np.sum(column * column) / np.float32(count))
        columns.append(column.astype(np.float32))
    return np.stack(columns, axis=1)


def mul(a, b):
    return (a[0] * b[0] - a[1] * b[1], a[0] * b[1] + a[1] * b[0])


def mul_conj(a, b):
    return (a[0] * b[0] + a[1] * b[1], a[1] * b[0] - a[0] * b[1])


def conj_mul(a, b):
    return (a[0] * b[0] + a[1] * b[1], a[0] * b[1] - a[1] * b[0])


def add(a, b):
    return (a[0] + b[0], a[1] + b[1])


def product(a, b):
    return [
        add(mul(a[0], b[0]), mul(a[1], b[2])),
        add(mul(a[0], b[1]), mul(a[1], b[3])),
        add(mul(a[2], b[0]), mul(a[3], b[2])),
        add(mul(a[2], b[1]), mul(a[3], b[3])),
    ]


def product_with_adjoint(a, b):
    return [
        add(mul_conj(a[0], b[0]), mul_conj(a[1], b[1])),
        add(mul_conj(a[0], b[2]), mul_conj(a[1], b[3])),
        add(mul_conj(a[2], b[0]), mul_conj(a[3], b[1])),
        add(mul_conj(a[2], b[2]), mul_conj(a[3], b[3])),
    ]


def adjoint_product(a, b):
    return [
        add(conj_mul(a[0], b[0]), conj_mul(a[2], b[2])),
        add(conj_mul(a[0], b[1]), conj_mul(a[2], b[3])),
        add(conj_mul(a[1], b[0]), conj_mul(a[3], b[2])),
        add(conj_mul(a[1], b[1]), conj_mul(a[3], b[3])),
    ]


def power(a):
    return a[0] * a[0] + a[1] * a[1]


def gram(y):
    cross = add(mul_conj(y[0], y[2]), mul_conj(y[1], y[3]))
    return [power(y[0]) + power(y[1]), power(y[2]) + power(y[3]), cross[0], cross[1]]


def gram_of_adjoint(h):
    cross = add(conj_mul(h[0], h[1]), conj_mul(h[2], h[3]))
    return [power(h[0]) + power(h[2]), power(h[1]) + power(h[3]), cross[0], cross[1]]


def halves(x):
    top = x.astype(bf16)
    return top, (x - top.astype(f32)).astype(bf16)


def swap(x):
    return pltpu.roll(x, 64, 1)


def take(table, index):
    return jnp.take_along_axis(table, index, axis=1, mode="promise_in_bounds")


def masks_by_hops(everyone):
    hop = (0, 1, 2, 1)
    hops = lambda m: hop[m >> 1 & 3] + hop[m >> 3 & 3] + hop[m >> 5 & 3]
    return sorted(range(1, everyone), key=lambda m: (-hops(m), m))


SCRATCH = []


def scratch(name, *shape, dtype=f32):
    SCRATCH.append((name, pltpu.VMEM(shape, dtype)))


def lay_out(chans, blocks, baselines, stations):
    SCRATCH.clear()
    everyone = chans * blocks
    scratch("vis", 8, baselines)
    scratch("model", 8 * SOURCES, baselines)
    scratch("pairs", 2, baselines, dtype=jnp.int32)
    scratch("whole", 64 * stations // 128, 128)
    scratch("poly", 64 * TERMS * stations // 128, 128)
    scratch("dual_in", 64 * stations // 128, 128)
    scratch("coherent", 64, baselines)
    scratch("d_src", baselines // 128 * 64, 128)
    scratch("d_all", baselines // 128 * 64, 128)
    scratch("d_own", 64, baselines)
    scratch("pairs_all", blocks, 2, baselines, dtype=jnp.int32)
    scratch("index_p", blocks, baselines, dtype=jnp.int32)
    scratch("index_q", blocks, baselines, dtype=jnp.int32)
    scratch("table_q", 8 * stations // 128 * 8, 128)
    scratch("table_p", 64, 128)
    scratch("collect", blocks * baselines, 256, dtype=bf16)
    scratch("in_tile", blocks * 4 * 16, baselines, dtype=bf16)
    scratch("toward", 64, baselines)
    scratch("terms", 64, baselines)
    scratch("back", 64, baselines)
    scratch("parts_p", baselines // 128 * 16 * blocks, 128)
    scratch("parts_q", baselines // 128 * 16 * blocks, 128)
    scratch("weights", blocks, baselines)
    scratch("sums", 128, 128)
    scratch("gain", 64, 128)
    scratch("anchor", 64, 128)
    scratch("dual", stations // 16, 128)
    scratch("e_src", PASSES, 8, 128)
    scratch("e_all", PASSES, everyone, 128)
    scratch("r_src", PASSES, baselines // 16, 128)
    scratch("r_all", PASSES, blocks * baselines // 16, 128)
    scratch("g_src", PASSES, stations // 16, 128)
    scratch("g_all", PASSES, blocks * stations // 16, 128)
    scratch("f_src", stations // 16, 128)
    scratch("f_all", chans, stations // 16, 128)
    scratch("s_src", blocks, 4, 128)
    scratch("s_all", everyone, 4, 128)
    scratch("j_src", blocks, 4, 128)
    scratch("j_all", blocks, 4, 128)
    dma = pltpu.SemaphoreType.DMA
    SCRATCH.append(("load_sem", dma((3 + 3 * stations // 128,))))
    for name, *shape in (
        ("p_sem", 2),
        ("d_sem", 2),
        ("e_sem", PASSES, 2),
        ("r_sem", PASSES, 3),
        ("g_sem", PASSES, 2),
        ("f_sem", 2),
        ("s_sem", 2),
        ("j_sem", 2),
    ):
        SCRATCH.append((name, dma(tuple(shape))))


class Held:
    def __init__(self, refs):
        for (name, _), ref in zip(SCRATCH, refs, strict=True):
            setattr(self, name, ref)


def kernel(
    chans,
    blocks,
    table,
    pointing,
    rhos,
    vis_hbm,
    model_hbm,
    pairs_hbm,
    gain_hbm,
    poly_hbm,
    dual_hbm,
    packed,
    *refs,
):
    v = Held(refs)
    stations = gain_hbm.shape[1]
    chan = lax.axis_index("chan")
    stn = lax.axis_index("stn")
    everyone = chans * blocks
    me = chan * blocks + stn
    baselines = v.vis.shape[1]
    tiles = stations // 128
    chunks = baselines // WIDE
    samples = float(everyone * baselines)

    flips = [(1 - 2 * lax.rem(lax.div(me, 1 << n), 2)) * (1 << n) for n in range(7)]

    def flipped(mask, start, count, base):
        for n in range(count):
            if mask >> n & 1:
                base = base + flips[start + n]
        return base

    uppers = [flipped(m, 4, 3, me) for m in range(8)]
    lowers = [flipped(m, 0, 4, 0) for m in range(16)]
    masks = masks_by_hops(everyone)

    def peer_of(mask):
        return uppers[mask >> 4] + lowers[mask & 15]

    stn_masks = [m for m in masks if m < blocks]
    chan_masks = [m for m in masks if m % blocks == 0]

    barrier = pltpu.get_barrier_semaphore()
    for mask in masks:
        pl.semaphore_signal(barrier, inc=1, device_id=peer_of(mask), device_id_type=LOGICAL)

    moves = [(model_hbm, v.model), (pairs_hbm, v.pairs), (vis_hbm, v.vis)]
    for src, dst in ((gain_hbm, v.whole), (dual_hbm, v.dual_in), (poly_hbm, v.poly)):
        rows = src.shape[0]
        moves += [
            (src.at[:, pl.ds(128 * j, 128)], dst.at[pl.ds(rows * j, rows)]) for j in range(tiles)
        ]
    loads = [pltpu.make_async_copy(a, b, v.load_sem.at[n]) for n, (a, b) in enumerate(moves)]
    for copy in loads:
        copy.start()

    def remote(src, dst, sem, peer):
        pltpu.make_async_remote_copy(
            src_ref=src,
            dst_ref=dst,
            send_sem=sem.at[0],
            recv_sem=sem.at[1],
            device_id=peer,
            device_id_type=LOGICAL,
        ).start()

    def to_stn(src, dst, sem):
        for mask in stn_masks:
            remote(src(stn + lowers[mask]), dst, sem, peer_of(mask))

    def to_partner(src, dst, sem):
        pltpu.make_async_remote_copy(
            src_ref=src,
            dst_ref=dst,
            send_sem=sem.at[0],
            recv_sem=sem.at[2],
            device_id=peer_of(1),
            device_id_type=LOGICAL,
        ).start()

    def wait_all(ref, sem):
        pltpu.make_async_copy(ref, ref, sem).wait()

    def chunk(i):
        return pl.ds(pl.multiple_of(i * WIDE, WIDE), WIDE)

    def entries(ref, at):
        return [(ref[8 * i : 8 * i + 8, at], ref[32 + 8 * i : 40 + 8 * i, at]) for i in range(4)]

    def keep(ref, at, values):
        for i in range(4):
            ref[8 * i : 8 * i + 8, at] = values[i][0]
            ref[32 + 8 * i : 40 + 8 * i, at] = values[i][1]

    def as_entries(values):
        return [(values[i], values[4 + i]) for i in range(4)]

    def picked(tile_of, index):
        within, tile = index & 127, index >> 7
        out = []
        for c in range(8):
            value = take(tile_of(c, 0), within)
            for j in range(1, tiles):
                value = jnp.where(tile == j, take(tile_of(c, j), within), value)
            out.append(value)
        return as_entries(out)

    lane = lax.broadcasted_iota(jnp.int32, (128, 128), 1)
    high = lax.broadcasted_iota(jnp.int32, (128, 128), 0)
    point = jnp.zeros((128, 128), jnp.int32)
    for s in range(SOURCES):
        point = jnp.where(lane % SOURCES == s, pointing[s], point)
    left, right = high % 64 // PATHS, high % PATHS
    component = jnp.where(high < 64, left, right)
    direction = jnp.where(high < 64, right, left)
    member = jnp.where((component == lane // SOURCES) & (direction == point), 1.0, 0.0).astype(bf16)
    loads[0].wait()

    def combine(*accs):
        twice = jnp.concatenate([member, member], axis=1)
        for i in range(baselines // 256):
            m = v.model[:, 256 * i : 256 * i + 256]
            m0 = m.astype(bf16)
            rest = m - m0.astype(f32)
            m1 = rest.astype(bf16)
            m2 = (rest - m1.astype(f32)).astype(bf16)
            two = jnp.concatenate([m0, m1], axis=0)
            one = jnp.concatenate([m2, jnp.zeros((128, 256), bf16)], axis=0)
            for n, part in enumerate((two, one)):
                pltpu.matmul_push_rhs(part, staging_register=n, mxu_index=i % 2)
                pltpu.matmul_acc_lhs(accs[i % 2], twice, load_staged_rhs=n)
            both = pltpu.matmul_pop(accs[i % 2])
            v.coherent[:, 256 * i : 256 * i + 256] = both[0:64]
            for k in range(PATHS):
                for j in range(2):
                    row = 64 * k + 8 * (2 * i + j)
                    v.d_src[row : row + 8] = both[64 + 8 * k : 72 + 8 * k, 128 * j : 128 * j + 128]

    pl.run_scoped(combine, *[pltpu.ACC(m)((128, 256), f32) for m in range(2)])

    def mine(t):
        value = f32(0.0)
        for f in range(chans):
            value = jnp.where(chan == f, f32(table[f, t]), value)
        return value

    my_basis = [mine(t) for t in range(TERMS)]
    for copy in loads[1:]:
        copy.wait()

    def consensus_of(fit):
        value = my_basis[0] * fit[0]
        for t in range(1, TERMS):
            value = value + my_basis[t] * fit[t]
        return value

    def to_tiles(ref, rows):
        for j in range(tiles):
            ref[pl.ds(j, 8, stride=8), :] = rows[8 * j : 8 * j + 8]

    def own_of(ref, rows, start):
        return jnp.concatenate(
            [ref[pl.ds(rows * j + start + stn, 8, stride=8), :] for j in range(tiles)], axis=0
        )

    v.gain[...] = jnp.zeros((64, 128), f32)
    v.anchor[...] = jnp.zeros((64, 128), f32)
    v.sums[...] = jnp.zeros((128, 128), f32)
    to_tiles(v.gain, own_of(v.whole, 64, 0))
    dual_rows = own_of(v.dual_in, 64, 0)
    v.dual[...] = dual_rows
    to_tiles(v.anchor, consensus_of([own_of(v.poly, 64 * TERMS, 64 * t) for t in range(TERMS)]) - dual_rows)
    rho = rhos[stn]

    def keep_part(ref, i, n, value):
        ref[pl.ds(16 * blocks * i + n, blocks, stride=16), :] = value

    zeros = jnp.zeros((8, WIDE), f32)
    for n in range(12, 16):
        for i in range(chunks):
            keep_part(v.parts_p, i, n, zeros)
            keep_part(v.parts_q, i, n, zeros)
    sub = lax.broadcasted_iota(jnp.int32, (8, 128), 0)
    own_tile = pl.multiple_of(lax.div(stn, 2) * 64, 64)

    def spread_tables():
        rows = [v.gain[pl.ds(j, 8, stride=8), :] for j in range(tiles)]
        for c in range(8):
            per_block = None
            for j in range(tiles):
                value = jnp.broadcast_to(rows[j][c : c + 1], (8, 128))
                at = 8 * (c * tiles + j)
                v.table_q[at : at + 8, :] = value
                per_block = value if j == 0 else jnp.where(sub // 2 == j, value, per_block)
            v.table_p[8 * c : 8 * c + 8, :] = per_block

    def own_terms(i, _):
        at = chunk(i)
        d = entries(v.d_own, at)
        p = v.index_p[:, at]
        gain_p = as_entries([take(v.table_p[8 * c : 8 * c + 8, :], p) for c in range(8)])
        h = product(gain_p, d)
        keep(v.back, at, h)
        for n, part in enumerate(gram_of_adjoint(h)):
            keep_part(v.parts_q, i, n, part)

        def tile_of(c, j):
            return v.table_q[8 * (c * tiles + j) : 8 * (c * tiles + j) + 8, :]

        y = product_with_adjoint(d, picked(tile_of, v.index_q[:, at]))
        keep(v.toward, at, y)
        for n, part in enumerate(gram(y)):
            keep_part(v.parts_p, i, n, part)
        keep(v.terms, at, product(gain_p, y))
        return 0

    own_g, own_r = stations // 16, baselines // 16
    g_rows = pl.ds(pl.multiple_of(own_g * stn, own_g), own_g)
    r_rows = pl.ds(pl.multiple_of(own_r * stn, own_r), own_r)

    def pass_on(it):
        wait_all(v.r_all.at[it, pl.ds(0, (blocks // 2 - 1) * own_r)], v.r_sem.at[it, 1])
        for mask in stn_masks:
            if mask % 2 == 0:
                start = pl.multiple_of(own_r * (stn + lowers[mask]), own_r)
                rows = v.r_all.at[it, pl.ds(start, own_r)]
                to_partner(rows, rows, v.r_sem.at[it])

    def one_pass(it, _):
        spread_tables()

        @pl.when(it > 0)
        def _():
            lax.fori_loop(0, chunks, own_terms, 0, unroll=True)
            wait_all(v.g_all.at[it - 1, pl.ds(0, (blocks - 1) * own_g)], v.g_sem.at[it - 1, 1])
            for j in range(tiles):
                for c in range(8):
                    v.whole[64 * j + 8 * c : 64 * j + 8 * c + 8] = v.g_all[
                        it - 1, pl.ds(8 * j + c, blocks, stride=own_g), :
                    ]

        def residuals(i, total):
            at = chunk(i)
            first = jnp.broadcast_to(v.pairs[0:1, at], (8, WIDE)) & 127
            second = jnp.broadcast_to(v.pairs[1:2, at], (8, WIDE))

            def tile_of(c, j):
                return v.whole[64 * j + 8 * c : 64 * j + 8 * c + 8]

            y = product_with_adjoint(entries(v.coherent, at), picked(tile_of, second))
            gain_p = as_entries(
                [take(v.whole[pl.ds(own_tile + 8 * c, 8)], first) for c in range(8)]
            )
            g = product(gain_p, y)
            e = None
            for n in range(4):
                for part in range(2):
                    c = n + 4 * part
                    left = v.vis[c : c + 1, at] - jnp.sum(g[n][part], axis=0, keepdims=True)
                    e = left * left if e is None else e + left * left
                    v.r_src[it, pl.ds(8 * i + c, 1)] = left
            return total + e

        total = lax.fori_loop(0, chunks, residuals, jnp.zeros((1, WIDE), f32), unroll=True)
        v.e_src[it, 0:1] = total
        v.e_all[it, pl.ds(me, 1)] = total
        v.r_all[it, r_rows] = v.r_src[it]

        @pl.when(it == 0)
        def _():
            pl.semaphore_wait(barrier, everyone - 1)
            to_stn(lambda _: v.pairs, v.pairs_all.at[stn], v.p_sem)
            to_stn(
                lambda peer: v.d_src.at[pl.ds(pl.multiple_of(own_r * peer, own_r), own_r)],
                v.d_all.at[r_rows],
                v.d_sem,
            )

        for mask in stn_masks:
            if mask % 2 == 0:
                remote(v.r_src.at[it], v.r_all.at[it, r_rows], v.r_sem.at[it], peer_of(mask))
        to_partner(v.r_src.at[it], v.r_all.at[it, r_rows], v.r_sem.at[it])
        for mask in masks:
            remote(v.e_src.at[it, pl.ds(0, 1)], v.e_all.at[it, pl.ds(me, 1)], v.e_sem.at[it], peer_of(mask))

        @pl.when(it == 0)
        def _():
            v.pairs_all[stn] = v.pairs[...]
            v.d_all[r_rows] = v.d_src[r_rows]
            wait_all(v.pairs_all.at[pl.ds(0, blocks - 1)], v.p_sem.at[1])
            column = lax.broadcasted_iota(jnp.int32, (baselines, 128), 1).astype(f32)
            for i in range(blocks):
                first = v.pairs_all[i, 0:1, :] & 127
                second = v.pairs_all[i, 1:2, :]
                v.index_p[i : i + 1, :] = first
                v.index_q[i : i + 1, :] = second
                for start, index in ((0, second & 127), (128, first)):
                    across = jnp.broadcast_to(index.astype(f32), (128, baselines)).T
                    v.collect[baselines * i : baselines * i + baselines, start : start + 128] = jnp.where(
                        column == across, 1.0, 0.0
                    ).astype(bf16)
                for j in range(tiles):
                    inside = jnp.where((second >> 7) == j, 1.0, 0.0)
                    at = 16 * (4 * i + j)
                    v.in_tile[at : at + 16, :] = jnp.broadcast_to(inside, (16, baselines)).astype(bf16)
            wait_all(v.d_all.at[pl.ds(0, (blocks - 1) * own_r)], v.d_sem.at[1])
            for i in range(chunks):
                at = slice(WIDE * i, WIDE * i + WIDE)
                for c in range(8):
                    v.d_own[8 * c : 8 * c + 8, at] = v.d_all[pl.ds(8 * i + c, blocks, stride=own_r), :]
            pass_on(it)
            lax.fori_loop(0, chunks, own_terms, 0, unroll=True)

        @pl.when(it > 0)
        def _():
            pass_on(it)

        wait_all(v.r_all.at[it, pl.ds(0, blocks // 2 * own_r)], v.r_sem.at[it, 2])

        def products(i, _):
            at = chunk(i)
            y, h, g = entries(v.toward, at), entries(v.back, at), entries(v.terms, at)
            r = as_entries([v.r_all[it, pl.ds(8 * i + c, blocks, stride=own_r), :] for c in range(8)])
            v.weights[:, at] = power(r[0]) + power(r[1]) + power(r[2]) + power(r[3])
            x = [add(a, b) for a, b in zip(r, g)]
            b = product_with_adjoint(x, y)
            for n, part in enumerate([z[0] for z in b] + [z[1] for z in b]):
                keep_part(v.parts_p, i, 4 + n, part)
            b = adjoint_product(x, h)
            for n, part in enumerate([z[0] for z in b] + [z[1] for z in b]):
                keep_part(v.parts_q, i, 4 + n, part)
            return 0

        lax.fori_loop(0, chunks, products, 0, unroll=True)

        @pl.when(it == INNER)
        def _():
            wait_all(v.f_all.at[pl.ds(0, chans - 1)], v.f_sem.at[1])
            fit = [jnp.zeros((own_g, 128), f32)] * TERMS
            for f in range(chans):
                value = v.f_all[f]
                fit = [fit[t] + f32(table[f, t]) * value for t in range(TERMS)]
            consensus = consensus_of([z * f32(1.0 / chans) for z in fit])
            after = v.f_src[...] - consensus
            v.dual[...] = after
            to_tiles(v.anchor, consensus - after)

        wait_all(v.e_all.at[it, pl.ds(0, everyone - 1)], v.e_sem.at[it, 1])
        total = jnp.sum(v.e_all[it], axis=0, keepdims=True)
        noise = jnp.sum(total, axis=1, keepdims=True) * f32(1.0 / samples) + TINY
        scale = jnp.broadcast_to(1.0 / noise, (1, 128))
        scale = jnp.concatenate([scale] * (baselines // 128), axis=1)
        v.weights[...] = (NU + 2.0) / (NU + v.weights[...] * scale)

        def block_of(ref, i, start):
            rows = [16 * (blocks * n + i) for n in range(start // 128, start // 128 + 2)]
            return jnp.concatenate([ref[row : row + 16, :] for row in rows], axis=1)

        def accumulate(*accs):
            acc_q, acc_p = accs[:2], (accs[2 : 2 + tiles], accs[2 + tiles :])
            for step in range(blocks * baselines // 512):
                for m in range(2):
                    i = 2 * (step * 256 // baselines) + m
                    start = baselines * i + step * 256 % baselines
                    at = slice(start, start + 256)
                    pltpu.matmul_push_rhs(v.collect[at, :], staging_register=step % 2, mxu_index=m)
                    here = slice(start - baselines * i, start - baselines * i + 256)
                    weight = v.weights[i : i + 1, here]
                    top, rest = halves(block_of(v.parts_q, i, here.start) * weight)
                    pieces = []
                    for j in range(tiles):
                        inside = v.in_tile[16 * (4 * i + j) : 16 * (4 * i + j) + 16, here]
                        pieces += [top * inside, rest * inside]
                    pltpu.matmul_acc_lhs(
                        acc_q[m], jnp.concatenate(pieces, axis=0), load_staged_rhs=step % 2
                    )
                    pieces = halves(block_of(v.parts_p, i, here.start) * weight)
                    pltpu.matmul_acc_lhs(acc_p[m][i // 2], jnp.concatenate(pieces, axis=0))
            every = pltpu.matmul_pop(acc_q[0]) + pltpu.matmul_pop(acc_q[1])
            for j in range(tiles):
                here = pltpu.matmul_pop(acc_p[0][j]) + pltpu.matmul_pop(acc_p[1][j])
                got = every[32 * j : 32 * j + 32, 0:128] + here[:, 128:256]
                v.sums[pl.ds(j, 16, stride=8), :] = got[0:16] + got[16:32]

        accs = [pltpu.ACC(m)((128, 256), f32) for m in range(2)]
        accs += [pltpu.ACC(m)((32, 256), f32) for m in range(2) for _ in range(tiles)]
        pl.run_scoped(accumulate, *accs)

        def part(n):
            return v.sums[8 * n : 8 * n + 8, :]

        d1, d2, cr, ci = part(0) + rho, part(1) + rho, part(2), part(3)
        over = 1.0 / (d1 * d2 - cr * cr - ci * ci)
        right = as_entries([part(4 + n) + rho * v.anchor[8 * n : 8 * n + 8, :] for n in range(8)])
        up = (cr * over, ci * over)
        s1, s2 = d2 * over, d1 * over
        solved = []
        for r in range(2):
            x, y = right[2 * r], right[2 * r + 1]
            one = mul_conj(y, up)
            two = mul(x, up)
            solved.append((x[0] * s1 - one[0], x[1] * s1 - one[1]))
            solved.append((y[0] * s2 - two[0], y[1] * s2 - two[1]))
        for n in range(4):
            for k in range(2):
                at = 8 * (n + 4 * k)
                v.gain[at : at + 8, :] = 0.5 * (v.gain[at : at + 8, :] + solved[n][k])
        for j in range(tiles):
            v.g_src[it, 8 * j : 8 * j + 8, :] = v.gain[pl.ds(j, 8, stride=8), :]

        @pl.when(it < PASSES - 1)
        def _():
            to_stn(lambda _: v.g_src.at[it], v.g_all.at[it, g_rows], v.g_sem.at[it])
            v.g_all[it, g_rows] = v.g_src[it]

        @pl.when(it == INNER - 1)
        def _():
            v.f_src[...] = v.g_src[it] + v.dual[...]
            v.f_all[chan] = v.f_src[...]
            for mask in chan_masks:
                remote(v.f_src, v.f_all.at[chan], v.f_sem, peer_of(mask))

        return 0

    lax.fori_loop(0, PASSES, one_pass, 0)

    low = lax.broadcasted_iota(jnp.int32, (8, 128), 1) < 64

    def slices(ref, rows):
        for j in range(tiles):
            a = rows[8 * j : 8 * j + 8]
            under = pltpu.roll(a, 4, 0)
            ref[2 * j] = jnp.where(low, a, swap(under))[0:4]
            ref[2 * j + 1] = jnp.where(low, swap(a), under)[0:4]

    last = v.g_src[PASSES - 1]
    slices(v.s_src, last + v.dual[...])
    slices(v.j_src, last)
    for mask in masks:
        block = stn + lowers[mask & 7]
        remote(v.s_src.at[block], v.s_all.at[me], v.s_sem, peer_of(mask))
    to_stn(lambda peer: v.j_src.at[peer], v.j_all.at[stn], v.j_sem)
    v.s_all[me] = v.s_src[stn]
    v.j_all[stn] = v.j_src[stn]
    wait_all(v.j_all.at[pl.ds(0, blocks - 1)], v.j_sem.at[1])

    packed[0:32, :] = v.j_all[...].reshape(32, 128)
    wait_all(v.s_all.at[pl.ds(0, everyone - 1)], v.s_sem.at[1])
    fit = [jnp.zeros((32, 128), f32)] * TERMS
    for f in range(chans):
        value = v.s_all[blocks * f : blocks * f + blocks].reshape(32, 128)
        fit = [fit[t] + f32(table[f, t]) * value for t in range(TERMS)]
    fit = [z * f32(1.0 / chans) for z in fit]
    packed[32:64, :] = v.s_all[pl.ds(blocks * chan, blocks)].reshape(32, 128) - consensus_of(fit)
    for t in range(TERMS):
        packed[64 + 32 * t : 96 + 32 * t, :] = fit[t]

    wait_all(v.pairs_all.at[pl.ds(0, blocks - 1)], v.p_sem.at[0])
    wait_all(v.d_all.at[pl.ds(0, (blocks - 1) * own_r)], v.d_sem.at[0])
    wait_all(v.f_all.at[pl.ds(0, chans - 1)], v.f_sem.at[0])
    wait_all(v.s_all.at[pl.ds(0, everyone - 1)], v.s_sem.at[0])
    wait_all(v.j_all.at[pl.ds(0, blocks - 1)], v.j_sem.at[0])
    for it in range(PASSES):
        wait_all(v.e_all.at[it, pl.ds(0, everyone - 1)], v.e_sem.at[it, 0])
        wait_all(v.r_all.at[it, pl.ds(0, (blocks - 1) * own_r)], v.r_sem.at[it, 0])
        if it < PASSES - 1:
            wait_all(v.g_all.at[it, pl.ds(0, (blocks - 1) * own_g)], v.g_sem.at[it, 0])


def unpack(packed, gain_out, dual_out, fit_out):
    spots = [(gain_out, 0), (dual_out, 0)] + [(fit_out, 64 * t) for t in range(TERMS)]
    for m, (ref, start) in enumerate(spots):
        for n in range(4):
            rows = packed[pl.ds(32 * m + n, PATHS, stride=4), :]
            ref[start + 8 * n : start + 8 * n + 8, :] = rows[:, 0:64]
            ref[start + 32 + 8 * n : start + 40 + 8 * n, :] = swap(rows)[:, 0:64]


def solution(mesh):
    chans, blocks = mesh.shape["chan"], mesh.shape["stn"]
    table = basis_table(chans)
    abstract = mesh.abstract_mesh

    def body(vis, model, pointing, pairs, gains, poly, dual, rhos):
        baselines = vis.shape[2]
        stations = gains.shape[3]

        def run(*refs):
            kernel(chans, blocks, table, *refs)

        lay_out(chans, blocks, baselines, stations)
        any_spec = pl.BlockSpec(memory_space=pltpu.HBM)
        smem = pl.BlockSpec(memory_space=pltpu.SMEM)
        vmem = pl.BlockSpec(memory_space=pltpu.VMEM)
        packed = pl.pallas_call(
            run,
            out_shape=jax.ShapeDtypeStruct((32 * (2 + TERMS), 128), f32),
            in_specs=[smem, smem] + [any_spec] * 6,
            out_specs=vmem,
            scratch_shapes=[shape for _, shape in SCRATCH],
            compiler_params=pltpu.CompilerParams(
                collective_id=0, has_side_effects=True, vmem_limit_bytes=62 << 20
            ),
            name="calibrate",
        )(
            pointing.reshape(SOURCES),
            rhos,
            vis.reshape(8, baselines),
            model.reshape(8 * SOURCES, baselines),
            pairs,
            gains.reshape(64, stations),
            poly.reshape(64 * TERMS, stations),
            dual.reshape(64, stations),
        )
        out = pl.pallas_call(
            unpack,
            out_shape=(
                jax.ShapeDtypeStruct((64, 64), f32),
                jax.ShapeDtypeStruct((64, 64), f32),
                jax.ShapeDtypeStruct((64 * TERMS, 64), f32),
            ),
            in_specs=[vmem],
            out_specs=(vmem, vmem, vmem),
            compiler_params=pltpu.CompilerParams(vmem_limit_bytes=62 << 20),
            name="unpack",
        )(packed)
        return (
            out[0].reshape(1, 8, PATHS, 64),
            out[1].reshape(1, 8, PATHS, 64),
            out[2].reshape(TERMS, 8, PATHS, 64),
        )

    return jax.shard_map(
        body,
        mesh=mesh,
        in_specs=(
            P("chan", None, "stn"),
            P("chan", None, None, "stn"),
            P(),
            P(None, "stn"),
            P("chan", None, None, None),
            P(),
            P("chan", None, None, None),
            P(),
        ),
        out_specs=(
            P("chan", None, None, "stn"),
            P("chan", None, None, "stn"),
            P(None, None, None, "stn"),
        ),
        check_vma=False,
    )
```

```python
import numpy as np
import jax
import jax.numpy as jnp
from jax import lax
from jax.experimental import pallas as pl
from jax.experimental.pallas import tpu as pltpu
from jax.sharding import PartitionSpec as P

PATHS = 8
SOURCES = 16
TERMS = 3
STEPS = 2
INNER = 2
PASSES = STEPS * INNER
NU = 2.0
TINY = 1e-06
LOGICAL = pl.DeviceIdType.LOGICAL
WIDE = 128
bf16 = jnp.bfloat16
f32 = jnp.float32


def basis_table(count):
    frequency = (2.0 * np.arange(count, dtype=np.float32) + 1.0) / np.float32(count) - 1.0
    columns = []
    for degree in range(TERMS):
        column = (frequency**degree).astype(np.float32)
        for earlier in columns:
            column = column - np.sum(earlier * column) / np.float32(count) * earlier
        column = column / np.sqrt(np.sum(column * column) / np.float32(count))
        columns.append(column.astype(np.float32))
    return np.stack(columns, axis=1)


def mul(a, b):
    return (a[0] * b[0] - a[1] * b[1], a[0] * b[1] + a[1] * b[0])


def mul_conj(a, b):
    return (a[0] * b[0] + a[1] * b[1], a[1] * b[0] - a[0] * b[1])


def conj_mul(a, b):
    return (a[0] * b[0] + a[1] * b[1], a[0] * b[1] - a[1] * b[0])


def add(a, b):
    return (a[0] + b[0], a[1] + b[1])


def product(a, b):
    return [
        add(mul(a[0], b[0]), mul(a[1], b[2])),
        add(mul(a[0], b[1]), mul(a[1], b[3])),
        add(mul(a[2], b[0]), mul(a[3], b[2])),
        add(mul(a[2], b[1]), mul(a[3], b[3])),
    ]


def product_with_adjoint(a, b):
    return [
        add(mul_conj(a[0], b[0]), mul_conj(a[1], b[1])),
        add(mul_conj(a[0], b[2]), mul_conj(a[1], b[3])),
        add(mul_conj(a[2], b[0]), mul_conj(a[3], b[1])),
        add(mul_conj(a[2], b[2]), mul_conj(a[3], b[3])),
    ]


def adjoint_product(a, b):
    return [
        add(conj_mul(a[0], b[0]), conj_mul(a[2], b[2])),
        add(conj_mul(a[0], b[1]), conj_mul(a[2], b[3])),
        add(conj_mul(a[1], b[0]), conj_mul(a[3], b[2])),
        add(conj_mul(a[1], b[1]), conj_mul(a[3], b[3])),
    ]


def power(a):
    return a[0] * a[0] + a[1] * a[1]


def gram(y):
    cross = add(mul_conj(y[0], y[2]), mul_conj(y[1], y[3]))
    return [power(y[0]) + power(y[1]), power(y[2]) + power(y[3]), cross[0], cross[1]]


def gram_of_adjoint(h):
    cross = add(conj_mul(h[0], h[1]), conj_mul(h[2], h[3]))
    return [power(h[0]) + power(h[2]), power(h[1]) + power(h[3]), cross[0], cross[1]]


def halves(x):
    top = x.astype(bf16)
    return top, (x - top.astype(f32)).astype(bf16)


def swap(x):
    return pltpu.roll(x, 64, 1)


def take(table, index):
    return jnp.take_along_axis(table, index, axis=1, mode="promise_in_bounds")


def masks_by_hops(everyone):
    hop = (0, 1, 2, 1)
    hops = lambda m: hop[m >> 1 & 3] + hop[m >> 3 & 3] + hop[m >> 5 & 3]
    return sorted(range(1, everyone), key=lambda m: (-hops(m), m))


SCRATCH = []


def scratch(name, *shape, dtype=f32):
    SCRATCH.append((name, pltpu.VMEM(shape, dtype)))


def lay_out(chans, blocks, baselines, stations):
    SCRATCH.clear()
    everyone = chans * blocks
    scratch("vis", 8, baselines)
    scratch("model", 8 * SOURCES, baselines)
    scratch("pairs", 2, baselines, dtype=jnp.int32)
    scratch("whole", 64 * stations // 128, 128)
    scratch("poly", 64 * TERMS * stations // 128, 128)
    scratch("dual_in", 64 * stations // 128, 128)
    scratch("coherent", 64, baselines)
    scratch("d_src", baselines // 128 * 64, 128)
    scratch("d_all", baselines // 128 * 64, 128)
    scratch("d_own", 64, baselines)
    scratch("pairs_all", blocks, 2, baselines, dtype=jnp.int32)
    scratch("index_p", blocks, baselines, dtype=jnp.int32)
    scratch("index_q", blocks, baselines, dtype=jnp.int32)
    scratch("table_q", 8 * stations // 128 * 8, 128)
    scratch("table_p", 64, 128)
    scratch("collect", blocks * baselines, 256, dtype=bf16)
    scratch("in_tile", blocks * 4 * 16, baselines, dtype=bf16)
    scratch("toward", 64, baselines)
    scratch("terms", 64, baselines)
    scratch("back", 64, baselines)
    scratch("parts_p", baselines // 128 * 16 * blocks, 128)
    scratch("parts_q", baselines // 128 * 16 * blocks, 128)
    scratch("weights", blocks, baselines)
    scratch("sums", 128, 128)
    scratch("gain", 64, 128)
    scratch("anchor", 64, 128)
    scratch("dual", stations // 16, 128)
    scratch("e_src", PASSES, 8, 128)
    scratch("e_all", PASSES, everyone, 128)
    scratch("r_src", PASSES, baselines // 16, 128)
    scratch("r_all", PASSES, blocks * baselines // 16, 128)
    scratch("g_src", PASSES, stations // 16, 128)
    scratch("g_all", PASSES, blocks * stations // 16, 128)
    scratch("f_src", stations // 16, 128)
    scratch("f_all", chans, stations // 16, 128)
    scratch("s_src", blocks, 4, 128)
    scratch("s_all", everyone, 4, 128)
    scratch("j_src", blocks, 4, 128)
    scratch("j_all", blocks, 4, 128)
    SCRATCH.append(("pointing", pltpu.SMEM((SOURCES,), jnp.int32)))
    SCRATCH.append(("rhos", pltpu.SMEM((PATHS,), f32)))
    dma = pltpu.SemaphoreType.DMA
    SCRATCH.append(("load_sem", dma((5 + 3 * stations // 128,))))
    for name, *shape in (
        ("p_sem", 2),
        ("d_sem", 2),
        ("e_sem", PASSES, 2),
        ("r_sem", PASSES, 3),
        ("g_sem", PASSES, 2),
        ("f_sem", 2),
        ("s_sem", 2),
        ("j_sem", 2),
    ):
        SCRATCH.append((name, dma(tuple(shape))))


class Held:
    def __init__(self, refs):
        for (name, _), ref in zip(SCRATCH, refs, strict=True):
            setattr(self, name, ref)


def kernel(
    chans,
    blocks,
    table,
    pointing_hbm,
    rhos_hbm,
    vis_hbm,
    model_hbm,
    pairs_hbm,
    gain_hbm,
    poly_hbm,
    dual_hbm,
    packed,
    *refs,
):
    v = Held(refs)
    stations = gain_hbm.shape[1]
    chan = lax.axis_index("chan")
    stn = lax.axis_index("stn")
    everyone = chans * blocks
    me = chan * blocks + stn
    baselines = v.vis.shape[1]
    tiles = stations // 128
    chunks = baselines // WIDE
    samples = float(everyone * baselines)

    flips = [(1 - 2 * lax.rem(lax.div(me, 1 << n), 2)) * (1 << n) for n in range(7)]

    def flipped(mask, start, count, base):
        for n in range(count):
            if mask >> n & 1:
                base = base + flips[start + n]
        return base

    uppers = [flipped(m, 4, 3, me) for m in range(8)]
    lowers = [flipped(m, 0, 4, 0) for m in range(16)]
    masks = masks_by_hops(everyone)

    def peer_of(mask):
        return uppers[mask >> 4] + lowers[mask & 15]

    stn_masks = [m for m in masks if m < blocks]
    chan_masks = [m for m in masks if m % blocks == 0]

    barrier = pltpu.get_barrier_semaphore()
    for mask in masks:
        pl.semaphore_signal(barrier, inc=1, device_id=peer_of(mask), device_id_type=LOGICAL)

    pointing, rhos = v.pointing, v.rhos
    moves = [(pointing_hbm, pointing), (rhos_hbm, rhos), (model_hbm, v.model)]
    moves += [(pairs_hbm, v.pairs), (vis_hbm, v.vis)]
    for src, dst in ((gain_hbm, v.whole), (dual_hbm, v.dual_in), (poly_hbm, v.poly)):
        rows = src.shape[0]
        moves += [
            (src.at[:, pl.ds(128 * j, 128)], dst.at[pl.ds(rows * j, rows)]) for j in range(tiles)
        ]
    loads = [pltpu.make_async_copy(a, b, v.load_sem.at[n]) for n, (a, b) in enumerate(moves)]
    for copy in loads:
        copy.start()

    def remote(src, dst, sem, peer):
        pltpu.make_async_remote_copy(
            src_ref=src,
            dst_ref=dst,
            send_sem=sem.at[0],
            recv_sem=sem.at[1],
            device_id=peer,
            device_id_type=LOGICAL,
        ).start()

    def to_stn(src, dst, sem):
        for mask in stn_masks:
            remote(src(stn + lowers[mask]), dst, sem, peer_of(mask))

    def to_partner(src, dst, sem):
        pltpu.make_async_remote_copy(
            src_ref=src,
            dst_ref=dst,
            send_sem=sem.at[0],
            recv_sem=sem.at[2],
            device_id=peer_of(1),
            device_id_type=LOGICAL,
        ).start()

    def wait_all(ref, sem):
        pltpu.make_async_copy(ref, ref, sem).wait()

    def chunk(i):
        return pl.ds(pl.multiple_of(i * WIDE, WIDE), WIDE)

    def entries(ref, at):
        return [(ref[8 * i : 8 * i + 8, at], ref[32 + 8 * i : 40 + 8 * i, at]) for i in range(4)]

    def keep(ref, at, values):
        for i in range(4):
            ref[8 * i : 8 * i + 8, at] = values[i][0]
            ref[32 + 8 * i : 40 + 8 * i, at] = values[i][1]

    def as_entries(values):
        return [(values[i], values[4 + i]) for i in range(4)]

    def picked(tile_of, index):
        within, tile = index & 127, index >> 7
        out = []
        for c in range(8):
            value = take(tile_of(c, 0), within)
            for j in range(1, tiles):
                value = jnp.where(tile == j, take(tile_of(c, j), within), value)
            out.append(value)
        return as_entries(out)

    loads[0].wait()
    loads[1].wait()

    lane = lax.broadcasted_iota(jnp.int32, (128, 128), 1)
    high = lax.broadcasted_iota(jnp.int32, (128, 128), 0)
    point = jnp.zeros((128, 128), jnp.int32)
    for s in range(SOURCES):
        point = jnp.where(lane % SOURCES == s, pointing[s], point)
    left, right = high % 64 // PATHS, high % PATHS
    component = jnp.where(high < 64, left, right)
    direction = jnp.where(high < 64, right, left)
    member = jnp.where((component == lane // SOURCES) & (direction == point), 1.0, 0.0).astype(bf16)
    loads[2].wait()

    def combine(*accs):
        twice = jnp.concatenate([member, member], axis=1)
        for i in range(baselines // 256):
            m = v.model[:, 256 * i : 256 * i + 256]
            m0 = m.astype(bf16)
            rest = m - m0.astype(f32)
            m1 = rest.astype(bf16)
            m2 = (rest - m1.astype(f32)).astype(bf16)
            two = jnp.concatenate([m0, m1], axis=0)
            one = jnp.concatenate([m2, jnp.zeros((128, 256), bf16)], axis=0)
            for n, part in enumerate((two, one)):
                pltpu.matmul_push_rhs(part, staging_register=n, mxu_index=i % 2)
                pltpu.matmul_acc_lhs(accs[i % 2], twice, load_staged_rhs=n)
            both = pltpu.matmul_pop(accs[i % 2])
            v.coherent[:, 256 * i : 256 * i + 256] = both[0:64]
            for k in range(PATHS):
                for j in range(2):
                    row = 64 * k + 8 * (2 * i + j)
                    v.d_src[row : row + 8] = both[64 + 8 * k : 72 + 8 * k, 128 * j : 128 * j + 128]

    pl.run_scoped(combine, *[pltpu.ACC(m)((128, 256), f32) for m in range(2)])

    def mine(t):
        value = f32(0.0)
        for f in range(chans):
            value = jnp.where(chan == f, f32(table[f, t]), value)
        return value

    my_basis = [mine(t) for t in range(TERMS)]
    for copy in loads[3:]:
        copy.wait()

    def consensus_of(fit):
        value = my_basis[0] * fit[0]
        for t in range(1, TERMS):
            value = value + my_basis[t] * fit[t]
        return value

    def to_tiles(ref, rows):
        for j in range(tiles):
            ref[pl.ds(j, 8, stride=8), :] = rows[8 * j : 8 * j + 8]

    def own_of(ref, rows, start):
        return jnp.concatenate(
            [ref[pl.ds(rows * j + start + stn, 8, stride=8), :] for j in range(tiles)], axis=0
        )

    v.gain[...] = jnp.zeros((64, 128), f32)
    v.anchor[...] = jnp.zeros((64, 128), f32)
    v.sums[...] = jnp.zeros((128, 128), f32)
    to_tiles(v.gain, own_of(v.whole, 64, 0))
    dual_rows = own_of(v.dual_in, 64, 0)
    v.dual[...] = dual_rows
    to_tiles(v.anchor, consensus_of([own_of(v.poly, 64 * TERMS, 64 * t) for t in range(TERMS)]) - dual_rows)
    rho = rhos[stn]

    def keep_part(ref, i, n, value):
        ref[pl.ds(16 * blocks * i + n, blocks, stride=16), :] = value

    zeros = jnp.zeros((8, WIDE), f32)
    for n in range(12, 16):
        for i in range(chunks):
            keep_part(v.parts_p, i, n, zeros)
            keep_part(v.parts_q, i, n, zeros)
    sub = lax.broadcasted_iota(jnp.int32, (8, 128), 0)
    own_tile = pl.multiple_of(lax.div(stn, 2) * 64, 64)

    def spread_tables():
        rows = [v.gain[pl.ds(j, 8, stride=8), :] for j in range(tiles)]
        for c in range(8):
            per_block = None
            for j in range(tiles):
                value = jnp.broadcast_to(rows[j][c : c + 1], (8, 128))
                at = 8 * (c * tiles + j)
                v.table_q[at : at + 8, :] = value
                per_block = value if j == 0 else jnp.where(sub // 2 == j, value, per_block)
            v.table_p[8 * c : 8 * c + 8, :] = per_block

    def own_terms(i, _):
        at = chunk(i)
        d = entries(v.d_own, at)
        p = v.index_p[:, at]
        gain_p = as_entries([take(v.table_p[8 * c : 8 * c + 8, :], p) for c in range(8)])
        h = product(gain_p, d)
        keep(v.back, at, h)
        for n, part in enumerate(gram_of_adjoint(h)):
            keep_part(v.parts_q, i, n, part)

        def tile_of(c, j):
            return v.table_q[8 * (c * tiles + j) : 8 * (c * tiles + j) + 8, :]

        y = product_with_adjoint(d, picked(tile_of, v.index_q[:, at]))
        keep(v.toward, at, y)
        for n, part in enumerate(gram(y)):
            keep_part(v.parts_p, i, n, part)
        keep(v.terms, at, product(gain_p, y))
        return 0

    own_g, own_r = stations // 16, baselines // 16
    g_rows = pl.ds(pl.multiple_of(own_g * stn, own_g), own_g)
    r_rows = pl.ds(pl.multiple_of(own_r * stn, own_r), own_r)

    def pass_on(it):
        wait_all(v.r_all.at[it, pl.ds(0, (blocks // 2 - 1) * own_r)], v.r_sem.at[it, 1])
        for mask in stn_masks:
            if mask % 2 == 0:
                start = pl.multiple_of(own_r * (stn + lowers[mask]), own_r)
                rows = v.r_all.at[it, pl.ds(start, own_r)]
                to_partner(rows, rows, v.r_sem.at[it])

    def one_pass(it, _):
        spread_tables()

        @pl.when(it > 0)
        def _():
            lax.fori_loop(0, chunks, own_terms, 0, unroll=True)
            wait_all(v.g_all.at[it - 1, pl.ds(0, (blocks - 1) * own_g)], v.g_sem.at[it - 1, 1])
            for j in range(tiles):
                for c in range(8):
                    v.whole[64 * j + 8 * c : 64 * j + 8 * c + 8] = v.g_all[
                        it - 1, pl.ds(8 * j + c, blocks, stride=own_g), :
                    ]

        def residuals(i, total):
            at = chunk(i)
            first = jnp.broadcast_to(v.pairs[0:1, at], (8, WIDE)) & 127
            second = jnp.broadcast_to(v.pairs[1:2, at], (8, WIDE))

            def tile_of(c, j):
                return v.whole[64 * j + 8 * c : 64 * j + 8 * c + 8]

            y = product_with_adjoint(entries(v.coherent, at), picked(tile_of, second))
            gain_p = as_entries(
                [take(v.whole[pl.ds(own_tile + 8 * c, 8)], first) for c in range(8)]
            )
            g = product(gain_p, y)
            e = None
            for n in range(4):
                for part in range(2):
                    c = n + 4 * part
                    left = v.vis[c : c + 1, at] - jnp.sum(g[n][part], axis=0, keepdims=True)
                    e = left * left if e is None else e + left * left
                    v.r_src[it, pl.ds(8 * i + c, 1)] = left
            return total + e

        total = lax.fori_loop(0, chunks, residuals, jnp.zeros((1, WIDE), f32), unroll=True)
        v.e_src[it, 0:1] = total
        v.e_all[it, pl.ds(me, 1)] = total
        v.r_all[it, r_rows] = v.r_src[it]

        @pl.when(it == 0)
        def _():
            pl.semaphore_wait(barrier, everyone - 1)
            to_stn(lambda _: v.pairs, v.pairs_all.at[stn], v.p_sem)

        for mask in stn_masks:
            if mask % 2 == 0:
                remote(v.r_src.at[it], v.r_all.at[it, r_rows], v.r_sem.at[it], peer_of(mask))
        to_partner(v.r_src.at[it], v.r_all.at[it, r_rows], v.r_sem.at[it])
        for mask in masks:
            remote(v.e_src.at[it, pl.ds(0, 1)], v.e_all.at[it, pl.ds(me, 1)], v.e_sem.at[it], peer_of(mask))

        @pl.when(it == 0)
        def _():
            to_stn(
                lambda peer: v.d_src.at[pl.ds(pl.multiple_of(own_r * peer, own_r), own_r)],
                v.d_all.at[r_rows],
                v.d_sem,
            )
            v.pairs_all[stn] = v.pairs[...]
            v.d_all[r_rows] = v.d_src[r_rows]
            wait_all(v.pairs_all.at[pl.ds(0, blocks - 1)], v.p_sem.at[1])
            column = lax.broadcasted_iota(jnp.int32, (baselines, 128), 1).astype(f32)
            for i in range(blocks):
                first = v.pairs_all[i, 0:1, :] & 127
                second = v.pairs_all[i, 1:2, :]
                v.index_p[i : i + 1, :] = first
                v.index_q[i : i + 1, :] = second
                for start, index in ((0, second & 127), (128, first)):
                    across = jnp.broadcast_to(index.astype(f32), (128, baselines)).T
                    v.collect[baselines * i : baselines * i + baselines, start : start + 128] = jnp.where(
                        column == across, 1.0, 0.0
                    ).astype(bf16)
                for j in range(tiles):
                    inside = jnp.where((second >> 7) == j, 1.0, 0.0)
                    at = 16 * (4 * i + j)
                    v.in_tile[at : at + 16, :] = jnp.broadcast_to(inside, (16, baselines)).astype(bf16)
            wait_all(v.d_all.at[pl.ds(0, (blocks - 1) * own_r)], v.d_sem.at[1])
            for i in range(chunks):
                at = slice(WIDE * i, WIDE * i + WIDE)
                for c in range(8):
                    v.d_own[8 * c : 8 * c + 8, at] = v.d_all[pl.ds(8 * i + c, blocks, stride=own_r), :]
            pass_on(it)
            lax.fori_loop(0, chunks, own_terms, 0, unroll=True)

        @pl.when(it > 0)
        def _():
            pass_on(it)

        wait_all(v.r_all.at[it, pl.ds(0, blocks // 2 * own_r)], v.r_sem.at[it, 2])

        def products(i, _):
            at = chunk(i)
            y, h, g = entries(v.toward, at), entries(v.back, at), entries(v.terms, at)
            r = as_entries([v.r_all[it, pl.ds(8 * i + c, blocks, stride=own_r), :] for c in range(8)])
            v.weights[:, at] = power(r[0]) + power(r[1]) + power(r[2]) + power(r[3])
            x = [add(a, b) for a, b in zip(r, g)]
            b = product_with_adjoint(x, y)
            for n, part in enumerate([z[0] for z in b] + [z[1] for z in b]):
                keep_part(v.parts_p, i, 4 + n, part)
            b = adjoint_product(x, h)
            for n, part in enumerate([z[0] for z in b] + [z[1] for z in b]):
                keep_part(v.parts_q, i, 4 + n, part)
            return 0

        lax.fori_loop(0, chunks, products, 0, unroll=True)

        @pl.when(it == INNER)
        def _():
            wait_all(v.f_all.at[pl.ds(0, chans - 1)], v.f_sem.at[1])
            fit = [jnp.zeros((own_g, 128), f32)] * TERMS
            for f in range(chans):
                value = v.f_all[f]
                fit = [fit[t] + f32(table[f, t]) * value for t in range(TERMS)]
            consensus = consensus_of([z * f32(1.0 / chans) for z in fit])
            after = v.f_src[...] - consensus
            v.dual[...] = after
            to_tiles(v.anchor, consensus - after)

        wait_all(v.e_all.at[it, pl.ds(0, everyone - 1)], v.e_sem.at[it, 1])
        total = jnp.sum(v.e_all[it], axis=0, keepdims=True)
        noise = jnp.sum(total, axis=1, keepdims=True) * f32(1.0 / samples) + TINY
        scale = jnp.broadcast_to(1.0 / noise, (1, 128))
        scale = jnp.concatenate([scale] * (baselines // 128), axis=1)
        v.weights[...] = (NU + 2.0) / (NU + v.weights[...] * scale)

        def block_of(ref, i, start):
            rows = [16 * (blocks * n + i) for n in range(start // 128, start // 128 + 2)]
            return jnp.concatenate([ref[row : row + 16, :] for row in rows], axis=1)

        def accumulate(*accs):
            acc_q, acc_p = accs[:2], (accs[2 : 2 + tiles], accs[2 + tiles :])
            for step in range(blocks * baselines // 512):
                for m in range(2):
                    i = 2 * (step * 256 // baselines) + m
                    start = baselines * i + step * 256 % baselines
                    at = slice(start, start + 256)
                    pltpu.matmul_push_rhs(v.collect[at, :], staging_register=step % 2, mxu_index=m)
                    here = slice(start - baselines * i, start - baselines * i + 256)
                    weight = v.weights[i : i + 1, here]
                    top, rest = halves(block_of(v.parts_q, i, here.start) * weight)
                    pieces = []
                    for j in range(tiles):
                        inside = v.in_tile[16 * (4 * i + j) : 16 * (4 * i + j) + 16, here]
                        pieces += [top * inside, rest * inside]
                    pltpu.matmul_acc_lhs(
                        acc_q[m], jnp.concatenate(pieces, axis=0), load_staged_rhs=step % 2
                    )
                    pieces = halves(block_of(v.parts_p, i, here.start) * weight)
                    pltpu.matmul_acc_lhs(acc_p[m][i // 2], jnp.concatenate(pieces, axis=0))
            every = pltpu.matmul_pop(acc_q[0]) + pltpu.matmul_pop(acc_q[1])
            for j in range(tiles):
                here = pltpu.matmul_pop(acc_p[0][j]) + pltpu.matmul_pop(acc_p[1][j])
                got = every[32 * j : 32 * j + 32, 0:128] + here[:, 128:256]
                v.sums[pl.ds(j, 16, stride=8), :] = got[0:16] + got[16:32]

        accs = [pltpu.ACC(m)((128, 256), f32) for m in range(2)]
        accs += [pltpu.ACC(m)((32, 256), f32) for m in range(2) for _ in range(tiles)]
        pl.run_scoped(accumulate, *accs)

        def part(n):
            return v.sums[8 * n : 8 * n + 8, :]

        d1, d2, cr, ci = part(0) + rho, part(1) + rho, part(2), part(3)
        over = 1.0 / (d1 * d2 - cr * cr - ci * ci)
        right = as_entries([part(4 + n) + rho * v.anchor[8 * n : 8 * n + 8, :] for n in range(8)])
        up = (cr * over, ci * over)
        s1, s2 = d2 * over, d1 * over
        solved = []
        for r in range(2):
            x, y = right[2 * r], right[2 * r + 1]
            one = mul_conj(y, up)
            two = mul(x, up)
            solved.append((x[0] * s1 - one[0], x[1] * s1 - one[1]))
            solved.append((y[0] * s2 - two[0], y[1] * s2 - two[1]))
        for n in range(4):
            for k in range(2):
                at = 8 * (n + 4 * k)
                v.gain[at : at + 8, :] = 0.5 * (v.gain[at : at + 8, :] + solved[n][k])
        for j in range(tiles):
            v.g_src[it, 8 * j : 8 * j + 8, :] = v.gain[pl.ds(j, 8, stride=8), :]

        @pl.when(it < PASSES - 1)
        def _():
            to_stn(lambda _: v.g_src.at[it], v.g_all.at[it, g_rows], v.g_sem.at[it])
            v.g_all[it, g_rows] = v.g_src[it]

        @pl.when(it == INNER - 1)
        def _():
            v.f_src[...] = v.g_src[it] + v.dual[...]
            v.f_all[chan] = v.f_src[...]
            for mask in chan_masks:
                remote(v.f_src, v.f_all.at[chan], v.f_sem, peer_of(mask))

        return 0

    lax.fori_loop(0, PASSES, one_pass, 0)

    low = lax.broadcasted_iota(jnp.int32, (8, 128), 1) < 64

    def slices(ref, rows):
        for j in range(tiles):
            a = rows[8 * j : 8 * j + 8]
            under = pltpu.roll(a, 4, 0)
            ref[2 * j] = jnp.where(low, a, swap(under))[0:4]
            ref[2 * j + 1] = jnp.where(low, swap(a), under)[0:4]

    last = v.g_src[PASSES - 1]
    slices(v.s_src, last + v.dual[...])
    slices(v.j_src, last)
    for mask in masks:
        block = stn + lowers[mask & 7]
        remote(v.s_src.at[block], v.s_all.at[me], v.s_sem, peer_of(mask))
    to_stn(lambda peer: v.j_src.at[peer], v.j_all.at[stn], v.j_sem)
    v.s_all[me] = v.s_src[stn]
    v.j_all[stn] = v.j_src[stn]
    wait_all(v.j_all.at[pl.ds(0, blocks - 1)], v.j_sem.at[1])

    packed[0:32, :] = v.j_all[...].reshape(32, 128)
    wait_all(v.s_all.at[pl.ds(0, everyone - 1)], v.s_sem.at[1])
    fit = [jnp.zeros((32, 128), f32)] * TERMS
    for f in range(chans):
        value = v.s_all[blocks * f : blocks * f + blocks].reshape(32, 128)
        fit = [fit[t] + f32(table[f, t]) * value for t in range(TERMS)]
    fit = [z * f32(1.0 / chans) for z in fit]
    packed[32:64, :] = v.s_all[pl.ds(blocks * chan, blocks)].reshape(32, 128) - consensus_of(fit)
    for t in range(TERMS):
        packed[64 + 32 * t : 96 + 32 * t, :] = fit[t]

    wait_all(v.pairs_all.at[pl.ds(0, blocks - 1)], v.p_sem.at[0])
    wait_all(v.d_all.at[pl.ds(0, (blocks - 1) * own_r)], v.d_sem.at[0])
    wait_all(v.f_all.at[pl.ds(0, chans - 1)], v.f_sem.at[0])
    wait_all(v.s_all.at[pl.ds(0, everyone - 1)], v.s_sem.at[0])
    wait_all(v.j_all.at[pl.ds(0, blocks - 1)], v.j_sem.at[0])
    for it in range(PASSES):
        wait_all(v.e_all.at[it, pl.ds(0, everyone - 1)], v.e_sem.at[it, 0])
        wait_all(v.r_all.at[it, pl.ds(0, (blocks - 1) * own_r)], v.r_sem.at[it, 0])
        if it < PASSES - 1:
            wait_all(v.g_all.at[it, pl.ds(0, (blocks - 1) * own_g)], v.g_sem.at[it, 0])


def unpack(packed, gain_out, dual_out, fit_out):
    spots = [(gain_out, 0), (dual_out, 0)] + [(fit_out, 64 * t) for t in range(TERMS)]
    for m, (ref, start) in enumerate(spots):
        for n in range(4):
            rows = packed[pl.ds(32 * m + n, PATHS, stride=4), :]
            ref[start + 8 * n : start + 8 * n + 8, :] = rows[:, 0:64]
            ref[start + 32 + 8 * n : start + 40 + 8 * n, :] = swap(rows)[:, 0:64]


def solution(mesh):
    chans, blocks = mesh.shape["chan"], mesh.shape["stn"]
    table = basis_table(chans)
    abstract = mesh.abstract_mesh

    def body(vis, model, pointing, pairs, gains, poly, dual, rhos):
        baselines = vis.shape[2]
        stations = gains.shape[3]

        def run(*refs):
            kernel(chans, blocks, table, *refs)

        lay_out(chans, blocks, baselines, stations)
        any_spec = pl.BlockSpec(memory_space=pltpu.HBM)
        vmem = pl.BlockSpec(memory_space=pltpu.VMEM)
        packed = pl.pallas_call(
            run,
            out_shape=jax.ShapeDtypeStruct((32 * (2 + TERMS), 128), f32),
            in_specs=[any_spec] * 8,
            out_specs=vmem,
            scratch_shapes=[shape for _, shape in SCRATCH],
            compiler_params=pltpu.CompilerParams(
                collective_id=0, has_side_effects=True, vmem_limit_bytes=40 << 20
            ),
            name="calibrate",
        )(
            pltpu.with_memory_space_constraint(pointing.reshape(SOURCES), pltpu.HBM),
            pltpu.with_memory_space_constraint(rhos, pltpu.HBM),
            pltpu.with_memory_space_constraint(vis.reshape(8, baselines), pltpu.HBM),
            pltpu.with_memory_space_constraint(model.reshape(8 * SOURCES, baselines), pltpu.HBM),
            pltpu.with_memory_space_constraint(pairs, pltpu.HBM),
            pltpu.with_memory_space_constraint(gains.reshape(64, stations), pltpu.HBM),
            pltpu.with_memory_space_constraint(poly.reshape(64 * TERMS, stations), pltpu.HBM),
            pltpu.with_memory_space_constraint(dual.reshape(64, stations), pltpu.HBM),
        )
        out = pl.pallas_call(
            unpack,
            out_shape=(
                jax.ShapeDtypeStruct((64, 64), f32),
                jax.ShapeDtypeStruct((64, 64), f32),
                jax.ShapeDtypeStruct((64 * TERMS, 64), f32),
            ),
            in_specs=[vmem],
            out_specs=(vmem, vmem, vmem),
            compiler_params=pltpu.CompilerParams(vmem_limit_bytes=16 << 20),
            name="unpack",
        )(packed)
        return (
            out[0].reshape(1, 8, PATHS, 64),
            out[1].reshape(1, 8, PATHS, 64),
            out[2].reshape(TERMS, 8, PATHS, 64),
        )

    return jax.shard_map(
        body,
        mesh=mesh,
        in_specs=(
            P("chan", None, "stn"),
            P("chan", None, None, "stn"),
            P(),
            P(None, "stn"),
            P("chan", None, None, None),
            P(),
            P("chan", None, None, None),
            P(),
        ),
        out_specs=(
            P("chan", None, None, "stn"),
            P("chan", None, None, "stn"),
            P(None, None, None, "stn"),
        ),
        check_vma=False,
    )
```

```python
import numpy as np
import jax
import jax.numpy as jnp
from jax import lax
from jax.experimental import pallas as pl
from jax.experimental.pallas import tpu as pltpu
from jax.sharding import PartitionSpec as P

PATHS = 8
SOURCES = 16
TERMS = 3
STEPS = 2
INNER = 2
PASSES = STEPS * INNER
NU = 2.0
TINY = 1e-06
LOGICAL = pl.DeviceIdType.LOGICAL
WIDE = 128
bf16 = jnp.bfloat16
f32 = jnp.float32


def basis_table(count):
    frequency = (2.0 * np.arange(count, dtype=np.float32) + 1.0) / np.float32(count) - 1.0
    columns = []
    for degree in range(TERMS):
        column = (frequency**degree).astype(np.float32)
        for earlier in columns:
            column = column - np.sum(earlier * column) / np.float32(count) * earlier
        column = column / np.sqrt(np.sum(column * column) / np.float32(count))
        columns.append(column.astype(np.float32))
    return np.stack(columns, axis=1)


def mul(a, b):
    return (a[0] * b[0] - a[1] * b[1], a[0] * b[1] + a[1] * b[0])


def mul_conj(a, b):
    return (a[0] * b[0] + a[1] * b[1], a[1] * b[0] - a[0] * b[1])


def conj_mul(a, b):
    return (a[0] * b[0] + a[1] * b[1], a[0] * b[1] - a[1] * b[0])


def add(a, b):
    return (a[0] + b[0], a[1] + b[1])


def product(a, b):
    return [
        add(mul(a[0], b[0]), mul(a[1], b[2])),
        add(mul(a[0], b[1]), mul(a[1], b[3])),
        add(mul(a[2], b[0]), mul(a[3], b[2])),
        add(mul(a[2], b[1]), mul(a[3], b[3])),
    ]


def product_with_adjoint(a, b):
    return [
        add(mul_conj(a[0], b[0]), mul_conj(a[1], b[1])),
        add(mul_conj(a[0], b[2]), mul_conj(a[1], b[3])),
        add(mul_conj(a[2], b[0]), mul_conj(a[3], b[1])),
        add(mul_conj(a[2], b[2]), mul_conj(a[3], b[3])),
    ]


def adjoint_product(a, b):
    return [
        add(conj_mul(a[0], b[0]), conj_mul(a[2], b[2])),
        add(conj_mul(a[0], b[1]), conj_mul(a[2], b[3])),
        add(conj_mul(a[1], b[0]), conj_mul(a[3], b[2])),
        add(conj_mul(a[1], b[1]), conj_mul(a[3], b[3])),
    ]


def power(a):
    return a[0] * a[0] + a[1] * a[1]


def gram(y):
    cross = add(mul_conj(y[0], y[2]), mul_conj(y[1], y[3]))
    return [power(y[0]) + power(y[1]), power(y[2]) + power(y[3]), cross[0], cross[1]]


def gram_of_adjoint(h):
    cross = add(conj_mul(h[0], h[1]), conj_mul(h[2], h[3]))
    return [power(h[0]) + power(h[2]), power(h[1]) + power(h[3]), cross[0], cross[1]]


def halves(x):
    top = x.astype(bf16)
    return top, (x - top.astype(f32)).astype(bf16)


def swap(x):
    return pltpu.roll(x, 64, 1)


def take(table, index):
    return jnp.take_along_axis(table, index, axis=1, mode="promise_in_bounds")


def masks_by_hops(everyone):
    hop = (0, 1, 2, 1)
    hops = lambda m: hop[m >> 1 & 3] + hop[m >> 3 & 3] + hop[m >> 5 & 3]
    return sorted(range(1, everyone), key=lambda m: (-hops(m), m))


SCRATCH = []


def scratch(name, *shape, dtype=f32):
    SCRATCH.append((name, pltpu.VMEM(shape, dtype)))


def lay_out(chans, blocks, baselines, stations):
    SCRATCH.clear()
    everyone = chans * blocks
    scratch("vis", 8, baselines)
    scratch("model", 8 * SOURCES, baselines)
    scratch("pairs", 2, baselines, dtype=jnp.int32)
    scratch("whole", 64 * stations // 128, 128)
    scratch("poly", 64 * TERMS * stations // 128, 128)
    scratch("dual_in", 64 * stations // 128, 128)
    scratch("coherent", 64, baselines)
    scratch("d_src", baselines // 128 * 64, 128)
    scratch("d_all", baselines // 128 * 64, 128)
    scratch("d_own", 64, baselines)
    scratch("pairs_all", blocks, 2, baselines, dtype=jnp.int32)
    scratch("index_p", blocks, baselines, dtype=jnp.int32)
    scratch("index_q", blocks, baselines, dtype=jnp.int32)
    scratch("table_q", 8 * stations // 128 * 8, 128)
    scratch("table_p", 64, 128)
    scratch("collect", blocks * baselines, 256, dtype=bf16)
    scratch("in_tile", blocks * 4 * 16, baselines, dtype=bf16)
    scratch("toward", 64, baselines)
    scratch("terms", 64, baselines)
    scratch("back", 64, baselines)
    scratch("parts_p", baselines // 128 * 16 * blocks, 128)
    scratch("parts_q", baselines // 128 * 16 * blocks, 128)
    scratch("weights", blocks, baselines)
    scratch("sums", 128, 128)
    scratch("gain", 64, 128)
    scratch("anchor", 64, 128)
    scratch("dual", stations // 16, 128)
    scratch("e_src", PASSES, 8, 128)
    scratch("e_all", PASSES, everyone, 128)
    scratch("r_src", PASSES, baselines // 16, 128)
    scratch("r_all", PASSES, blocks * baselines // 16, 128)
    scratch("g_src", PASSES, stations // 16, 128)
    scratch("g_all", PASSES, blocks * stations // 16, 128)
    scratch("f_src", stations // 16, 128)
    scratch("f_all", chans, stations // 16, 128)
    scratch("s_src", blocks, 4, 128)
    scratch("s_all", everyone, 4, 128)
    scratch("j_src", blocks, 4, 128)
    scratch("j_all", blocks, 4, 128)
    SCRATCH.append(("pointing", pltpu.SMEM((SOURCES,), jnp.int32)))
    SCRATCH.append(("rhos", pltpu.SMEM((PATHS,), f32)))
    dma = pltpu.SemaphoreType.DMA
    SCRATCH.append(("load_sem", dma((5 + 3 * stations // 128,))))
    for name, *shape in (
        ("p_sem", 2),
        ("d_sem", 2),
        ("e_sem", PASSES, 2),
        ("r_sem", PASSES, 3),
        ("g_sem", PASSES, 2),
        ("f_sem", 2),
        ("s_sem", 2),
        ("j_sem", 2),
    ):
        SCRATCH.append((name, dma(tuple(shape))))


class Held:
    def __init__(self, refs):
        for (name, _), ref in zip(SCRATCH, refs, strict=True):
            setattr(self, name, ref)


def kernel(
    chans,
    blocks,
    table,
    pointing_hbm,
    rhos_hbm,
    vis_hbm,
    model_hbm,
    pairs_hbm,
    gain_hbm,
    poly_hbm,
    dual_hbm,
    packed,
    *refs,
):
    v = Held(refs)
    stations = gain_hbm.shape[1]
    chan = lax.axis_index("chan")
    stn = lax.axis_index("stn")
    everyone = chans * blocks
    me = chan * blocks + stn
    baselines = v.vis.shape[1]
    tiles = stations // 128
    chunks = baselines // WIDE
    samples = float(everyone * baselines)

    flips = [(1 - 2 * lax.rem(lax.div(me, 1 << n), 2)) * (1 << n) for n in range(7)]

    def flipped(mask, start, count, base):
        for n in range(count):
            if mask >> n & 1:
                base = base + flips[start + n]
        return base

    uppers = [flipped(m, 4, 3, me) for m in range(8)]
    lowers = [flipped(m, 0, 4, 0) for m in range(16)]
    masks = masks_by_hops(everyone)

    def peer_of(mask):
        return uppers[mask >> 4] + lowers[mask & 15]

    stn_masks = [m for m in masks if m < blocks]
    chan_masks = [m for m in masks if m % blocks == 0]

    barrier = pltpu.get_barrier_semaphore()
    for mask in masks:
        pl.semaphore_signal(barrier, inc=1, device_id=peer_of(mask), device_id_type=LOGICAL)

    pointing, rhos = v.pointing, v.rhos
    moves = [(pointing_hbm, pointing), (rhos_hbm, rhos), (model_hbm, v.model)]
    moves += [(pairs_hbm, v.pairs), (vis_hbm, v.vis)]
    for src, dst in ((gain_hbm, v.whole), (dual_hbm, v.dual_in), (poly_hbm, v.poly)):
        rows = src.shape[0]
        moves += [
            (src.at[:, pl.ds(128 * j, 128)], dst.at[pl.ds(rows * j, rows)]) for j in range(tiles)
        ]
    loads = [pltpu.make_async_copy(a, b, v.load_sem.at[n]) for n, (a, b) in enumerate(moves)]
    for copy in loads:
        copy.start()

    def remote(src, dst, sem, peer):
        pltpu.make_async_remote_copy(
            src_ref=src,
            dst_ref=dst,
            send_sem=sem.at[0],
            recv_sem=sem.at[1],
            device_id=peer,
            device_id_type=LOGICAL,
        ).start()

    def to_stn(src, dst, sem):
        for mask in stn_masks:
            remote(src(stn + lowers[mask]), dst, sem, peer_of(mask))

    def to_partner(src, dst, sem):
        pltpu.make_async_remote_copy(
            src_ref=src,
            dst_ref=dst,
            send_sem=sem.at[0],
            recv_sem=sem.at[2],
            device_id=peer_of(1),
            device_id_type=LOGICAL,
        ).start()

    def wait_all(ref, sem):
        pltpu.make_async_copy(ref, ref, sem).wait()

    def chunk(i):
        return pl.ds(pl.multiple_of(i * WIDE, WIDE), WIDE)

    def entries(ref, at):
        return [(ref[8 * i : 8 * i + 8, at], ref[32 + 8 * i : 40 + 8 * i, at]) for i in range(4)]

    def keep(ref, at, values):
        for i in range(4):
            ref[8 * i : 8 * i + 8, at] = values[i][0]
            ref[32 + 8 * i : 40 + 8 * i, at] = values[i][1]

    def as_entries(values):
        return [(values[i], values[4 + i]) for i in range(4)]

    def picked(tile_of, index):
        within, tile = index & 127, index >> 7
        out = []
        for c in range(8):
            value = take(tile_of(c, 0), within)
            for j in range(1, tiles):
                value = jnp.where(tile == j, take(tile_of(c, j), within), value)
            out.append(value)
        return as_entries(out)

    loads[0].wait()
    loads[1].wait()

    lane = lax.broadcasted_iota(jnp.int32, (128, 128), 1)
    high = lax.broadcasted_iota(jnp.int32, (128, 128), 0)
    point = jnp.zeros((128, 128), jnp.int32)
    for s in range(SOURCES):
        point = jnp.where(lane % SOURCES == s, pointing[s], point)
    left, right = high % 64 // PATHS, high % PATHS
    component = jnp.where(high < 64, left, right)
    direction = jnp.where(high < 64, right, left)
    member = jnp.where((component == lane // SOURCES) & (direction == point), 1.0, 0.0).astype(bf16)
    loads[2].wait()

    def combine(*accs):
        twice = jnp.concatenate([member, member], axis=1)
        for i in range(baselines // 256):
            m = v.model[:, 256 * i : 256 * i + 256]
            m0 = m.astype(bf16)
            rest = m - m0.astype(f32)
            m1 = rest.astype(bf16)
            m2 = (rest - m1.astype(f32)).astype(bf16)
            two = jnp.concatenate([m0, m1], axis=0)
            one = jnp.concatenate([m2, jnp.zeros((128, 256), bf16)], axis=0)
            for n, part in enumerate((two, one)):
                pltpu.matmul_push_rhs(part, staging_register=n, mxu_index=i % 2)
                pltpu.matmul_acc_lhs(accs[i % 2], twice, load_staged_rhs=n)
            both = pltpu.matmul_pop(accs[i % 2])
            v.coherent[:, 256 * i : 256 * i + 256] = both[0:64]
            for k in range(PATHS):
                for j in range(2):
                    row = 64 * k + 8 * (2 * i + j)
                    v.d_src[row : row + 8] = both[64 + 8 * k : 72 + 8 * k, 128 * j : 128 * j + 128]

    pl.run_scoped(combine, *[pltpu.ACC(m)((128, 256), f32) for m in range(2)])

    def mine(t):
        value = f32(0.0)
        for f in range(chans):
            value = jnp.where(chan == f, f32(table[f, t]), value)
        return value

    my_basis = [mine(t) for t in range(TERMS)]
    for copy in loads[3:]:
        copy.wait()

    def consensus_of(fit):
        value = my_basis[0] * fit[0]
        for t in range(1, TERMS):
            value = value + my_basis[t] * fit[t]
        return value

    def to_tiles(ref, rows):
        for j in range(tiles):
            ref[pl.ds(j, 8, stride=8), :] = rows[8 * j : 8 * j + 8]

    def own_of(ref, rows, start):
        return jnp.concatenate(
            [ref[pl.ds(rows * j + start + stn, 8, stride=8), :] for j in range(tiles)], axis=0
        )

    v.gain[...] = jnp.zeros((64, 128), f32)
    v.anchor[...] = jnp.zeros((64, 128), f32)
    v.sums[...] = jnp.zeros((128, 128), f32)
    to_tiles(v.gain, own_of(v.whole, 64, 0))
    dual_rows = own_of(v.dual_in, 64, 0)
    v.dual[...] = dual_rows
    to_tiles(v.anchor, consensus_of([own_of(v.poly, 64 * TERMS, 64 * t) for t in range(TERMS)]) - dual_rows)
    rho = rhos[stn]

    def keep_part(ref, i, n, value):
        ref[pl.ds(16 * blocks * i + n, blocks, stride=16), :] = value

    zeros = jnp.zeros((8, WIDE), f32)
    for n in range(12, 16):
        for i in range(chunks):
            keep_part(v.parts_p, i, n, zeros)
            keep_part(v.parts_q, i, n, zeros)
    sub = lax.broadcasted_iota(jnp.int32, (8, 128), 0)
    own_tile = pl.multiple_of(lax.div(stn, 2) * 64, 64)

    def spread_tables():
        rows = [v.gain[pl.ds(j, 8, stride=8), :] for j in range(tiles)]
        for c in range(8):
            per_block = None
            for j in range(tiles):
                value = jnp.broadcast_to(rows[j][c : c + 1], (8, 128))
                at = 8 * (c * tiles + j)
                v.table_q[at : at + 8, :] = value
                per_block = value if j == 0 else jnp.where(sub // 2 == j, value, per_block)
            v.table_p[8 * c : 8 * c + 8, :] = per_block

    def own_terms(i, _):
        at = chunk(i)
        d = entries(v.d_own, at)
        p = v.index_p[:, at]
        gain_p = as_entries([take(v.table_p[8 * c : 8 * c + 8, :], p) for c in range(8)])
        h = product(gain_p, d)
        keep(v.back, at, h)
        for n, part in enumerate(gram_of_adjoint(h)):
            keep_part(v.parts_q, i, n, part)

        def tile_of(c, j):
            return v.table_q[8 * (c * tiles + j) : 8 * (c * tiles + j) + 8, :]

        y = product_with_adjoint(d, picked(tile_of, v.index_q[:, at]))
        keep(v.toward, at, y)
        for n, part in enumerate(gram(y)):
            keep_part(v.parts_p, i, n, part)
        keep(v.terms, at, product(gain_p, y))
        return 0

    own_g, own_r = stations // 16, baselines // 16
    g_rows = pl.ds(pl.multiple_of(own_g * stn, own_g), own_g)
    r_rows = pl.ds(pl.multiple_of(own_r * stn, own_r), own_r)

    def pass_on(it):
        wait_all(v.r_all.at[it, pl.ds(0, (blocks // 2 - 1) * own_r)], v.r_sem.at[it, 1])
        for mask in stn_masks:
            if mask % 2 == 0:
                start = pl.multiple_of(own_r * (stn + lowers[mask]), own_r)
                rows = v.r_all.at[it, pl.ds(start, own_r)]
                to_partner(rows, rows, v.r_sem.at[it])

    def one_pass(it, _):
        spread_tables()

        @pl.when(it > 0)
        def _():
            lax.fori_loop(0, chunks, own_terms, 0, unroll=True)
            wait_all(v.g_all.at[it - 1, pl.ds(0, (blocks - 1) * own_g)], v.g_sem.at[it - 1, 1])
            for j in range(tiles):
                for c in range(8):
                    v.whole[64 * j + 8 * c : 64 * j + 8 * c + 8] = v.g_all[
                        it - 1, pl.ds(8 * j + c, blocks, stride=own_g), :
                    ]

        def residuals(i, total):
            at = chunk(i)
            first = jnp.broadcast_to(v.pairs[0:1, at], (8, WIDE)) & 127
            second = jnp.broadcast_to(v.pairs[1:2, at], (8, WIDE))

            def tile_of(c, j):
                return v.whole[64 * j + 8 * c : 64 * j + 8 * c + 8]

            y = product_with_adjoint(entries(v.coherent, at), picked(tile_of, second))
            gain_p = as_entries(
                [take(v.whole[pl.ds(own_tile + 8 * c, 8)], first) for c in range(8)]
            )
            g = product(gain_p, y)
            e = None
            for n in range(4):
                for part in range(2):
                    c = n + 4 * part
                    left = v.vis[c : c + 1, at] - jnp.sum(g[n][part], axis=0, keepdims=True)
                    e = left * left if e is None else e + left * left
                    v.r_src[it, pl.ds(8 * i + c, 1)] = left
            return total + e

        total = lax.fori_loop(0, chunks, residuals, jnp.zeros((1, WIDE), f32), unroll=True)
        v.e_src[it, 0:1] = total
        v.e_all[it, pl.ds(me, 1)] = total

        @pl.when(it == 0)
        def _():
            pl.semaphore_wait(barrier, everyone - 1)
            to_stn(lambda _: v.pairs, v.pairs_all.at[stn], v.p_sem)

        for mask in stn_masks:
            if mask % 2 == 0:
                remote(v.r_src.at[it], v.r_all.at[it, r_rows], v.r_sem.at[it], peer_of(mask))
        to_partner(v.r_src.at[it], v.r_all.at[it, r_rows], v.r_sem.at[it])
        for mask in masks:
            remote(v.e_src.at[it, pl.ds(0, 1)], v.e_all.at[it, pl.ds(me, 1)], v.e_sem.at[it], peer_of(mask))

        v.r_all[it, r_rows] = v.r_src[it]

        @pl.when(it == 0)
        def _():
            to_stn(
                lambda peer: v.d_src.at[pl.ds(pl.multiple_of(own_r * peer, own_r), own_r)],
                v.d_all.at[r_rows],
                v.d_sem,
            )
            v.pairs_all[stn] = v.pairs[...]
            v.d_all[r_rows] = v.d_src[r_rows]
            wait_all(v.pairs_all.at[pl.ds(0, blocks - 1)], v.p_sem.at[1])
            column = lax.broadcasted_iota(jnp.int32, (baselines, 128), 1).astype(f32).astype(bf16)
            for i in range(blocks):
                if i == blocks // 2:
                    pass_on(it)
                first = v.pairs_all[i, 0:1, :] & 127
                second = v.pairs_all[i, 1:2, :]
                v.index_p[i : i + 1, :] = first
                v.index_q[i : i + 1, :] = second
                for start, index in ((0, second & 127), (128, first)):
                    across = jnp.broadcast_to(index.astype(f32).astype(bf16), (128, baselines)).T
                    v.collect[baselines * i : baselines * i + baselines, start : start + 128] = jnp.where(
                        column == across, bf16(1.0), bf16(0.0)
                    )
                for j in range(tiles):
                    inside = jnp.where((second >> 7) == j, 1.0, 0.0)
                    at = 16 * (4 * i + j)
                    v.in_tile[at : at + 16, :] = jnp.broadcast_to(inside, (16, baselines)).astype(bf16)
            wait_all(v.d_all.at[pl.ds(0, (blocks - 1) * own_r)], v.d_sem.at[1])
            for i in range(chunks):
                at = slice(WIDE * i, WIDE * i + WIDE)
                for c in range(8):
                    v.d_own[8 * c : 8 * c + 8, at] = v.d_all[pl.ds(8 * i + c, blocks, stride=own_r), :]
            lax.fori_loop(0, chunks, own_terms, 0, unroll=True)

        @pl.when(it > 0)
        def _():
            pass_on(it)

        wait_all(v.r_all.at[it, pl.ds(0, blocks // 2 * own_r)], v.r_sem.at[it, 2])

        def products(i, _):
            at = chunk(i)
            y, h, g = entries(v.toward, at), entries(v.back, at), entries(v.terms, at)
            r = as_entries([v.r_all[it, pl.ds(8 * i + c, blocks, stride=own_r), :] for c in range(8)])
            v.weights[:, at] = power(r[0]) + power(r[1]) + power(r[2]) + power(r[3])
            x = [add(a, b) for a, b in zip(r, g)]
            b = product_with_adjoint(x, y)
            for n, part in enumerate([z[0] for z in b] + [z[1] for z in b]):
                keep_part(v.parts_p, i, 4 + n, part)
            b = adjoint_product(x, h)
            for n, part in enumerate([z[0] for z in b] + [z[1] for z in b]):
                keep_part(v.parts_q, i, 4 + n, part)
            return 0

        lax.fori_loop(0, chunks, products, 0, unroll=True)

        @pl.when(it == INNER)
        def _():
            wait_all(v.f_all.at[pl.ds(0, chans - 1)], v.f_sem.at[1])
            fit = [jnp.zeros((own_g, 128), f32)] * TERMS
            for f in range(chans):
                value = v.f_all[f]
                fit = [fit[t] + f32(table[f, t]) * value for t in range(TERMS)]
            consensus = consensus_of([z * f32(1.0 / chans) for z in fit])
            after = v.f_src[...] - consensus
            v.dual[...] = after
            to_tiles(v.anchor, consensus - after)

        wait_all(v.e_all.at[it, pl.ds(0, everyone - 1)], v.e_sem.at[it, 1])
        total = jnp.sum(v.e_all[it], axis=0, keepdims=True)
        noise = jnp.sum(total, axis=1, keepdims=True) * f32(1.0 / samples) + TINY
        scale = jnp.broadcast_to(1.0 / noise, (1, 128))
        scale = jnp.concatenate([scale] * (baselines // 128), axis=1)
        v.weights[...] = (NU + 2.0) / (NU + v.weights[...] * scale)

        def block_of(ref, i, start):
            rows = [16 * (blocks * n + i) for n in range(start // 128, start // 128 + 2)]
            return jnp.concatenate([ref[row : row + 16, :] for row in rows], axis=1)

        def accumulate(*accs):
            acc_q, acc_p = accs[:2], (accs[2 : 2 + tiles], accs[2 + tiles :])
            for step in range(blocks * baselines // 512):
                for m in range(2):
                    i = 2 * (step * 256 // baselines) + m
                    start = baselines * i + step * 256 % baselines
                    at = slice(start, start + 256)
                    pltpu.matmul_push_rhs(v.collect[at, :], staging_register=step % 2, mxu_index=m)
                    here = slice(start - baselines * i, start - baselines * i + 256)
                    weight = v.weights[i : i + 1, here]
                    top, rest = halves(block_of(v.parts_q, i, here.start) * weight)
                    pieces = []
                    for j in range(tiles):
                        inside = v.in_tile[16 * (4 * i + j) : 16 * (4 * i + j) + 16, here]
                        pieces += [top * inside, rest * inside]
                    pltpu.matmul_acc_lhs(
                        acc_q[m], jnp.concatenate(pieces, axis=0), load_staged_rhs=step % 2
                    )
                    pieces = halves(block_of(v.parts_p, i, here.start) * weight)
                    pltpu.matmul_acc_lhs(acc_p[m][i // 2], jnp.concatenate(pieces, axis=0))
            every = pltpu.matmul_pop(acc_q[0]) + pltpu.matmul_pop(acc_q[1])
            for j in range(tiles):
                here = pltpu.matmul_pop(acc_p[0][j]) + pltpu.matmul_pop(acc_p[1][j])
                got = every[32 * j : 32 * j + 32, 0:128] + here[:, 128:256]
                v.sums[pl.ds(j, 16, stride=8), :] = got[0:16] + got[16:32]

        accs = [pltpu.ACC(m)((128, 256), f32) for m in range(2)]
        accs += [pltpu.ACC(m)((32, 256), f32) for m in range(2) for _ in range(tiles)]
        pl.run_scoped(accumulate, *accs)

        def part(n):
            return v.sums[8 * n : 8 * n + 8, :]

        d1, d2, cr, ci = part(0) + rho, part(1) + rho, part(2), part(3)
        over = 1.0 / (d1 * d2 - cr * cr - ci * ci)
        right = as_entries([part(4 + n) + rho * v.anchor[8 * n : 8 * n + 8, :] for n in range(8)])
        up = (cr * over, ci * over)
        s1, s2 = d2 * over, d1 * over
        solved = []
        for r in range(2):
            x, y = right[2 * r], right[2 * r + 1]
            one = mul_conj(y, up)
            two = mul(x, up)
            solved.append((x[0] * s1 - one[0], x[1] * s1 - one[1]))
            solved.append((y[0] * s2 - two[0], y[1] * s2 - two[1]))
        for n in range(4):
            for k in range(2):
                at = 8 * (n + 4 * k)
                v.gain[at : at + 8, :] = 0.5 * (v.gain[at : at + 8, :] + solved[n][k])
        for j in range(tiles):
            v.g_src[it, 8 * j : 8 * j + 8, :] = v.gain[pl.ds(j, 8, stride=8), :]

        @pl.when(it < PASSES - 1)
        def _():
            to_stn(lambda _: v.g_src.at[it], v.g_all.at[it, g_rows], v.g_sem.at[it])
            v.g_all[it, g_rows] = v.g_src[it]

        @pl.when(it == INNER - 1)
        def _():
            v.f_src[...] = v.g_src[it] + v.dual[...]
            v.f_all[chan] = v.f_src[...]
            for mask in chan_masks:
                remote(v.f_src, v.f_all.at[chan], v.f_sem, peer_of(mask))

        return 0

    lax.fori_loop(0, PASSES, one_pass, 0)

    low = lax.broadcasted_iota(jnp.int32, (8, 128), 1) < 64

    def slices(ref, rows):
        for j in range(tiles):
            a = rows[8 * j : 8 * j + 8]
            under = pltpu.roll(a, 4, 0)
            ref[2 * j] = jnp.where(low, a, swap(under))[0:4]
            ref[2 * j + 1] = jnp.where(low, swap(a), under)[0:4]

    last = v.g_src[PASSES - 1]
    slices(v.s_src, last + v.dual[...])
    slices(v.j_src, last)
    for mask in masks:
        block = stn + lowers[mask & 7]
        remote(v.s_src.at[block], v.s_all.at[me], v.s_sem, peer_of(mask))
    to_stn(lambda peer: v.j_src.at[peer], v.j_all.at[stn], v.j_sem)
    v.s_all[me] = v.s_src[stn]
    v.j_all[stn] = v.j_src[stn]
    wait_all(v.j_all.at[pl.ds(0, blocks - 1)], v.j_sem.at[1])

    packed[0:32, :] = v.j_all[...].reshape(32, 128)
    wait_all(v.s_all.at[pl.ds(0, everyone - 1)], v.s_sem.at[1])
    fit = [jnp.zeros((32, 128), f32)] * TERMS
    for f in range(chans):
        value = v.s_all[blocks * f : blocks * f + blocks].reshape(32, 128)
        fit = [fit[t] + f32(table[f, t]) * value for t in range(TERMS)]
    fit = [z * f32(1.0 / chans) for z in fit]
    packed[32:64, :] = v.s_all[pl.ds(blocks * chan, blocks)].reshape(32, 128) - consensus_of(fit)
    for t in range(TERMS):
        packed[64 + 32 * t : 96 + 32 * t, :] = fit[t]

    wait_all(v.pairs_all.at[pl.ds(0, blocks - 1)], v.p_sem.at[0])
    wait_all(v.d_all.at[pl.ds(0, (blocks - 1) * own_r)], v.d_sem.at[0])
    wait_all(v.f_all.at[pl.ds(0, chans - 1)], v.f_sem.at[0])
    wait_all(v.s_all.at[pl.ds(0, everyone - 1)], v.s_sem.at[0])
    wait_all(v.j_all.at[pl.ds(0, blocks - 1)], v.j_sem.at[0])
    for it in range(PASSES):
        wait_all(v.e_all.at[it, pl.ds(0, everyone - 1)], v.e_sem.at[it, 0])
        wait_all(v.r_all.at[it, pl.ds(0, (blocks - 1) * own_r)], v.r_sem.at[it, 0])
        if it < PASSES - 1:
            wait_all(v.g_all.at[it, pl.ds(0, (blocks - 1) * own_g)], v.g_sem.at[it, 0])


def unpack(packed, gain_out, dual_out, fit_out):
    spots = [(gain_out, 0), (dual_out, 0)] + [(fit_out, 64 * t) for t in range(TERMS)]
    for m, (ref, start) in enumerate(spots):
        for n in range(4):
            rows = packed[pl.ds(32 * m + n, PATHS, stride=4), :]
            ref[start + 8 * n : start + 8 * n + 8, :] = rows[:, 0:64]
            ref[start + 32 + 8 * n : start + 40 + 8 * n, :] = swap(rows)[:, 0:64]


def solution(mesh):
    chans, blocks = mesh.shape["chan"], mesh.shape["stn"]
    table = basis_table(chans)
    abstract = mesh.abstract_mesh

    def body(vis, model, pointing, pairs, gains, poly, dual, rhos):
        baselines = vis.shape[2]
        stations = gains.shape[3]

        def run(*refs):
            kernel(chans, blocks, table, *refs)

        lay_out(chans, blocks, baselines, stations)
        any_spec = pl.BlockSpec(memory_space=pltpu.HBM)
        vmem = pl.BlockSpec(memory_space=pltpu.VMEM)
        packed = pl.pallas_call(
            run,
            out_shape=jax.ShapeDtypeStruct((32 * (2 + TERMS), 128), f32),
            in_specs=[any_spec] * 8,
            out_specs=vmem,
            scratch_shapes=[shape for _, shape in SCRATCH],
            compiler_params=pltpu.CompilerParams(
                collective_id=0, has_side_effects=True, vmem_limit_bytes=40 << 20
            ),
            name="calibrate",
        )(
            pltpu.with_memory_space_constraint(pointing.reshape(SOURCES), pltpu.HBM),
            pltpu.with_memory_space_constraint(rhos, pltpu.HBM),
            pltpu.with_memory_space_constraint(vis.reshape(8, baselines), pltpu.HBM),
            pltpu.with_memory_space_constraint(model.reshape(8 * SOURCES, baselines), pltpu.HBM),
            pltpu.with_memory_space_constraint(pairs, pltpu.HBM),
            pltpu.with_memory_space_constraint(gains.reshape(64, stations), pltpu.HBM),
            pltpu.with_memory_space_constraint(poly.reshape(64 * TERMS, stations), pltpu.HBM),
            pltpu.with_memory_space_constraint(dual.reshape(64, stations), pltpu.HBM),
        )
        out = pl.pallas_call(
            unpack,
            out_shape=(
                jax.ShapeDtypeStruct((64, 64), f32),
                jax.ShapeDtypeStruct((64, 64), f32),
                jax.ShapeDtypeStruct((64 * TERMS, 64), f32),
            ),
            in_specs=[vmem],
            out_specs=(vmem, vmem, vmem),
            compiler_params=pltpu.CompilerParams(vmem_limit_bytes=16 << 20),
            name="unpack",
        )(packed)
        return (
            out[0].reshape(1, 8, PATHS, 64),
            out[1].reshape(1, 8, PATHS, 64),
            out[2].reshape(TERMS, 8, PATHS, 64),
        )

    return jax.shard_map(
        body,
        mesh=mesh,
        in_specs=(
            P("chan", None, "stn"),
            P("chan", None, None, "stn"),
            P(),
            P(None, "stn"),
            P("chan", None, None, None),
            P(),
            P("chan", None, None, None),
            P(),
        ),
        out_specs=(
            P("chan", None, None, "stn"),
            P("chan", None, None, "stn"),
            P(None, None, None, "stn"),
        ),
        check_vma=False,
    )
```

```python
import numpy as np
import jax
import jax.numpy as jnp
from jax import lax
from jax.experimental import pallas as pl
from jax.experimental.pallas import tpu as pltpu
from jax.sharding import PartitionSpec as P

PATHS = 8
SOURCES = 16
TERMS = 3
STEPS = 2
INNER = 2
PASSES = STEPS * INNER
NU = 2.0
TINY = 1e-06
LOGICAL = pl.DeviceIdType.LOGICAL
WIDE = 128
bf16 = jnp.bfloat16
f32 = jnp.float32


def basis_table(count):
    frequency = (2.0 * np.arange(count, dtype=np.float32) + 1.0) / np.float32(count) - 1.0
    columns = []
    for degree in range(TERMS):
        column = (frequency**degree).astype(np.float32)
        for earlier in columns:
            column = column - np.sum(earlier * column) / np.float32(count) * earlier
        column = column / np.sqrt(np.sum(column * column) / np.float32(count))
        columns.append(column.astype(np.float32))
    return np.stack(columns, axis=1)


def mul(a, b):
    return (a[0] * b[0] - a[1] * b[1], a[0] * b[1] + a[1] * b[0])


def mul_conj(a, b):
    return (a[0] * b[0] + a[1] * b[1], a[1] * b[0] - a[0] * b[1])


def conj_mul(a, b):
    return (a[0] * b[0] + a[1] * b[1], a[0] * b[1] - a[1] * b[0])


def add(a, b):
    return (a[0] + b[0], a[1] + b[1])


def product(a, b):
    return [
        add(mul(a[0], b[0]), mul(a[1], b[2])),
        add(mul(a[0], b[1]), mul(a[1], b[3])),
        add(mul(a[2], b[0]), mul(a[3], b[2])),
        add(mul(a[2], b[1]), mul(a[3], b[3])),
    ]


def product_with_adjoint(a, b):
    return [
        add(mul_conj(a[0], b[0]), mul_conj(a[1], b[1])),
        add(mul_conj(a[0], b[2]), mul_conj(a[1], b[3])),
        add(mul_conj(a[2], b[0]), mul_conj(a[3], b[1])),
        add(mul_conj(a[2], b[2]), mul_conj(a[3], b[3])),
    ]


def adjoint_product(a, b):
    return [
        add(conj_mul(a[0], b[0]), conj_mul(a[2], b[2])),
        add(conj_mul(a[0], b[1]), conj_mul(a[2], b[3])),
        add(conj_mul(a[1], b[0]), conj_mul(a[3], b[2])),
        add(conj_mul(a[1], b[1]), conj_mul(a[3], b[3])),
    ]


def power(a):
    return a[0] * a[0] + a[1] * a[1]


def gram(y):
    cross = add(mul_conj(y[0], y[2]), mul_conj(y[1], y[3]))
    return [power(y[0]) + power(y[1]), power(y[2]) + power(y[3]), cross[0], cross[1]]


def gram_of_adjoint(h):
    cross = add(conj_mul(h[0], h[1]), conj_mul(h[2], h[3]))
    return [power(h[0]) + power(h[2]), power(h[1]) + power(h[3]), cross[0], cross[1]]


def halves(x):
    top = x.astype(bf16)
    return top, (x - top.astype(f32)).astype(bf16)


def swap(x):
    return pltpu.roll(x, 64, 1)


def take(table, index):
    return jnp.take_along_axis(table, index, axis=1, mode="promise_in_bounds")


def masks_by_hops(everyone):
    hop = (0, 1, 2, 1)
    hops = lambda m: hop[m >> 1 & 3] + hop[m >> 3 & 3] + hop[m >> 5 & 3]
    return sorted(range(1, everyone), key=lambda m: (-hops(m), m))


SCRATCH = []


def scratch(name, *shape, dtype=f32):
    SCRATCH.append((name, pltpu.VMEM(shape, dtype)))


def lay_out(chans, blocks, baselines, stations):
    SCRATCH.clear()
    everyone = chans * blocks
    scratch("vis", 8, baselines)
    scratch("model", 8 * SOURCES, baselines)
    scratch("pairs", 2, baselines, dtype=jnp.int32)
    scratch("whole", 64 * stations // 128, 128)
    scratch("poly", 64 * TERMS * stations // 128, 128)
    scratch("dual_in", 64 * stations // 128, 128)
    scratch("coherent", 64, baselines)
    scratch("d_src", baselines // 128 * 64, 128)
    scratch("d_all", baselines // 128 * 64, 128)
    scratch("d_own", 64, baselines)
    scratch("pairs_all", blocks, 2, baselines, dtype=jnp.int32)
    scratch("index_p", blocks, baselines, dtype=jnp.int32)
    scratch("index_q", blocks, baselines, dtype=jnp.int32)
    scratch("table_q", 8 * stations // 128 * 8, 128)
    scratch("table_p", 64, 128)
    scratch("collect", blocks * baselines, 256, dtype=bf16)
    scratch("in_tile", blocks * 4 * 16, baselines, dtype=bf16)
    scratch("toward", 64, baselines)
    scratch("terms", 64, baselines)
    scratch("back", 64, baselines)
    scratch("parts_p", baselines // 128 * 16 * blocks, 128)
    scratch("parts_q", baselines // 128 * 16 * blocks, 128)
    scratch("weights", blocks, baselines)
    scratch("sums", 128, 128)
    scratch("gain", 64, 128)
    scratch("anchor", 64, 128)
    scratch("dual", stations // 16, 128)
    scratch("e_src", PASSES, 8, 128)
    scratch("e_all", PASSES, everyone, 128)
    scratch("r_src", PASSES, baselines // 16, 128)
    scratch("r_all", PASSES, blocks * baselines // 16, 128)
    scratch("g_src", PASSES, stations // 16, 128)
    scratch("g_all", PASSES, blocks * stations // 16, 128)
    scratch("f_src", stations // 16, 128)
    scratch("f_all", chans, stations // 16, 128)
    scratch("s_src", blocks, 4, 128)
    scratch("s_all", everyone, 4, 128)
    scratch("j_src", blocks, 4, 128)
    scratch("j_all", blocks, 4, 128)
    SCRATCH.append(("pointing", pltpu.SMEM((SOURCES,), jnp.int32)))
    SCRATCH.append(("rhos", pltpu.SMEM((PATHS,), f32)))
    dma = pltpu.SemaphoreType.DMA
    SCRATCH.append(("load_sem", dma((5 + 3 * stations // 128,))))
    for name, *shape in (
        ("p_sem", 2),
        ("d_sem", 2),
        ("e_sem", PASSES, 2),
        ("r_sem", PASSES, 4),
        ("g_sem", PASSES, 2),
        ("f_sem", 2),
        ("s_sem", 2),
        ("j_sem", 2),
    ):
        SCRATCH.append((name, dma(tuple(shape))))


class Held:
    def __init__(self, refs):
        for (name, _), ref in zip(SCRATCH, refs, strict=True):
            setattr(self, name, ref)


def kernel(
    chans,
    blocks,
    table,
    pointing_hbm,
    rhos_hbm,
    vis_hbm,
    model_hbm,
    pairs_hbm,
    gain_hbm,
    poly_hbm,
    dual_hbm,
    packed,
    *refs,
):
    v = Held(refs)
    stations = gain_hbm.shape[1]
    chan = lax.axis_index("chan")
    stn = lax.axis_index("stn")
    everyone = chans * blocks
    me = chan * blocks + stn
    baselines = v.vis.shape[1]
    tiles = stations // 128
    chunks = baselines // WIDE
    samples = float(everyone * baselines)

    flips = [(1 - 2 * lax.rem(lax.div(me, 1 << n), 2)) * (1 << n) for n in range(7)]

    def flipped(mask, start, count, base):
        for n in range(count):
            if mask >> n & 1:
                base = base + flips[start + n]
        return base

    uppers = [flipped(m, 4, 3, me) for m in range(8)]
    lowers = [flipped(m, 0, 4, 0) for m in range(16)]
    masks = masks_by_hops(everyone)

    def peer_of(mask):
        return uppers[mask >> 4] + lowers[mask & 15]

    stn_masks = [m for m in masks if m < blocks]
    chan_masks = [m for m in masks if m % blocks == 0]

    barrier = pltpu.get_barrier_semaphore()
    for mask in masks:
        pl.semaphore_signal(barrier, inc=1, device_id=peer_of(mask), device_id_type=LOGICAL)

    pointing, rhos = v.pointing, v.rhos
    moves = [(pointing_hbm, pointing), (rhos_hbm, rhos), (model_hbm, v.model)]
    moves += [(pairs_hbm, v.pairs), (vis_hbm, v.vis)]
    for src, dst in ((gain_hbm, v.whole), (dual_hbm, v.dual_in), (poly_hbm, v.poly)):
        rows = src.shape[0]
        moves += [
            (src.at[:, pl.ds(128 * j, 128)], dst.at[pl.ds(rows * j, rows)]) for j in range(tiles)
        ]
    loads = [pltpu.make_async_copy(a, b, v.load_sem.at[n]) for n, (a, b) in enumerate(moves)]
    for copy in loads:
        copy.start()

    def remote(src, dst, sem, peer):
        pltpu.make_async_remote_copy(
            src_ref=src,
            dst_ref=dst,
            send_sem=sem.at[0],
            recv_sem=sem.at[1],
            device_id=peer,
            device_id_type=LOGICAL,
        ).start()

    def to_stn(src, dst, sem):
        for mask in stn_masks:
            remote(src(stn + lowers[mask]), dst, sem, peer_of(mask))

    def to_partner(src, dst, sem):
        pltpu.make_async_remote_copy(
            src_ref=src,
            dst_ref=dst,
            send_sem=sem.at[0],
            recv_sem=sem.at[3],
            device_id=peer_of(1),
            device_id_type=LOGICAL,
        ).start()

    def wait_all(ref, sem):
        pltpu.make_async_copy(ref, ref, sem).wait()

    def chunk(i):
        return pl.ds(pl.multiple_of(i * WIDE, WIDE), WIDE)

    def entries(ref, at):
        return [(ref[8 * i : 8 * i + 8, at], ref[32 + 8 * i : 40 + 8 * i, at]) for i in range(4)]

    def keep(ref, at, values):
        for i in range(4):
            ref[8 * i : 8 * i + 8, at] = values[i][0]
            ref[32 + 8 * i : 40 + 8 * i, at] = values[i][1]

    def as_entries(values):
        return [(values[i], values[4 + i]) for i in range(4)]

    def picked(tile_of, index):
        within, tile = index & 127, index >> 7
        out = []
        for c in range(8):
            value = take(tile_of(c, 0), within)
            for j in range(1, tiles):
                value = jnp.where(tile == j, take(tile_of(c, j), within), value)
            out.append(value)
        return as_entries(out)

    loads[0].wait()
    loads[1].wait()

    lane = lax.broadcasted_iota(jnp.int32, (128, 128), 1)
    high = lax.broadcasted_iota(jnp.int32, (128, 128), 0)
    point = jnp.zeros((128, 128), jnp.int32)
    for s in range(SOURCES):
        point = jnp.where(lane % SOURCES == s, pointing[s], point)
    left, right = high % 64 // PATHS, high % PATHS
    component = jnp.where(high < 64, left, right)
    direction = jnp.where(high < 64, right, left)
    member = jnp.where((component == lane // SOURCES) & (direction == point), 1.0, 0.0).astype(bf16)
    loads[2].wait()

    def combine(*accs):
        twice = jnp.concatenate([member, member], axis=1)
        for i in range(baselines // 256):
            m = v.model[:, 256 * i : 256 * i + 256]
            m0 = m.astype(bf16)
            rest = m - m0.astype(f32)
            m1 = rest.astype(bf16)
            m2 = (rest - m1.astype(f32)).astype(bf16)
            two = jnp.concatenate([m0, m1], axis=0)
            one = jnp.concatenate([m2, jnp.zeros((128, 256), bf16)], axis=0)
            for n, part in enumerate((two, one)):
                pltpu.matmul_push_rhs(part, staging_register=n, mxu_index=i % 2)
                pltpu.matmul_acc_lhs(accs[i % 2], twice, load_staged_rhs=n)
            both = pltpu.matmul_pop(accs[i % 2])
            v.coherent[:, 256 * i : 256 * i + 256] = both[0:64]
            for k in range(PATHS):
                for j in range(2):
                    row = 64 * k + 8 * (2 * i + j)
                    v.d_src[row : row + 8] = both[64 + 8 * k : 72 + 8 * k, 128 * j : 128 * j + 128]

    pl.run_scoped(combine, *[pltpu.ACC(m)((128, 256), f32) for m in range(2)])

    def mine(t):
        value = f32(0.0)
        for f in range(chans):
            value = jnp.where(chan == f, f32(table[f, t]), value)
        return value

    my_basis = [mine(t) for t in range(TERMS)]
    for copy in loads[3:]:
        copy.wait()

    def consensus_of(fit):
        value = my_basis[0] * fit[0]
        for t in range(1, TERMS):
            value = value + my_basis[t] * fit[t]
        return value

    def to_tiles(ref, rows):
        for j in range(tiles):
            ref[pl.ds(j, 8, stride=8), :] = rows[8 * j : 8 * j + 8]

    def own_of(ref, rows, start):
        return jnp.concatenate(
            [ref[pl.ds(rows * j + start + stn, 8, stride=8), :] for j in range(tiles)], axis=0
        )

    v.gain[...] = jnp.zeros((64, 128), f32)
    v.anchor[...] = jnp.zeros((64, 128), f32)
    v.sums[...] = jnp.zeros((128, 128), f32)
    to_tiles(v.gain, own_of(v.whole, 64, 0))
    dual_rows = own_of(v.dual_in, 64, 0)
    v.dual[...] = dual_rows
    to_tiles(v.anchor, consensus_of([own_of(v.poly, 64 * TERMS, 64 * t) for t in range(TERMS)]) - dual_rows)
    rho = rhos[stn]

    def keep_part(ref, i, n, value):
        ref[pl.ds(16 * blocks * i + n, blocks, stride=16), :] = value

    zeros = jnp.zeros((8, WIDE), f32)
    for n in range(12, 16):
        for i in range(chunks):
            keep_part(v.parts_p, i, n, zeros)
            keep_part(v.parts_q, i, n, zeros)
    sub = lax.broadcasted_iota(jnp.int32, (8, 128), 0)
    own_tile = pl.multiple_of(lax.div(stn, 2) * 64, 64)

    def spread_tables():
        rows = [v.gain[pl.ds(j, 8, stride=8), :] for j in range(tiles)]
        for c in range(8):
            per_block = None
            for j in range(tiles):
                value = jnp.broadcast_to(rows[j][c : c + 1], (8, 128))
                at = 8 * (c * tiles + j)
                v.table_q[at : at + 8, :] = value
                per_block = value if j == 0 else jnp.where(sub // 2 == j, value, per_block)
            v.table_p[8 * c : 8 * c + 8, :] = per_block

    def own_terms(i, _):
        at = chunk(i)
        d = entries(v.d_own, at)
        p = v.index_p[:, at]
        gain_p = as_entries([take(v.table_p[8 * c : 8 * c + 8, :], p) for c in range(8)])
        h = product(gain_p, d)
        keep(v.back, at, h)
        for n, part in enumerate(gram_of_adjoint(h)):
            keep_part(v.parts_q, i, n, part)

        def tile_of(c, j):
            return v.table_q[8 * (c * tiles + j) : 8 * (c * tiles + j) + 8, :]

        y = product_with_adjoint(d, picked(tile_of, v.index_q[:, at]))
        keep(v.toward, at, y)
        for n, part in enumerate(gram(y)):
            keep_part(v.parts_p, i, n, part)
        keep(v.terms, at, product(gain_p, y))
        return 0

    own_g, own_r = stations // 16, baselines // 16
    g_rows = pl.ds(pl.multiple_of(own_g * stn, own_g), own_g)
    r_rows = pl.ds(pl.multiple_of(own_r * stn, own_r), own_r)
    half = own_r // 2

    def half_rows(block, part):
        return pl.ds(pl.multiple_of(own_r * block + half * part, half), half)

    even_masks = [mask for mask in stn_masks if mask % 2 == 0]

    def send_residuals(it, part):
        src = v.r_src.at[it, pl.ds(half * part, half)]
        dst = v.r_all.at[it, half_rows(stn, part)]
        for mask in even_masks:
            pltpu.make_async_remote_copy(
                src_ref=src,
                dst_ref=dst,
                send_sem=v.r_sem.at[it, 0],
                recv_sem=v.r_sem.at[it, 1 + part],
                device_id=peer_of(mask),
                device_id_type=LOGICAL,
            ).start()
        to_partner(src, dst, v.r_sem.at[it])

    def pass_on(it):
        for part in range(2):
            wait_all(v.r_all.at[it, pl.ds(0, (blocks // 2 - 1) * half)], v.r_sem.at[it, 1 + part])
            for mask in even_masks:
                rows = v.r_all.at[it, half_rows(stn + lowers[mask], part)]
                to_partner(rows, rows, v.r_sem.at[it])

    def residuals_of(it, part):
        def residuals(i, total):
            at = chunk(i)
            first = jnp.broadcast_to(v.pairs[0:1, at], (8, WIDE)) & 127
            second = jnp.broadcast_to(v.pairs[1:2, at], (8, WIDE))

            def tile_of(c, j):
                return v.whole[64 * j + 8 * c : 64 * j + 8 * c + 8]

            y = product_with_adjoint(entries(v.coherent, at), picked(tile_of, second))
            gain_p = as_entries(
                [take(v.whole[pl.ds(own_tile + 8 * c, 8)], first) for c in range(8)]
            )
            g = product(gain_p, y)
            e = None
            for n in range(4):
                for part in range(2):
                    c = n + 4 * part
                    left = v.vis[c : c + 1, at] - jnp.sum(g[n][part], axis=0, keepdims=True)
                    e = left * left if e is None else e + left * left
                    v.r_src[it, pl.ds(8 * i + c, 1)] = left
            return total + e

        first = part * chunks // 2
        zero = jnp.zeros((1, WIDE), f32)
        return lax.fori_loop(first, first + chunks // 2, residuals, zero, unroll=True)

    def keep_energy(it, total):
        v.e_src[it, 0:1] = total
        v.e_all[it, pl.ds(me, 1)] = total

    keep_energy(0, residuals_of(0, 0) + residuals_of(0, 1))
    pl.semaphore_wait(barrier, everyone - 1)

    def one_pass(it, _):
        @pl.when(it > 0)
        def _():
            spread_tables()
            lax.fori_loop(0, chunks, own_terms, 0, unroll=True)
            wait_all(v.g_all.at[it - 1, pl.ds(0, (blocks - 1) * own_g)], v.g_sem.at[it - 1, 1])
            for j in range(tiles):
                for c in range(8):
                    v.whole[64 * j + 8 * c : 64 * j + 8 * c + 8] = v.g_all[
                        it - 1, pl.ds(8 * j + c, blocks, stride=own_g), :
                    ]
            total = residuals_of(it, 0)
            send_residuals(it, 0)
            keep_energy(it, total + residuals_of(it, 1))

        @pl.when(it == 0)
        def _():
            to_stn(lambda _: v.pairs, v.pairs_all.at[stn], v.p_sem)
            send_residuals(it, 0)

        send_residuals(it, 1)
        for mask in masks:
            remote(v.e_src.at[it, pl.ds(0, 1)], v.e_all.at[it, pl.ds(me, 1)], v.e_sem.at[it], peer_of(mask))

        v.r_all[it, r_rows] = v.r_src[it]

        @pl.when(it == 0)
        def _():
            to_stn(
                lambda peer: v.d_src.at[pl.ds(pl.multiple_of(own_r * peer, own_r), own_r)],
                v.d_all.at[r_rows],
                v.d_sem,
            )
            spread_tables()
            v.pairs_all[stn] = v.pairs[...]
            v.d_all[r_rows] = v.d_src[r_rows]
            wait_all(v.pairs_all.at[pl.ds(0, blocks - 1)], v.p_sem.at[1])
            column = lax.broadcasted_iota(jnp.int32, (baselines, 128), 1).astype(f32).astype(bf16)
            for i in range(blocks):
                if i == blocks // 2:
                    pass_on(it)
                first = v.pairs_all[i, 0:1, :] & 127
                second = v.pairs_all[i, 1:2, :]
                v.index_p[i : i + 1, :] = first
                v.index_q[i : i + 1, :] = second
                for start, index in ((0, second & 127), (128, first)):
                    across = jnp.broadcast_to(index.astype(f32).astype(bf16), (128, baselines)).T
                    v.collect[baselines * i : baselines * i + baselines, start : start + 128] = jnp.where(
                        column == across, bf16(1.0), bf16(0.0)
                    )
                for j in range(tiles):
                    inside = jnp.where((second >> 7) == j, 1.0, 0.0)
                    at = 16 * (4 * i + j)
                    v.in_tile[at : at + 16, :] = jnp.broadcast_to(inside, (16, baselines)).astype(bf16)
            wait_all(v.d_all.at[pl.ds(0, (blocks - 1) * own_r)], v.d_sem.at[1])
            for i in range(chunks):
                at = slice(WIDE * i, WIDE * i + WIDE)
                for c in range(8):
                    v.d_own[8 * c : 8 * c + 8, at] = v.d_all[pl.ds(8 * i + c, blocks, stride=own_r), :]
            lax.fori_loop(0, chunks, own_terms, 0, unroll=True)

        @pl.when(it > 0)
        def _():
            pass_on(it)

        wait_all(v.r_all.at[it, pl.ds(0, blocks // 2 * own_r)], v.r_sem.at[it, 3])

        def products(i, _):
            at = chunk(i)
            y, h, g = entries(v.toward, at), entries(v.back, at), entries(v.terms, at)
            r = as_entries([v.r_all[it, pl.ds(8 * i + c, blocks, stride=own_r), :] for c in range(8)])
            v.weights[:, at] = power(r[0]) + power(r[1]) + power(r[2]) + power(r[3])
            x = [add(a, b) for a, b in zip(r, g)]
            b = product_with_adjoint(x, y)
            for n, part in enumerate([z[0] for z in b] + [z[1] for z in b]):
                keep_part(v.parts_p, i, 4 + n, part)
            b = adjoint_product(x, h)
            for n, part in enumerate([z[0] for z in b] + [z[1] for z in b]):
                keep_part(v.parts_q, i, 4 + n, part)
            return 0

        lax.fori_loop(0, chunks, products, 0, unroll=True)

        @pl.when(it == INNER)
        def _():
            wait_all(v.f_all.at[pl.ds(0, chans - 1)], v.f_sem.at[1])
            fit = [jnp.zeros((own_g, 128), f32)] * TERMS
            for f in range(chans):
                value = v.f_all[f]
                fit = [fit[t] + f32(table[f, t]) * value for t in range(TERMS)]
            consensus = consensus_of([z * f32(1.0 / chans) for z in fit])
            after = v.f_src[...] - consensus
            v.dual[...] = after
            to_tiles(v.anchor, consensus - after)

        wait_all(v.e_all.at[it, pl.ds(0, everyone - 1)], v.e_sem.at[it, 1])
        total = jnp.sum(v.e_all[it], axis=0, keepdims=True)
        noise = jnp.sum(total, axis=1, keepdims=True) * f32(1.0 / samples) + TINY
        scale = jnp.broadcast_to(1.0 / noise, (1, 128))
        scale = jnp.concatenate([scale] * (baselines // 128), axis=1)
        v.weights[...] = (NU + 2.0) / (NU + v.weights[...] * scale)

        def block_of(ref, i, start):
            rows = [16 * (blocks * n + i) for n in range(start // 128, start // 128 + 2)]
            return jnp.concatenate([ref[row : row + 16, :] for row in rows], axis=1)

        def accumulate(*accs):
            acc_q, acc_p = accs[:2], (accs[2 : 2 + tiles], accs[2 + tiles :])
            for step in range(blocks * baselines // 512):
                for m in range(2):
                    i = 2 * (step * 256 // baselines) + m
                    start = baselines * i + step * 256 % baselines
                    at = slice(start, start + 256)
                    pltpu.matmul_push_rhs(v.collect[at, :], staging_register=step % 2, mxu_index=m)
                    here = slice(start - baselines * i, start - baselines * i + 256)
                    weight = v.weights[i : i + 1, here]
                    top, rest = halves(block_of(v.parts_q, i, here.start) * weight)
                    pieces = []
                    for j in range(tiles):
                        inside = v.in_tile[16 * (4 * i + j) : 16 * (4 * i + j) + 16, here]
                        pieces += [top * inside, rest * inside]
                    pltpu.matmul_acc_lhs(
                        acc_q[m], jnp.concatenate(pieces, axis=0), load_staged_rhs=step % 2
                    )
                    pieces = halves(block_of(v.parts_p, i, here.start) * weight)
                    pltpu.matmul_acc_lhs(acc_p[m][i // 2], jnp.concatenate(pieces, axis=0))
            every = pltpu.matmul_pop(acc_q[0]) + pltpu.matmul_pop(acc_q[1])
            for j in range(tiles):
                here = pltpu.matmul_pop(acc_p[0][j]) + pltpu.matmul_pop(acc_p[1][j])
                got = every[32 * j : 32 * j + 32, 0:128] + here[:, 128:256]
                v.sums[pl.ds(j, 16, stride=8), :] = got[0:16] + got[16:32]

        accs = [pltpu.ACC(m)((128, 256), f32) for m in range(2)]
        accs += [pltpu.ACC(m)((32, 256), f32) for m in range(2) for _ in range(tiles)]
        pl.run_scoped(accumulate, *accs)

        def part(n):
            return v.sums[8 * n : 8 * n + 8, :]

        d1, d2, cr, ci = part(0) + rho, part(1) + rho, part(2), part(3)
        over = 1.0 / (d1 * d2 - cr * cr - ci * ci)
        right = as_entries([part(4 + n) + rho * v.anchor[8 * n : 8 * n + 8, :] for n in range(8)])
        up = (cr * over, ci * over)
        s1, s2 = d2 * over, d1 * over
        solved = []
        for r in range(2):
            x, y = right[2 * r], right[2 * r + 1]
            one = mul_conj(y, up)
            two = mul(x, up)
            solved.append((x[0] * s1 - one[0], x[1] * s1 - one[1]))
            solved.append((y[0] * s2 - two[0], y[1] * s2 - two[1]))
        for n in range(4):
            for k in range(2):
                at = 8 * (n + 4 * k)
                v.gain[at : at + 8, :] = 0.5 * (v.gain[at : at + 8, :] + solved[n][k])
        for j in range(tiles):
            v.g_src[it, 8 * j : 8 * j + 8, :] = v.gain[pl.ds(j, 8, stride=8), :]

        @pl.when(it < PASSES - 1)
        def _():
            to_stn(lambda _: v.g_src.at[it], v.g_all.at[it, g_rows], v.g_sem.at[it])
            v.g_all[it, g_rows] = v.g_src[it]

        @pl.when(it == INNER - 1)
        def _():
            v.f_src[...] = v.g_src[it] + v.dual[...]
            v.f_all[chan] = v.f_src[...]
            for mask in chan_masks:
                remote(v.f_src, v.f_all.at[chan], v.f_sem, peer_of(mask))

        return 0

    lax.fori_loop(0, PASSES, one_pass, 0)

    low = lax.broadcasted_iota(jnp.int32, (8, 128), 1) < 64

    def slices(ref, rows):
        for j in range(tiles):
            a = rows[8 * j : 8 * j + 8]
            under = pltpu.roll(a, 4, 0)
            ref[2 * j] = jnp.where(low, a, swap(under))[0:4]
            ref[2 * j + 1] = jnp.where(low, swap(a), under)[0:4]

    last = v.g_src[PASSES - 1]
    slices(v.s_src, last + v.dual[...])
    slices(v.j_src, last)
    for mask in masks:
        block = stn + lowers[mask & 7]
        remote(v.s_src.at[block], v.s_all.at[me], v.s_sem, peer_of(mask))
    to_stn(lambda peer: v.j_src.at[peer], v.j_all.at[stn], v.j_sem)
    v.s_all[me] = v.s_src[stn]
    v.j_all[stn] = v.j_src[stn]
    wait_all(v.j_all.at[pl.ds(0, blocks - 1)], v.j_sem.at[1])

    packed[0:32, :] = v.j_all[...].reshape(32, 128)
    wait_all(v.s_all.at[pl.ds(0, everyone - 1)], v.s_sem.at[1])
    fit = [jnp.zeros((32, 128), f32)] * TERMS
    for f in range(chans):
        value = v.s_all[blocks * f : blocks * f + blocks].reshape(32, 128)
        fit = [fit[t] + f32(table[f, t]) * value for t in range(TERMS)]
    fit = [z * f32(1.0 / chans) for z in fit]
    packed[32:64, :] = v.s_all[pl.ds(blocks * chan, blocks)].reshape(32, 128) - consensus_of(fit)
    for t in range(TERMS):
        packed[64 + 32 * t : 96 + 32 * t, :] = fit[t]

    wait_all(v.pairs_all.at[pl.ds(0, blocks - 1)], v.p_sem.at[0])
    wait_all(v.d_all.at[pl.ds(0, (blocks - 1) * own_r)], v.d_sem.at[0])
    wait_all(v.f_all.at[pl.ds(0, chans - 1)], v.f_sem.at[0])
    wait_all(v.s_all.at[pl.ds(0, everyone - 1)], v.s_sem.at[0])
    wait_all(v.j_all.at[pl.ds(0, blocks - 1)], v.j_sem.at[0])
    for it in range(PASSES):
        wait_all(v.e_all.at[it, pl.ds(0, everyone - 1)], v.e_sem.at[it, 0])
        wait_all(v.r_all.at[it, pl.ds(0, (blocks - 1) * own_r)], v.r_sem.at[it, 0])
        if it < PASSES - 1:
            wait_all(v.g_all.at[it, pl.ds(0, (blocks - 1) * own_g)], v.g_sem.at[it, 0])


def unpack(packed, gain_out, dual_out, fit_out):
    spots = [(gain_out, 0), (dual_out, 0)] + [(fit_out, 64 * t) for t in range(TERMS)]
    for m, (ref, start) in enumerate(spots):
        for n in range(4):
            rows = packed[pl.ds(32 * m + n, PATHS, stride=4), :]
            ref[start + 8 * n : start + 8 * n + 8, :] = rows[:, 0:64]
            ref[start + 32 + 8 * n : start + 40 + 8 * n, :] = swap(rows)[:, 0:64]


def solution(mesh):
    chans, blocks = mesh.shape["chan"], mesh.shape["stn"]
    table = basis_table(chans)
    abstract = mesh.abstract_mesh

    def body(vis, model, pointing, pairs, gains, poly, dual, rhos):
        baselines = vis.shape[2]
        stations = gains.shape[3]

        def run(*refs):
            kernel(chans, blocks, table, *refs)

        lay_out(chans, blocks, baselines, stations)
        any_spec = pl.BlockSpec(memory_space=pltpu.HBM)
        vmem = pl.BlockSpec(memory_space=pltpu.VMEM)
        packed = pl.pallas_call(
            run,
            out_shape=jax.ShapeDtypeStruct((32 * (2 + TERMS), 128), f32),
            in_specs=[any_spec] * 8,
            out_specs=vmem,
            scratch_shapes=[shape for _, shape in SCRATCH],
            compiler_params=pltpu.CompilerParams(
                collective_id=0, has_side_effects=True, vmem_limit_bytes=40 << 20
            ),
            name="calibrate",
        )(
            pltpu.with_memory_space_constraint(pointing.reshape(SOURCES), pltpu.HBM),
            pltpu.with_memory_space_constraint(rhos, pltpu.HBM),
            pltpu.with_memory_space_constraint(vis.reshape(8, baselines), pltpu.HBM),
            pltpu.with_memory_space_constraint(model.reshape(8 * SOURCES, baselines), pltpu.HBM),
            pltpu.with_memory_space_constraint(pairs, pltpu.HBM),
            pltpu.with_memory_space_constraint(gains.reshape(64, stations), pltpu.HBM),
            pltpu.with_memory_space_constraint(poly.reshape(64 * TERMS, stations), pltpu.HBM),
            pltpu.with_memory_space_constraint(dual.reshape(64, stations), pltpu.HBM),
        )
        out = pl.pallas_call(
            unpack,
            out_shape=(
                jax.ShapeDtypeStruct((64, 64), f32),
                jax.ShapeDtypeStruct((64, 64), f32),
                jax.ShapeDtypeStruct((64 * TERMS, 64), f32),
            ),
            in_specs=[vmem],
            out_specs=(vmem, vmem, vmem),
            compiler_params=pltpu.CompilerParams(vmem_limit_bytes=16 << 20),
            name="unpack",
        )(packed)
        return (
            out[0].reshape(1, 8, PATHS, 64),
            out[1].reshape(1, 8, PATHS, 64),
            out[2].reshape(TERMS, 8, PATHS, 64),
        )

    return jax.shard_map(
        body,
        mesh=mesh,
        in_specs=(
            P("chan", None, "stn"),
            P("chan", None, None, "stn"),
            P(),
            P(None, "stn"),
            P("chan", None, None, None),
            P(),
            P("chan", None, None, None),
            P(),
        ),
        out_specs=(
            P("chan", None, None, "stn"),
            P("chan", None, None, "stn"),
            P(None, None, None, "stn"),
        ),
        check_vma=False,
    )
```

```python
import numpy as np
import jax
import jax.numpy as jnp
from jax import lax
from jax.experimental import pallas as pl
from jax.experimental.pallas import tpu as pltpu
from jax.sharding import PartitionSpec as P

PATHS = 8
SOURCES = 16
TERMS = 3
STEPS = 2
INNER = 2
PASSES = STEPS * INNER
NU = 2.0
TINY = 1e-06
LOGICAL = pl.DeviceIdType.LOGICAL
WIDE = 128
bf16 = jnp.bfloat16
f32 = jnp.float32


def basis_table(count):
    frequency = (2.0 * np.arange(count, dtype=np.float32) + 1.0) / np.float32(count) - 1.0
    columns = []
    for degree in range(TERMS):
        column = (frequency**degree).astype(np.float32)
        for earlier in columns:
            column = column - np.sum(earlier * column) / np.float32(count) * earlier
        column = column / np.sqrt(np.sum(column * column) / np.float32(count))
        columns.append(column.astype(np.float32))
    return np.stack(columns, axis=1)


def mul(a, b):
    return (a[0] * b[0] - a[1] * b[1], a[0] * b[1] + a[1] * b[0])


def mul_conj(a, b):
    return (a[0] * b[0] + a[1] * b[1], a[1] * b[0] - a[0] * b[1])


def conj_mul(a, b):
    return (a[0] * b[0] + a[1] * b[1], a[0] * b[1] - a[1] * b[0])


def add(a, b):
    return (a[0] + b[0], a[1] + b[1])


def product(a, b):
    return [
        add(mul(a[0], b[0]), mul(a[1], b[2])),
        add(mul(a[0], b[1]), mul(a[1], b[3])),
        add(mul(a[2], b[0]), mul(a[3], b[2])),
        add(mul(a[2], b[1]), mul(a[3], b[3])),
    ]


def product_with_adjoint(a, b):
    return [
        add(mul_conj(a[0], b[0]), mul_conj(a[1], b[1])),
        add(mul_conj(a[0], b[2]), mul_conj(a[1], b[3])),
        add(mul_conj(a[2], b[0]), mul_conj(a[3], b[1])),
        add(mul_conj(a[2], b[2]), mul_conj(a[3], b[3])),
    ]


def adjoint_product(a, b):
    return [
        add(conj_mul(a[0], b[0]), conj_mul(a[2], b[2])),
        add(conj_mul(a[0], b[1]), conj_mul(a[2], b[3])),
        add(conj_mul(a[1], b[0]), conj_mul(a[3], b[2])),
        add(conj_mul(a[1], b[1]), conj_mul(a[3], b[3])),
    ]


def power(a):
    return a[0] * a[0] + a[1] * a[1]


def gram(y):
    cross = add(mul_conj(y[0], y[2]), mul_conj(y[1], y[3]))
    return [power(y[0]) + power(y[1]), power(y[2]) + power(y[3]), cross[0], cross[1]]


def gram_of_adjoint(h):
    cross = add(conj_mul(h[0], h[1]), conj_mul(h[2], h[3]))
    return [power(h[0]) + power(h[2]), power(h[1]) + power(h[3]), cross[0], cross[1]]


def halves(x):
    top = x.astype(bf16)
    return top, (x - top.astype(f32)).astype(bf16)


def swap(x):
    return pltpu.roll(x, 64, 1)


def take(table, index):
    return jnp.take_along_axis(table, index, axis=1, mode="promise_in_bounds")


def masks_by_hops(everyone):
    hop = (0, 1, 2, 1)
    hops = lambda m: hop[m >> 1 & 3] + hop[m >> 3 & 3] + hop[m >> 5 & 3]
    return sorted(range(1, everyone), key=lambda m: (-hops(m), m))


SCRATCH = []


def scratch(name, *shape, dtype=f32):
    SCRATCH.append((name, pltpu.VMEM(shape, dtype)))


def lay_out(chans, blocks, baselines, stations):
    SCRATCH.clear()
    everyone = chans * blocks
    scratch("vis", 8, baselines)
    scratch("model", 8 * SOURCES, baselines)
    scratch("pairs", 2, baselines, dtype=jnp.int32)
    scratch("whole", 64 * stations // 128, 128)
    scratch("poly", 64 * TERMS * stations // 128, 128)
    scratch("dual_in", 64 * stations // 128, 128)
    scratch("coherent", 64, baselines)
    scratch("d_src", baselines // 128 * 64, 128)
    scratch("d_all", baselines // 128 * 64, 128)
    scratch("d_own", 64, baselines)
    scratch("pairs_all", blocks, 2, baselines, dtype=jnp.int32)
    scratch("index_p", blocks, baselines, dtype=jnp.int32)
    scratch("index_q", blocks, baselines, dtype=jnp.int32)
    scratch("table_q", 8 * stations // 128 * 8, 128)
    scratch("table_p", 64, 128)
    scratch("collect", blocks * baselines, 256, dtype=bf16)
    scratch("in_tile", blocks * 4 * 16, baselines, dtype=bf16)
    scratch("toward", 64, baselines)
    scratch("terms", 64, baselines)
    scratch("back", 64, baselines)
    scratch("parts_p", baselines // 128 * 16 * blocks, 128)
    scratch("parts_q", baselines // 128 * 16 * blocks, 128)
    scratch("weights", blocks, baselines)
    scratch("sums", 128, 128)
    scratch("gain", 64, 128)
    scratch("anchor", 64, 128)
    scratch("dual", stations // 16, 128)
    scratch("e_src", PASSES, 8, 128)
    scratch("e_all", PASSES, everyone, 128)
    scratch("r_src", PASSES, baselines // 16, 128)
    scratch("r_all", PASSES, blocks * baselines // 16, 128)
    scratch("g_src", PASSES, stations // 16, 128)
    scratch("g_all", PASSES, blocks * stations // 16, 128)
    scratch("f_src", stations // 16, 128)
    scratch("f_all", chans, stations // 16, 128)
    scratch("s_src", blocks, 4, 128)
    scratch("s_all", everyone, 4, 128)
    scratch("j_src", blocks, 4, 128)
    scratch("j_all", blocks, 4, 128)
    SCRATCH.append(("pointing", pltpu.SMEM((SOURCES,), jnp.int32)))
    SCRATCH.append(("rhos", pltpu.SMEM((PATHS,), f32)))
    dma = pltpu.SemaphoreType.DMA
    SCRATCH.append(("load_sem", dma((5 + 3 * stations // 128,))))
    for name, *shape in (
        ("p_sem", 2),
        ("d_sem", 2),
        ("e_sem", PASSES, 2),
        ("r_sem", PASSES, 4),
        ("g_sem", PASSES, 2),
        ("f_sem", 2),
        ("s_sem", 2),
        ("j_sem", 2),
    ):
        SCRATCH.append((name, dma(tuple(shape))))


class Held:
    def __init__(self, refs):
        for (name, _), ref in zip(SCRATCH, refs, strict=True):
            setattr(self, name, ref)


def kernel(
    chans,
    blocks,
    table,
    pointing_hbm,
    rhos_hbm,
    vis_hbm,
    model_hbm,
    pairs_hbm,
    gain_hbm,
    poly_hbm,
    dual_hbm,
    packed,
    *refs,
):
    v = Held(refs)
    stations = gain_hbm.shape[1]
    chan = lax.axis_index("chan")
    stn = lax.axis_index("stn")
    everyone = chans * blocks
    me = chan * blocks + stn
    baselines = v.vis.shape[1]
    tiles = stations // 128
    chunks = baselines // WIDE
    samples = float(everyone * baselines)

    flips = [(1 - 2 * lax.rem(lax.div(me, 1 << n), 2)) * (1 << n) for n in range(7)]

    def flipped(mask, start, count, base):
        for n in range(count):
            if mask >> n & 1:
                base = base + flips[start + n]
        return base

    uppers = [flipped(m, 4, 3, me) for m in range(8)]
    lowers = [flipped(m, 0, 4, 0) for m in range(16)]
    masks = masks_by_hops(everyone)

    def peer_of(mask):
        return uppers[mask >> 4] + lowers[mask & 15]

    stn_masks = [m for m in masks if m < blocks]
    chan_masks = [m for m in masks if m % blocks == 0]

    barrier = pltpu.get_barrier_semaphore()
    for mask in masks:
        pl.semaphore_signal(barrier, inc=1, device_id=peer_of(mask), device_id_type=LOGICAL)

    pointing, rhos = v.pointing, v.rhos
    moves = [(pointing_hbm, pointing), (rhos_hbm, rhos), (model_hbm, v.model)]
    moves += [(pairs_hbm, v.pairs), (vis_hbm, v.vis)]
    for src, dst in ((gain_hbm, v.whole), (dual_hbm, v.dual_in), (poly_hbm, v.poly)):
        rows = src.shape[0]
        moves += [
            (src.at[:, pl.ds(128 * j, 128)], dst.at[pl.ds(rows * j, rows)]) for j in range(tiles)
        ]
    loads = [pltpu.make_async_copy(a, b, v.load_sem.at[n]) for n, (a, b) in enumerate(moves)]
    for copy in loads:
        copy.start()

    def remote(src, dst, sem, peer):
        pltpu.make_async_remote_copy(
            src_ref=src,
            dst_ref=dst,
            send_sem=sem.at[0],
            recv_sem=sem.at[1],
            device_id=peer,
            device_id_type=LOGICAL,
        ).start()

    def to_stn(src, dst, sem):
        for mask in stn_masks:
            remote(src(stn + lowers[mask]), dst, sem, peer_of(mask))

    def to_partner(src, dst, sem):
        pltpu.make_async_remote_copy(
            src_ref=src,
            dst_ref=dst,
            send_sem=sem.at[0],
            recv_sem=sem.at[3],
            device_id=peer_of(1),
            device_id_type=LOGICAL,
        ).start()

    def wait_all(ref, sem):
        pltpu.make_async_copy(ref, ref, sem).wait()

    def chunk(i):
        return pl.ds(pl.multiple_of(i * WIDE, WIDE), WIDE)

    def entries(ref, at):
        return [(ref[8 * i : 8 * i + 8, at], ref[32 + 8 * i : 40 + 8 * i, at]) for i in range(4)]

    def keep(ref, at, values):
        for i in range(4):
            ref[8 * i : 8 * i + 8, at] = values[i][0]
            ref[32 + 8 * i : 40 + 8 * i, at] = values[i][1]

    def as_entries(values):
        return [(values[i], values[4 + i]) for i in range(4)]

    def picked(tile_of, index):
        within, tile = index & 127, index >> 7
        out = []
        for c in range(8):
            value = take(tile_of(c, 0), within)
            for j in range(1, tiles):
                value = jnp.where(tile == j, take(tile_of(c, j), within), value)
            out.append(value)
        return as_entries(out)

    loads[0].wait()
    loads[1].wait()

    lane = lax.broadcasted_iota(jnp.int32, (128, 128), 1)
    high = lax.broadcasted_iota(jnp.int32, (128, 128), 0)
    point = jnp.zeros((128, 128), jnp.int32)
    for s in range(SOURCES):
        point = jnp.where(lane % SOURCES == s, pointing[s], point)
    left, right = high % 64 // PATHS, high % PATHS
    component = jnp.where(high < 64, left, right)
    direction = jnp.where(high < 64, right, left)
    member = jnp.where((component == lane // SOURCES) & (direction == point), 1.0, 0.0).astype(bf16)
    loads[2].wait()

    def combine(*accs):
        twice = jnp.concatenate([member, member], axis=1)
        for i in range(baselines // 256):
            m = v.model[:, 256 * i : 256 * i + 256]
            m0 = m.astype(bf16)
            rest = m - m0.astype(f32)
            m1 = rest.astype(bf16)
            m2 = (rest - m1.astype(f32)).astype(bf16)
            two = jnp.concatenate([m0, m1], axis=0)
            one = jnp.concatenate([m2, jnp.zeros((128, 256), bf16)], axis=0)
            for n, part in enumerate((two, one)):
                pltpu.matmul_push_rhs(part, staging_register=n, mxu_index=i % 2)
                pltpu.matmul_acc_lhs(accs[i % 2], twice, load_staged_rhs=n)
            both = pltpu.matmul_pop(accs[i % 2])
            v.coherent[:, 256 * i : 256 * i + 256] = both[0:64]
            for k in range(PATHS):
                for j in range(2):
                    row = 64 * k + 8 * (2 * i + j)
                    v.d_src[row : row + 8] = both[64 + 8 * k : 72 + 8 * k, 128 * j : 128 * j + 128]

    pl.run_scoped(combine, *[pltpu.ACC(m)((128, 256), f32) for m in range(2)])

    def mine(t):
        value = f32(0.0)
        for f in range(chans):
            value = jnp.where(chan == f, f32(table[f, t]), value)
        return value

    my_basis = [mine(t) for t in range(TERMS)]
    for copy in loads[3:]:
        copy.wait()

    def consensus_of(fit):
        value = my_basis[0] * fit[0]
        for t in range(1, TERMS):
            value = value + my_basis[t] * fit[t]
        return value

    def to_tiles(ref, rows):
        for j in range(tiles):
            ref[pl.ds(j, 8, stride=8), :] = rows[8 * j : 8 * j + 8]

    def own_of(ref, rows, start):
        return jnp.concatenate(
            [ref[pl.ds(rows * j + start + stn, 8, stride=8), :] for j in range(tiles)], axis=0
        )

    v.gain[...] = jnp.zeros((64, 128), f32)
    v.anchor[...] = jnp.zeros((64, 128), f32)
    v.sums[...] = jnp.zeros((128, 128), f32)
    to_tiles(v.gain, own_of(v.whole, 64, 0))
    dual_rows = own_of(v.dual_in, 64, 0)
    v.dual[...] = dual_rows
    to_tiles(v.anchor, consensus_of([own_of(v.poly, 64 * TERMS, 64 * t) for t in range(TERMS)]) - dual_rows)
    rho = rhos[stn]

    def keep_part(ref, i, n, value):
        ref[pl.ds(16 * blocks * i + n, blocks, stride=16), :] = value

    zeros = jnp.zeros((8, WIDE), f32)
    for n in range(12, 16):
        for i in range(chunks):
            keep_part(v.parts_p, i, n, zeros)
            keep_part(v.parts_q, i, n, zeros)
    sub = lax.broadcasted_iota(jnp.int32, (8, 128), 0)
    own_tile = pl.multiple_of(lax.div(stn, 2) * 64, 64)

    def spread_tables():
        rows = [v.gain[pl.ds(j, 8, stride=8), :] for j in range(tiles)]
        for c in range(8):
            per_block = None
            for j in range(tiles):
                value = jnp.broadcast_to(rows[j][c : c + 1], (8, 128))
                at = 8 * (c * tiles + j)
                v.table_q[at : at + 8, :] = value
                per_block = value if j == 0 else jnp.where(sub // 2 == j, value, per_block)
            v.table_p[8 * c : 8 * c + 8, :] = per_block

    def own_terms(i, _):
        at = chunk(i)
        d = entries(v.d_own, at)
        p = v.index_p[:, at]
        gain_p = as_entries([take(v.table_p[8 * c : 8 * c + 8, :], p) for c in range(8)])
        h = product(gain_p, d)
        keep(v.back, at, h)
        for n, part in enumerate(gram_of_adjoint(h)):
            keep_part(v.parts_q, i, n, part)

        def tile_of(c, j):
            return v.table_q[8 * (c * tiles + j) : 8 * (c * tiles + j) + 8, :]

        y = product_with_adjoint(d, picked(tile_of, v.index_q[:, at]))
        keep(v.toward, at, y)
        for n, part in enumerate(gram(y)):
            keep_part(v.parts_p, i, n, part)
        keep(v.terms, at, product(gain_p, y))
        return 0

    own_g, own_r = stations // 16, baselines // 16
    g_rows = pl.ds(pl.multiple_of(own_g * stn, own_g), own_g)
    r_rows = pl.ds(pl.multiple_of(own_r * stn, own_r), own_r)
    half = own_r // 2

    def half_rows(block, part):
        return pl.ds(pl.multiple_of(own_r * block + half * part, half), half)

    even_masks = [mask for mask in stn_masks if mask % 2 == 0]

    def send_residuals(it, part):
        src = v.r_src.at[it, pl.ds(half * part, half)]
        dst = v.r_all.at[it, half_rows(stn, part)]
        for mask in even_masks:
            pltpu.make_async_remote_copy(
                src_ref=src,
                dst_ref=dst,
                send_sem=v.r_sem.at[it, 0],
                recv_sem=v.r_sem.at[it, 1 + part],
                device_id=peer_of(mask),
                device_id_type=LOGICAL,
            ).start()
        to_partner(src, dst, v.r_sem.at[it])

    def pass_on(it):
        for part in range(2):
            wait_all(v.r_all.at[it, pl.ds(0, (blocks // 2 - 1) * half)], v.r_sem.at[it, 1 + part])
            for mask in even_masks:
                rows = v.r_all.at[it, half_rows(stn + lowers[mask], part)]
                to_partner(rows, rows, v.r_sem.at[it])

    def residuals_of(it, part):
        def residuals(i, total):
            at = chunk(i)
            first = jnp.broadcast_to(v.pairs[0:1, at], (8, WIDE)) & 127
            second = jnp.broadcast_to(v.pairs[1:2, at], (8, WIDE))

            def tile_of(c, j):
                return v.whole[64 * j + 8 * c : 64 * j + 8 * c + 8]

            y = product_with_adjoint(entries(v.coherent, at), picked(tile_of, second))
            gain_p = as_entries(
                [take(v.whole[pl.ds(own_tile + 8 * c, 8)], first) for c in range(8)]
            )
            g = product(gain_p, y)
            e = None
            for n in range(4):
                for part in range(2):
                    c = n + 4 * part
                    left = v.vis[c : c + 1, at] - jnp.sum(g[n][part], axis=0, keepdims=True)
                    e = left * left if e is None else e + left * left
                    v.r_src[it, pl.ds(8 * i + c, 1)] = left
            return total + e

        first = part * chunks // 2
        zero = jnp.zeros((1, WIDE), f32)
        return lax.fori_loop(first, first + chunks // 2, residuals, zero, unroll=True)

    def keep_energy(it, total):
        v.e_src[it, 0:1] = total
        v.e_all[it, pl.ds(me, 1)] = total

    keep_energy(0, residuals_of(0, 0) + residuals_of(0, 1))
    pl.semaphore_wait(barrier, everyone - 1)

    def one_pass(it, _):
        @pl.when(it > 0)
        def _():
            spread_tables()
            lax.fori_loop(0, chunks, own_terms, 0, unroll=True)
            wait_all(v.g_all.at[it - 1, pl.ds(0, (blocks - 1) * own_g)], v.g_sem.at[it - 1, 1])
            for j in range(tiles):
                for c in range(8):
                    v.whole[64 * j + 8 * c : 64 * j + 8 * c + 8] = v.g_all[
                        it - 1, pl.ds(8 * j + c, blocks, stride=own_g), :
                    ]
            total = residuals_of(it, 0)
            send_residuals(it, 0)
            keep_energy(it, total + residuals_of(it, 1))

        @pl.when(it == 0)
        def _():
            to_stn(lambda _: v.pairs, v.pairs_all.at[stn], v.p_sem)
            send_residuals(it, 0)

        send_residuals(it, 1)
        for mask in masks:
            remote(v.e_src.at[it, pl.ds(0, 1)], v.e_all.at[it, pl.ds(me, 1)], v.e_sem.at[it], peer_of(mask))

        v.r_all[it, r_rows] = v.r_src[it]

        @pl.when(it == 0)
        def _():
            to_stn(
                lambda peer: v.d_src.at[pl.ds(pl.multiple_of(own_r * peer, own_r), own_r)],
                v.d_all.at[r_rows],
                v.d_sem,
            )
            spread_tables()
            v.pairs_all[stn] = v.pairs[...]
            v.d_all[r_rows] = v.d_src[r_rows]
            wait_all(v.pairs_all.at[pl.ds(0, blocks - 1)], v.p_sem.at[1])
            column = lax.broadcasted_iota(jnp.int32, (baselines, 128), 1).astype(f32).astype(bf16)
            for i in range(blocks):
                if i == blocks // 2:
                    pass_on(it)
                first = v.pairs_all[i, 0:1, :] & 127
                second = v.pairs_all[i, 1:2, :]
                v.index_p[i : i + 1, :] = first
                v.index_q[i : i + 1, :] = second
                for start, index in ((0, second & 127), (128, first)):
                    across = jnp.broadcast_to(index.astype(f32).astype(bf16), (128, baselines)).T
                    v.collect[baselines * i : baselines * i + baselines, start : start + 128] = jnp.where(
                        column == across, bf16(1.0), bf16(0.0)
                    )
                for j in range(tiles):
                    inside = jnp.where((second >> 7) == j, 1.0, 0.0)
                    at = 16 * (4 * i + j)
                    v.in_tile[at : at + 16, :] = jnp.broadcast_to(inside, (16, baselines)).astype(bf16)
            wait_all(v.d_all.at[pl.ds(0, (blocks - 1) * own_r)], v.d_sem.at[1])
            for i in range(chunks):
                at = slice(WIDE * i, WIDE * i + WIDE)
                for c in range(8):
                    v.d_own[8 * c : 8 * c + 8, at] = v.d_all[pl.ds(8 * i + c, blocks, stride=own_r), :]
            lax.fori_loop(0, chunks, own_terms, 0, unroll=True)

        @pl.when(it == INNER)
        def _():
            wait_all(v.f_all.at[pl.ds(0, chans - 1)], v.f_sem.at[1])
            fit = [jnp.zeros((own_g, 128), f32)] * TERMS
            for f in range(chans):
                value = v.f_all[f]
                fit = [fit[t] + f32(table[f, t]) * value for t in range(TERMS)]
            consensus = consensus_of([z * f32(1.0 / chans) for z in fit])
            after = v.f_src[...] - consensus
            v.dual[...] = after
            to_tiles(v.anchor, consensus - after)

        @pl.when(it > 0)
        def _():
            pass_on(it)

        wait_all(v.r_all.at[it, pl.ds(0, blocks // 2 * own_r)], v.r_sem.at[it, 3])

        def products(i, _):
            at = chunk(i)
            y, h, g = entries(v.toward, at), entries(v.back, at), entries(v.terms, at)
            r = as_entries([v.r_all[it, pl.ds(8 * i + c, blocks, stride=own_r), :] for c in range(8)])
            v.weights[:, at] = power(r[0]) + power(r[1]) + power(r[2]) + power(r[3])
            x = [add(a, b) for a, b in zip(r, g)]
            b = product_with_adjoint(x, y)
            for n, part in enumerate([z[0] for z in b] + [z[1] for z in b]):
                keep_part(v.parts_p, i, 4 + n, part)
            b = adjoint_product(x, h)
            for n, part in enumerate([z[0] for z in b] + [z[1] for z in b]):
                keep_part(v.parts_q, i, 4 + n, part)
            return 0

        lax.fori_loop(0, chunks, products, 0, unroll=True)

        wait_all(v.e_all.at[it, pl.ds(0, everyone - 1)], v.e_sem.at[it, 1])
        total = jnp.sum(v.e_all[it], axis=0, keepdims=True)
        noise = jnp.sum(total, axis=1, keepdims=True) * f32(1.0 / samples) + TINY
        scale = jnp.broadcast_to(1.0 / noise, (1, 128))
        scale = jnp.concatenate([scale] * (baselines // 128), axis=1)
        v.weights[...] = (NU + 2.0) / (NU + v.weights[...] * scale)

        def block_of(ref, i, start):
            rows = [16 * (blocks * n + i) for n in range(start // 128, start // 128 + 2)]
            return jnp.concatenate([ref[row : row + 16, :] for row in rows], axis=1)

        def accumulate(*accs):
            acc_q, acc_p = accs[:2], (accs[2 : 2 + tiles], accs[2 + tiles :])
            for step in range(blocks * baselines // 512):
                for m in range(2):
                    i = 2 * (step * 256 // baselines) + m
                    start = baselines * i + step * 256 % baselines
                    at = slice(start, start + 256)
                    pltpu.matmul_push_rhs(v.collect[at, :], staging_register=step % 2, mxu_index=m)
                    here = slice(start - baselines * i, start - baselines * i + 256)
                    weight = v.weights[i : i + 1, here]
                    top, rest = halves(block_of(v.parts_q, i, here.start) * weight)
                    pieces = []
                    for j in range(tiles):
                        inside = v.in_tile[16 * (4 * i + j) : 16 * (4 * i + j) + 16, here]
                        pieces += [top * inside, rest * inside]
                    pltpu.matmul_acc_lhs(
                        acc_q[m], jnp.concatenate(pieces, axis=0), load_staged_rhs=step % 2
                    )
                    pieces = halves(block_of(v.parts_p, i, here.start) * weight)
                    pltpu.matmul_acc_lhs(acc_p[m][i // 2], jnp.concatenate(pieces, axis=0))
            every = pltpu.matmul_pop(acc_q[0]) + pltpu.matmul_pop(acc_q[1])
            for j in range(tiles):
                here = pltpu.matmul_pop(acc_p[0][j]) + pltpu.matmul_pop(acc_p[1][j])
                got = every[32 * j : 32 * j + 32, 0:128] + here[:, 128:256]
                v.sums[pl.ds(j, 16, stride=8), :] = got[0:16] + got[16:32]

        accs = [pltpu.ACC(m)((128, 256), f32) for m in range(2)]
        accs += [pltpu.ACC(m)((32, 256), f32) for m in range(2) for _ in range(tiles)]
        pl.run_scoped(accumulate, *accs)

        def part(n):
            return v.sums[8 * n : 8 * n + 8, :]

        d1, d2, cr, ci = part(0) + rho, part(1) + rho, part(2), part(3)
        over = 1.0 / (d1 * d2 - cr * cr - ci * ci)
        right = as_entries([part(4 + n) + rho * v.anchor[8 * n : 8 * n + 8, :] for n in range(8)])
        up = (cr * over, ci * over)
        s1, s2 = d2 * over, d1 * over
        solved = []
        for r in range(2):
            x, y = right[2 * r], right[2 * r + 1]
            one = mul_conj(y, up)
            two = mul(x, up)
            solved.append((x[0] * s1 - one[0], x[1] * s1 - one[1]))
            solved.append((y[0] * s2 - two[0], y[1] * s2 - two[1]))
        for n in range(4):
            for k in range(2):
                at = 8 * (n + 4 * k)
                v.gain[at : at + 8, :] = 0.5 * (v.gain[at : at + 8, :] + solved[n][k])
        for j in range(tiles):
            v.g_src[it, 8 * j : 8 * j + 8, :] = v.gain[pl.ds(j, 8, stride=8), :]

        @pl.when(it < PASSES - 1)
        def _():
            to_stn(lambda _: v.g_src.at[it], v.g_all.at[it, g_rows], v.g_sem.at[it])
            v.g_all[it, g_rows] = v.g_src[it]

        @pl.when(it == INNER - 1)
        def _():
            v.f_src[...] = v.g_src[it] + v.dual[...]
            v.f_all[chan] = v.f_src[...]
            for mask in chan_masks:
                remote(v.f_src, v.f_all.at[chan], v.f_sem, peer_of(mask))

        return 0

    lax.fori_loop(0, PASSES, one_pass, 0)

    low = lax.broadcasted_iota(jnp.int32, (8, 128), 1) < 64

    def slices(ref, rows):
        for j in range(tiles):
            a = rows[8 * j : 8 * j + 8]
            under = pltpu.roll(a, 4, 0)
            ref[2 * j] = jnp.where(low, a, swap(under))[0:4]
            ref[2 * j + 1] = jnp.where(low, swap(a), under)[0:4]

    last = v.g_src[PASSES - 1]
    slices(v.s_src, last + v.dual[...])
    slices(v.j_src, last)
    for mask in masks:
        block = stn + lowers[mask & 7]
        remote(v.s_src.at[block], v.s_all.at[me], v.s_sem, peer_of(mask))
    to_stn(lambda peer: v.j_src.at[peer], v.j_all.at[stn], v.j_sem)
    v.s_all[me] = v.s_src[stn]
    v.j_all[stn] = v.j_src[stn]
    wait_all(v.pairs_all.at[pl.ds(0, blocks - 1)], v.p_sem.at[0])
    wait_all(v.d_all.at[pl.ds(0, (blocks - 1) * own_r)], v.d_sem.at[0])
    wait_all(v.f_all.at[pl.ds(0, chans - 1)], v.f_sem.at[0])
    for it in range(PASSES):
        wait_all(v.e_all.at[it, pl.ds(0, everyone - 1)], v.e_sem.at[it, 0])
        wait_all(v.r_all.at[it, pl.ds(0, (blocks - 1) * own_r)], v.r_sem.at[it, 0])
        if it < PASSES - 1:
            wait_all(v.g_all.at[it, pl.ds(0, (blocks - 1) * own_g)], v.g_sem.at[it, 0])
    wait_all(v.j_all.at[pl.ds(0, blocks - 1)], v.j_sem.at[1])

    packed[0:32, :] = v.j_all[...].reshape(32, 128)
    wait_all(v.s_all.at[pl.ds(0, everyone - 1)], v.s_sem.at[1])
    fit = [jnp.zeros((32, 128), f32)] * TERMS
    for f in range(chans):
        value = v.s_all[blocks * f : blocks * f + blocks].reshape(32, 128)
        fit = [fit[t] + f32(table[f, t]) * value for t in range(TERMS)]
    fit = [z * f32(1.0 / chans) for z in fit]
    packed[32:64, :] = v.s_all[pl.ds(blocks * chan, blocks)].reshape(32, 128) - consensus_of(fit)
    for t in range(TERMS):
        packed[64 + 32 * t : 96 + 32 * t, :] = fit[t]

    wait_all(v.s_all.at[pl.ds(0, everyone - 1)], v.s_sem.at[0])
    wait_all(v.j_all.at[pl.ds(0, blocks - 1)], v.j_sem.at[0])


def unpack(packed, gain_out, dual_out, fit_out):
    spots = [(gain_out, 0), (dual_out, 0)] + [(fit_out, 64 * t) for t in range(TERMS)]
    for m, (ref, start) in enumerate(spots):
        for n in range(4):
            rows = packed[pl.ds(32 * m + n, PATHS, stride=4), :]
            ref[start + 8 * n : start + 8 * n + 8, :] = rows[:, 0:64]
            ref[start + 32 + 8 * n : start + 40 + 8 * n, :] = swap(rows)[:, 0:64]


def solution(mesh):
    chans, blocks = mesh.shape["chan"], mesh.shape["stn"]
    table = basis_table(chans)
    abstract = mesh.abstract_mesh

    def body(vis, model, pointing, pairs, gains, poly, dual, rhos):
        baselines = vis.shape[2]
        stations = gains.shape[3]

        def run(*refs):
            kernel(chans, blocks, table, *refs)

        lay_out(chans, blocks, baselines, stations)
        any_spec = pl.BlockSpec(memory_space=pltpu.HBM)
        vmem = pl.BlockSpec(memory_space=pltpu.VMEM)
        packed = pl.pallas_call(
            run,
            out_shape=jax.ShapeDtypeStruct((32 * (2 + TERMS), 128), f32),
            in_specs=[any_spec] * 8,
            out_specs=vmem,
            scratch_shapes=[shape for _, shape in SCRATCH],
            compiler_params=pltpu.CompilerParams(
                collective_id=0, has_side_effects=True, vmem_limit_bytes=40 << 20
            ),
            name="calibrate",
        )(
            pltpu.with_memory_space_constraint(pointing.reshape(SOURCES), pltpu.HBM),
            pltpu.with_memory_space_constraint(rhos, pltpu.HBM),
            pltpu.with_memory_space_constraint(vis.reshape(8, baselines), pltpu.HBM),
            pltpu.with_memory_space_constraint(model.reshape(8 * SOURCES, baselines), pltpu.HBM),
            pltpu.with_memory_space_constraint(pairs, pltpu.HBM),
            pltpu.with_memory_space_constraint(gains.reshape(64, stations), pltpu.HBM),
            pltpu.with_memory_space_constraint(poly.reshape(64 * TERMS, stations), pltpu.HBM),
            pltpu.with_memory_space_constraint(dual.reshape(64, stations), pltpu.HBM),
        )
        out = pl.pallas_call(
            unpack,
            out_shape=(
                jax.ShapeDtypeStruct((64, 64), f32),
                jax.ShapeDtypeStruct((64, 64), f32),
                jax.ShapeDtypeStruct((64 * TERMS, 64), f32),
            ),
            in_specs=[vmem],
            out_specs=(vmem, vmem, vmem),
            compiler_params=pltpu.CompilerParams(vmem_limit_bytes=16 << 20),
            name="unpack",
        )(packed)
        return (
            out[0].reshape(1, 8, PATHS, 64),
            out[1].reshape(1, 8, PATHS, 64),
            out[2].reshape(TERMS, 8, PATHS, 64),
        )

    return jax.shard_map(
        body,
        mesh=mesh,
        in_specs=(
            P("chan", None, "stn"),
            P("chan", None, None, "stn"),
            P(),
            P(None, "stn"),
            P("chan", None, None, None),
            P(),
            P("chan", None, None, None),
            P(),
        ),
        out_specs=(
            P("chan", None, None, "stn"),
            P("chan", None, None, "stn"),
            P(None, None, None, "stn"),
        ),
        check_vma=False,
    )
```
